32 devices in a mesh: row: 8 (over y, x, core), col: 4 (over z).
Axes of the slice: x: 2, y: 2, z: 4, core: 2. Of those that a mesh axis runs over, the one named last changes fastest.
Arguments:
- pair_rep: bfloat16 [384, 384, 256], P('row', 'col'), may hold values from -6 to 6
- single_rep: bfloat16 [384, 768], replicated, may hold values from -6 to 6
- length: int32 [1], replicated, may hold values from 192 to 384
- pair_gain: float32 [256], replicated, may hold values from 0.25 to 1.75
- pair_proj: bfloat16 [4, 256, 256], replicated, may hold values from -0.375 to 0.375
- bias_weight: bfloat16 [256, 8], replicated, may hold values from -12 to 12
- pair_out_weight: bfloat16 [256, 256], replicated, may hold values from -1 to 1
- single_gain: float32 [768], replicated, may hold values from 0.25 to 1.75
- single_proj: bfloat16 [4, 768, 768], P(None, None, 'col'), may hold values from -0.21875 to 0.21875
- bias_norm_gain: float32 [256], replicated, may hold values from 0.25 to 1.75
- single_bias_weight: bfloat16 [256, 16], replicated, may hold values from -12 to 12
- single_out_weight: bfloat16 [768, 768], P('col'), may hold values from -0.625 to 0.625
Outputs:
- pair_out: bfloat16 [384, 384, 256], P('row', 'col')
- single_out: bfloat16 [384, 768], P('row', 'col')
The draws below stay inside these ranges and needn't reach their ends.
Inputs may be any that keep to these rules, and one draw needn't show every extreme that they name: Positions from length[0] on are padding and never serve as keys.
All inputs are finite; a program needn't handle non-finite values.
Results may differ from the reference program's by a relative error of at most 0.019.
Values may be sent and summed in bfloat16 or wider, within the bound.
A program may use at most 128 MiB of HBM per device.

```python
import math
import jax
import jax.numpy as jnp
from jax import lax

TOKENS = 384
PAIR_DIM = 256
PAIR_HEADS = 8
PAIR_HEAD_DIM = 32
SINGLE_DIM = 768
SINGLE_HEADS = 16
SINGLE_HEAD_DIM = 48


def draw_bias_weight(key, part):
    base = jax.random.normal(jax.random.fold_in(key, 11), (PAIR_DIM, PAIR_HEADS), jnp.float32) / math.sqrt(PAIR_DIM)
    return jnp.clip(base, -12.0, 12.0).astype(jnp.bfloat16)


def draw_single_bias_weight(key, part):
    base = jax.random.normal(jax.random.fold_in(key, 23), (PAIR_DIM, SINGLE_HEADS), jnp.float32) / math.sqrt(PAIR_DIM)
    return jnp.clip(base, -12.0, 12.0).astype(jnp.bfloat16)


def level_of(key, extent, shards, least, top_value):
    gain = 1.0
    for dim, shards_of in shards:
        heights = jax.random.uniform(jax.random.fold_in(jax.random.fold_in(key, 6), dim), (shards_of,), jnp.float32, least / len(shards), top_value / len(shards))
        gain = gain * jnp.repeat(jnp.exp(heights), extent[dim] // shards_of).reshape((-1,) + (1,) * (len(extent) - 1 - dim))
    return gain


def normal_values(own_key, extent, scale, bound, pieces=(), held_as=jnp.bfloat16):
    entries = jax.random.normal(own_key, extent, jnp.float32) * scale
    if len(pieces) > 0:
        entries = level_of(own_key, extent, pieces, -0.22, 0.18) * entries
    return jnp.clip(entries, min=-bound, max=bound).astype(held_as)


def setup_inputs(seed: int = 0) -> dict:
    splits = jax.random.split(jax.random.key(seed), 13)
    return {
        "pair_rep": normal_values(splits[0], (TOKENS, TOKENS, PAIR_DIM), 1.0, 6.0, ((0, 8), (1, 4))),
        "single_rep": normal_values(splits[1], (TOKENS, SINGLE_DIM), 1.0, 6.0),
        "length": jax.random.randint(splits[2], (1,), TOKENS // 2, TOKENS + 1).astype(jnp.int32),
        "pair_gain": jnp.clip(1.0 + 0.15 * jax.random.normal(splits[3], (PAIR_DIM,), jnp.float32), 0.25, 1.75),
        "pair_proj": normal_values(splits[4], (4, PAIR_DIM, PAIR_DIM), PAIR_DIM ** -0.5, 0.375),
        "bias_weight": draw_bias_weight(jax.random.fold_in(splits[12], 71), 0),
        "pair_out_weight": normal_values(splits[6], (PAIR_DIM, PAIR_DIM), (PAIR_DIM // 8) ** -0.5, 1.0),
        "single_gain": jnp.clip(1.0 + 0.15 * jax.random.normal(splits[7], (SINGLE_DIM,), jnp.float32), 0.25, 1.75),
        "single_proj": normal_values(splits[8], (4, SINGLE_DIM, SINGLE_DIM), SINGLE_DIM ** -0.5, 0.21875, ((2, 4),)),
        "bias_norm_gain": jnp.clip(1.0 + 0.15 * jax.random.normal(splits[9], (PAIR_DIM,), jnp.float32), 0.25, 1.75),
        "single_bias_weight": draw_single_bias_weight(jax.random.fold_in(splits[12], 71), 0),
        "single_out_weight": normal_values(splits[11], (SINGLE_DIM, SINGLE_DIM), (SINGLE_DIM // 8) ** -0.5, 0.625, ((0, 4),)),
    }


masked_value = -1e+30

def normalize(values, scales):
    floated = values.astype(jnp.float32)
    center = lax.optimization_barrier(jnp.mean(floated, axis=-1, keepdims=True))
    spread = lax.optimization_barrier(jnp.mean(jnp.square(floated - center), axis=-1, keepdims=True))
    return ((floated - center) * lax.rsqrt(spread + 1e-05) * scales).astype(jnp.bfloat16)

def project(inputs, matrix):
    return jnp.dot(inputs, matrix, preferred_element_type=jnp.float32).astype(jnp.bfloat16)

def softmax_weights(scores):
    row_max = lax.optimization_barrier(jnp.max(scores, axis=-1, keepdims=True))
    exponent = jnp.exp(scores - row_max)
    return (exponent / lax.optimization_barrier(jnp.sum(exponent, axis=-1, keepdims=True))).astype(jnp.bfloat16)

def reference(pair_rep, single_rep, length, pair_gain, pair_proj, bias_weight, pair_out_weight, single_gain, single_proj, bias_norm_gain, single_bias_weight, single_out_weight):
    block_rows = math.gcd(TOKENS, 8)
    groups = TOKENS // block_rows
    stacked = pair_rep.reshape(groups, block_rows, TOKENS, PAIR_DIM)

    def triangle_bias(rows_block):
        normed = normalize(rows_block, pair_gain)
        return project(normed, bias_weight)
    tri_bias = lax.map(triangle_bias, stacked).reshape(TOKENS, TOKENS, PAIR_HEADS)
    tri_bias = jnp.transpose(tri_bias, (2, 0, 1)).astype(jnp.float32)
    usable = jnp.arange(TOKENS, dtype=jnp.int32) < length[0]
    pair_scale = 1.0 / math.sqrt(PAIR_HEAD_DIM)

    def attend(rows_block):
        normed = normalize(rows_block, pair_gain)
        shape_heads = (block_rows, TOKENS, PAIR_HEADS, PAIR_HEAD_DIM)
        queries = project(normed, pair_proj[0]).reshape(shape_heads).astype(jnp.float32)
        key_rows = project(normed, pair_proj[1]).reshape(shape_heads).astype(jnp.float32)
        value_rows = project(normed, pair_proj[2]).reshape(shape_heads).astype(jnp.float32)
        gating = jax.nn.sigmoid(jnp.dot(normed, pair_proj[3], preferred_element_type=jnp.float32))
        scores = jnp.einsum('ijhd,ikhd->ihjk', queries, key_rows) * pair_scale + tri_bias[None]
        scores = jnp.where(usable, scores, masked_value)
        weights = softmax_weights(scores)
        attended = jnp.einsum('ihjk,ikhd->ijhd', weights.astype(jnp.float32), value_rows)
        attended = attended.reshape(block_rows, TOKENS, PAIR_DIM)
        hidden = (gating * attended).astype(jnp.bfloat16)
        updated = (rows_block.astype(jnp.float32) + jnp.dot(hidden, pair_out_weight, preferred_element_type=jnp.float32)).astype(jnp.bfloat16)
        bias_normed = normalize(updated, bias_norm_gain)
        head_bias = project(bias_normed, single_bias_weight)
        return (updated, head_bias)
    pair_out, head_bias = lax.map(attend, stacked)
    pair_out = pair_out.reshape(TOKENS, TOKENS, PAIR_DIM)
    head_bias = jnp.transpose(head_bias.reshape(TOKENS, TOKENS, SINGLE_HEADS), (2, 0, 1)).astype(jnp.float32)
    single_normed = normalize(single_rep, single_gain)
    shape_single = (TOKENS, SINGLE_HEADS, SINGLE_HEAD_DIM)
    s_query = project(single_normed, single_proj[0]).reshape(shape_single).astype(jnp.float32)
    s_key = project(single_normed, single_proj[1]).reshape(shape_single).astype(jnp.float32)
    s_value = project(single_normed, single_proj[2]).reshape(shape_single).astype(jnp.float32)
    s_gate = jax.nn.sigmoid(jnp.dot(single_normed, single_proj[3], preferred_element_type=jnp.float32))
    scores = jnp.einsum('ihd,jhd->hij', s_query, s_key) / math.sqrt(SINGLE_HEAD_DIM) + head_bias
    scores = jnp.where(usable, scores, masked_value)
    weights = softmax_weights(scores)
    blended = jnp.einsum('hij,jhd->ihd', weights.astype(jnp.float32), s_value).reshape(TOKENS, SINGLE_DIM)
    s_hidden = (s_gate * blended).astype(jnp.bfloat16)
    single_out = (single_rep.astype(jnp.float32) + jnp.dot(s_hidden, single_out_weight, preferred_element_type=jnp.float32)).astype(jnp.bfloat16)
    return (pair_out, single_out)
```

```python
import math

import jax
import jax.numpy as jnp
from jax import lax
from jax.experimental import pallas as pl
from jax.experimental.pallas import tpu as pltpu
from jax.sharding import PartitionSpec as P

PAIR_HEADS = 8
PAIR_HEAD_DIM = 32
SINGLE_HEAD_DIM = 48
LOG2E = math.log2(math.e)

masked_value = -1e30
NT = (((1,), (1,)), ((), ()))


def normalize(values, scales):
    floated = values.astype(jnp.float32)
    center = jnp.mean(floated, axis=-1, keepdims=True)
    spread = jnp.mean(jnp.square(floated - center), axis=-1, keepdims=True)
    return ((floated - center) * lax.rsqrt(spread + 1e-05) * scales).astype(jnp.bfloat16)


def project(inputs, matrix):
    return jnp.dot(inputs, matrix, preferred_element_type=jnp.float32).astype(jnp.bfloat16)


def project_t(inputs, matrix):
    return lax.dot_general(inputs, matrix, NT, preferred_element_type=jnp.float32).astype(
        jnp.bfloat16
    )


def row_update(rep, gain, proj_ref, out_weight, bias_of):
    channels = rep.shape[1]
    half = channels // 2
    heads_per_half = PAIR_HEADS // 2
    normed = normalize(rep, gain)
    f32 = jnp.float32
    query = jnp.dot(normed, proj_ref[0], preferred_element_type=f32)
    query = (query * (LOG2E / math.sqrt(PAIR_HEAD_DIM))).astype(jnp.bfloat16)
    key = project(normed, proj_ref[1])
    value = project(normed, proj_ref[2])
    gate = jax.nn.sigmoid(jnp.dot(normed, proj_ref[3], preferred_element_type=f32))
    head_of_lane = lax.broadcasted_iota(jnp.int32, (1, half), 1) // PAIR_HEAD_DIM
    halves = []
    for side in range(2):
        span = slice(side * half, (side + 1) * half)
        q_half, k_half, v_half = query[:, span], key[:, span], value[:, span]
        top = bottom = None
        for sub in range(heads_per_half):
            head = side * heads_per_half + sub
            mine = head_of_lane == sub
            q_head = jnp.where(mine, q_half, jnp.zeros_like(q_half))
            scores = lax.dot_general(q_head, k_half, NT, preferred_element_type=f32)
            scores = scores + bias_of(head)
            peak = jnp.max(scores, axis=-1, keepdims=True)
            exponent = jnp.exp2(scores - peak).astype(jnp.bfloat16)
            v_ext = jnp.concatenate([v_half, jnp.ones_like(v_half)], axis=1)
            both = jnp.dot(exponent, v_ext, preferred_element_type=f32)
            num, den = both[:, :half], both[:, half:]
            top = num if top is None else jnp.where(mine, num, top)
            bottom = den if bottom is None else jnp.where(mine, den, bottom)
        halves.append(top / bottom)
    attended = jnp.concatenate(halves, axis=1)
    hidden = (gate * attended).astype(jnp.bfloat16)
    return (
        rep.astype(f32) + jnp.dot(hidden, out_weight, preferred_element_type=f32)
    ).astype(jnp.bfloat16)


def slot(ref, *index):
    return ref.at[index]


def window_kernel(
    length_hbm, pair_ref, single_hbm, proj_hbm, out_weight_hbm, single_proj_hbm, single_out_hbm,
    gain_hbm, tri_weight_hbm, bias_gain_hbm, head_weight_hbm, single_gain_hbm,
    pair_out_ref, single_new_ref,
    local, tri_kept, tri_ref, single_ref, proj_ref, out_weight_ref, single_proj_ref, single_out_ref,
    gain_ref, tri_weight_ref, bias_gain_ref, head_weight_ref, single_gain_ref, length_ref,
    rest_ref, local_sem, weight_sem,
    slab, fresh, bands, bias_held, head_kept, head_sent, head_got, head_full,
    s_query, s_key, s_value, s_gate, part_sent, part_got,
    in_send, in_recv, out_send, out_recv,
    col_send, col_recv, chip_send, chip_recv, core_send, core_recv,
    head_send, head_recv, part_send, part_recv,
):
    f32 = jnp.float32
    slab_rows, cols, cols_here, channels = slab.shape
    rows, _, heads, rows_here, _ = bands.shape
    tokens = cols * cols_here
    chips = rows // 2
    row, col = lax.axis_index("row"), lax.axis_index("col")
    chip, core = row // 2, lax.rem(row, 2)
    partner = chip * 2 + 1 - core
    mesh_id = pl.DeviceIdType.MESH

    def peer(step):
        return lax.rem(col + step, cols)

    def chip_row(step):
        return lax.rem(chip + step, chips) * 2 + core

    def chip_back(step):
        return lax.rem(chip + chips - step, chips) * 2 + core

    def local_copy(part):
        span = pl.ds(part * slab_rows, slab_rows)
        return pltpu.make_async_copy(pair_ref.at[span], local.at[span], local_sem.at[part])

    weight_copies = [
        pltpu.make_async_copy(src, dst, weight_sem.at[i])
        for i, (src, dst) in enumerate(
            (
                (gain_hbm, gain_ref),
                (tri_weight_hbm, tri_weight_ref),
                (length_hbm, length_ref),
                (bias_gain_hbm, bias_gain_ref),
                (head_weight_hbm, head_weight_ref),
                (single_gain_hbm, single_gain_ref),
                (single_hbm, single_ref),
                (single_proj_hbm, single_proj_ref),
                (proj_hbm, proj_ref),
                (out_weight_hbm, out_weight_ref),
                (single_out_hbm, single_out_ref),
            )
        )
    ]
    barrier = pltpu.get_barrier_semaphore()
    for step in range(1, cols):
        pl.semaphore_signal(barrier, inc=1, device_id=(row, peer(step)), device_id_type=mesh_id)
    for step in range(1, chips):
        pl.semaphore_signal(barrier, inc=1, device_id=(chip_row(step), col), device_id_type=mesh_id)
    pl.semaphore_signal(barrier, inc=1, device_id=(partner, col), device_id_type=mesh_id)
    for copy in weight_copies[:2]:
        copy.start()
    for part in range(cols):
        local_copy(part).start()
    for copy in weight_copies[2:]:
        copy.start()
    with jax.named_scope('bar'):
        pl.semaphore_wait(barrier, cols + chips - 1)

    def remote(src, dst, send, recv, to):
        return pltpu.make_async_remote_copy(
            src_ref=src, dst_ref=dst, send_sem=send, recv_sem=recv,
            device_id=to, device_id_type=mesh_id,
        )

    near = cols // 2
    mirror = peer(near)

    def near_peer(step):
        return col // near * near + lax.rem(lax.rem(col, near) + step, near)

    own_steps = range(1, near)
    mirror_steps = range(near + 1, 2 * near)

    def col_copy(step):
        to = mirror if step == 0 else near_peer(step % near)
        src, place = (tri_ref, col) if step < near else (slot(bands, row, mirror), mirror)
        return remote(
            src, slot(bands, row, place), col_send, col_recv.at[min(step, 1)], (row, to)
        )

    def chip_copy(step):
        return remote(
            slot(bands, row), slot(bands, row), chip_send, chip_recv.at[step - 1],
            (chip_row(step), col),
        )

    def core_copy(step):
        band = chip_back(step)
        return remote(
            slot(bands, band), slot(bands, band), core_send, core_recv.at[step],
            (partner, col),
        )

    def in_copy(s, step):
        to = peer(step)
        return remote(
            slot(pair_ref, to * slab_rows + s), slot(slab, s, col),
            in_send, in_recv.at[s], (row, to),
        )

    def own_in(s):
        return pltpu.make_async_copy(
            slot(pair_ref, col * slab_rows + s), slot(slab, s, col), in_recv.at[s]
        )

    def out_copy(s, step):
        to = peer(step)
        return remote(
            slot(fresh, s, to), slot(pair_out_ref, col * slab_rows + s),
            out_send, out_recv, (row, to),
        )

    def own_out(s):
        return pltpu.make_async_copy(
            slot(fresh, s, col), slot(pair_out_ref, col * slab_rows + s), out_recv
        )

    def head_copy(step):
        to = peer(step)
        return remote(
            slot(head_sent, to), slot(head_got, col), head_send, head_recv,
            (row, to),
        )

    def part_copy(step):
        to = peer(step)
        return remote(
            slot(part_sent, to), slot(part_got, step), part_send, part_recv,
            (row, to),
        )

    def settle(ref, sem):
        pltpu.make_async_copy(ref, ref, sem).wait()

    others = pl.ds(0, cols - 1)

    def bring_row(s):
        own_in(s).start()
        for step in range(1, cols):
            in_copy(s, step).start()

    bring_row(0)
    for copy in weight_copies[:2]:
        copy.wait()
    with jax.named_scope('tri'):
        group = math.gcd(slab_rows, 6)
        for part in range(cols):
            local_copy(part).wait()

            @pl.loop(0, slab_rows // group)
            def _(i):
                for j in range(group):
                    r = part * slab_rows + i * group + j
                    tri_kept[:, r, :] = lax.dot_general(
                        tri_weight_ref[...], normalize(local[r], gain_ref[...]), NT,
                        preferred_element_type=f32,
                    )

    tri_ref[...] = tri_kept[...].astype(jnp.bfloat16)
    for step in (0, *own_steps):
        col_copy(step).start()
    own_block = pltpu.make_async_copy(tri_ref, slot(bands, row, col), col_recv.at[1])
    own_block.start()

    ahead = min(3, slab_rows)
    for s in range(1, ahead):
        bring_row(s)
    with jax.named_scope('waitmirror'):
        col_copy(0).wait_recv()
    for step in mirror_steps:
        col_copy(step).start()

    @pl.loop(ahead, slab_rows)
    def _(s):
        bring_row(s)

    for copy in weight_copies[2:]:
        copy.wait()

    with jax.named_scope('waitcols'):
        settle(slot(bands, row, others), col_recv.at[1])
    for step in range(1, chips):
        chip_copy(step).start()
    core_copy(0).start()

    with jax.named_scope('sproj'):
        s_normed = normalize(single_ref[...], single_gain_ref[...])
        s_key[...] = project_t(s_normed, single_proj_ref[1])
        s_value[...] = project_t(s_normed, single_proj_ref[2])
        width = s_key.shape[1]
        my_rows = pl.ds(pl.multiple_of(row * rows_here, rows_here), rows_here)
        for part in range(cols):

            @pl.when(col == part)
            def _():
                rest_ref[...] = single_ref[my_rows, part * width : (part + 1) * width]

        mine = normalize(
            single_ref[my_rows, :],
            single_gain_ref[...],
        )
        s_query[...] = (
            lax.dot_general(mine, single_proj_ref[0], NT, preferred_element_type=f32)
            * (LOG2E / math.sqrt(SINGLE_HEAD_DIM))
        ).astype(jnp.bfloat16)
        s_gate[...] = jax.nn.sigmoid(
            lax.dot_general(mine, single_proj_ref[3], NT, preferred_element_type=f32)
        )

    def take_band(band):
        start = pl.multiple_of(band * rows_here, rows_here)
        for part in range(cols):
            usable = (
                lax.broadcasted_iota(jnp.int32, (1, 1, cols_here), 2) + part * cols_here
                < length_ref[0]
            )
            piece = bands[band, part].astype(f32) * LOG2E
            bias_held[:, pl.ds(start, rows_here), part * cols_here : (part + 1) * cols_here] = (
                jnp.where(usable, piece, masked_value)
            )

    with jax.named_scope('bands'):
        take_band(row)
        for step in range(1, chips):
            chip_copy(step).wait_recv()
            core_copy(step).start()
            take_band(chip_back(step))
        for step in range(chips):
            core_copy(step).wait_recv()
            take_band(chip_back(step) + 1 - 2 * core)

    early = 2 * slab_rows // 3
    late = slab_rows - slab_rows // 6

    def one_row(s):
        settle(slot(slab, s), in_recv.at[s])
        rep = slab[s].reshape(tokens, channels)
        updated = row_update(
            rep, gain_ref[...], proj_ref, out_weight_ref[...], lambda head: bias_held[head]
        )
        fresh[s] = updated.reshape(cols, cols_here, channels)
        again = normalize(updated, bias_gain_ref[...])
        head_kept[:, s, :] = lax.dot_general(
            head_weight_ref[...], again, NT, preferred_element_type=f32
        )

    def send_row(s):
        own_out(s).start()
        for step in range(1, cols):
            out_copy(s, step).start()

    with jax.named_scope('rows'):
        @pl.loop(0, slab_rows)
        def _(s):
            one_row(s)

            @pl.when(s < early)
            def _():
                send_row(s)

    head_sent[...] = head_kept[...].astype(jnp.bfloat16).reshape(head_sent.shape)
    for step in range(1, cols):
        head_copy(step).start()

    @pl.loop(early, late)
    def _(s):
        send_row(s)

    with jax.named_scope('headwait'):
        settle(slot(head_got, others), head_recv)
    for part in range(cols):
        span = slice(part * slab_rows, (part + 1) * slab_rows)

        @pl.when(col == part)
        def _():
            head_full[:, span, :] = head_sent[part].astype(f32) * LOG2E

        @pl.when(col != part)
        def _():
            head_full[:, span, :] = head_got[part].astype(f32) * LOG2E

    with jax.named_scope('sattn'):
        s_heads = head_full.shape[0]
        usable = lax.broadcasted_iota(jnp.int32, (1, tokens), 1) < length_ref[0]
        head_of_lane = lax.broadcasted_iota(jnp.int32, (1, width), 1) // SINGLE_HEAD_DIM
        blended = jnp.zeros((rows_here, width), f32)
        for head in range(s_heads):
            here = head_of_lane == head
            q_head = jnp.where(here, s_query[...], jnp.zeros_like(s_query[...]))
            scores = lax.dot_general(q_head, s_key[...], NT, preferred_element_type=f32)
            scores = jnp.where(usable, scores + head_full[head], masked_value)
            exponent = jnp.exp2(scores - jnp.max(scores, axis=-1, keepdims=True))
            total = jnp.sum(exponent, axis=-1, keepdims=True)
            weights = (exponent / total).astype(jnp.bfloat16)
            blended = jnp.where(
                here, jnp.dot(weights, s_value[...], preferred_element_type=f32), blended
            )
        s_hidden = (s_gate[...] * blended).astype(jnp.bfloat16)
        share = jnp.dot(s_hidden, single_out_ref[...], preferred_element_type=f32)
        for part in range(cols):
            part_sent[part] = share[:, part * width : (part + 1) * width].astype(jnp.bfloat16)
        for step in range(1, cols):
            part_copy(step).start()

    @pl.loop(late, slab_rows)
    def _(s):
        send_row(s)

    with jax.named_scope('part'):
        total = rest_ref[...].astype(f32) + part_sent[col].astype(f32)
        settle(slot(part_got, others), part_recv)
        for step in range(1, cols):
            total = total + part_got[step].astype(f32)
        single_new_ref[...] = total.astype(jnp.bfloat16)

    with jax.named_scope('drain'):
        settle(slot(head_sent, others), head_send)
        settle(slot(part_sent, others), part_send)
        settle(slot(bands, row, others), col_send)
        settle(slot(bands, pl.ds(0, chips - 1)), chip_send)
        settle(slot(bands, pl.ds(0, chips)), core_send)
        sent = slot(local, pl.ds(0, slab_rows * (cols - 1)))
        settle(sent, in_send)
        settle(sent, out_send)
        settle(pair_out_ref, out_recv)


def per_device(
    pair_rep,
    single_rep,
    length,
    pair_gain,
    pair_proj,
    bias_weight,
    pair_out_weight,
    single_gain,
    single_proj,
    bias_norm_gain,
    single_bias_weight,
    single_out_weight,
):
    rows_here, cols_here, channels = pair_rep.shape
    rows, cols = lax.axis_size("row"), lax.axis_size("col")
    tokens = rows_here * rows
    slab_rows = rows_here // cols
    chips = rows // 2
    heads = bias_weight.shape[1]
    single_heads = single_bias_weight.shape[1]
    heads_here = single_heads // cols
    width = single_proj.shape[2]
    single_proj_t = single_proj.transpose(0, 2, 1)
    bf16, f32 = jnp.bfloat16, jnp.float32
    dma = pltpu.SemaphoreType.DMA
    anywhere = pl.BlockSpec(memory_space=pl.ANY)
    stay = pl.BlockSpec(memory_space=pltpu.HBM)
    held = pl.BlockSpec(memory_space=pltpu.VMEM)
    pair_out, single_out = pl.pallas_call(
        window_kernel,
        in_specs=[stay] * 12,
        out_specs=[anywhere, held],
        out_shape=[
            pltpu.VMEM(pair_rep.shape, bf16),
            pltpu.VMEM((rows_here, width), bf16),
        ],
        scratch_shapes=[
            pltpu.VMEM(pair_rep.shape, bf16),
            pltpu.VMEM((heads, rows_here, cols_here), f32),
            pltpu.VMEM((heads, rows_here, cols_here), bf16),
            pltpu.VMEM(single_rep.shape, bf16),
            pltpu.VMEM(pair_proj.shape, bf16),
            pltpu.VMEM(pair_out_weight.shape, bf16),
            pltpu.VMEM(single_proj_t.shape, bf16),
            pltpu.VMEM(single_out_weight.shape, bf16),
            pltpu.VMEM(pair_gain.shape, f32),
            pltpu.VMEM((heads, channels), bf16),
            pltpu.VMEM(bias_norm_gain.shape, f32),
            pltpu.VMEM((single_heads, channels), bf16),
            pltpu.VMEM(single_gain.shape, f32),
            pltpu.SMEM(length.shape, jnp.int32),
            pltpu.VMEM((rows_here, width), bf16),
            dma((cols,)),
            dma((11,)),
            pltpu.VMEM((slab_rows, cols, cols_here, channels), bf16),
            pltpu.VMEM((slab_rows, cols, cols_here, channels), bf16),
            pltpu.VMEM((rows, cols, heads, rows_here, cols_here), bf16),
            pltpu.VMEM((heads, tokens, tokens), f32),
            pltpu.VMEM((single_heads, slab_rows, tokens), f32),
            pltpu.VMEM((cols, heads_here, slab_rows, tokens), bf16),
            pltpu.VMEM((cols, heads_here, slab_rows, tokens), bf16),
            pltpu.VMEM((heads_here, rows_here, tokens), f32),
            pltpu.VMEM((rows_here, width), bf16),
            pltpu.VMEM((tokens, width), bf16),
            pltpu.VMEM((tokens, width), bf16),
            pltpu.VMEM((rows_here, width), f32),
            pltpu.VMEM((cols, rows_here, width), bf16),
            pltpu.VMEM((cols, rows_here, width), bf16),
            dma,
            dma((slab_rows,)),
            dma,
            dma,
            dma,
            dma((2,)),
            dma,
            dma((chips - 1,)),
            dma,
            dma((chips,)),
            dma,
            dma,
            dma,
            dma,
        ],
        compiler_params=pltpu.CompilerParams(
            collective_id=0, has_side_effects=True, vmem_limit_bytes=56 * 2**20
        ),
        name="window",
    )(
        length, pair_rep, single_rep, pair_proj, pair_out_weight, single_proj_t, single_out_weight,
        pair_gain, bias_weight.T, bias_norm_gain, single_bias_weight.T, single_gain,
    )
    return (pair_out, single_out)


def solution(mesh):
    in_specs = (
        P("row", "col", None),
        P(),
        P(),
        P(),
        P(),
        P(),
        P(),
        P(),
        P(None, None, "col"),
        P(),
        P(),
        P("col", None),
    )
    out_specs = (P("row", "col", None), P("row", "col"))
    return jax.shard_map(
        per_device, mesh=mesh, in_specs=in_specs, out_specs=out_specs, check_vma=False
    )
```

```python
import math

import jax
import jax.numpy as jnp
from jax import lax
from jax.experimental import pallas as pl
from jax.experimental.pallas import tpu as pltpu
from jax.sharding import PartitionSpec as P

PAIR_HEADS = 8
PAIR_HEAD_DIM = 32
SINGLE_HEAD_DIM = 48
LOG2E = math.log2(math.e)

masked_value = -1e30
NT = (((1,), (1,)), ((), ()))


def normalize(values, scales):
    floated = values.astype(jnp.float32)
    center = jnp.mean(floated, axis=-1, keepdims=True)
    spread = jnp.mean(jnp.square(floated - center), axis=-1, keepdims=True)
    return ((floated - center) * lax.rsqrt(spread + 1e-05) * scales).astype(jnp.bfloat16)


def project(inputs, matrix):
    return jnp.dot(inputs, matrix, preferred_element_type=jnp.float32).astype(jnp.bfloat16)


def project_t(inputs, matrix):
    return lax.dot_general(inputs, matrix, NT, preferred_element_type=jnp.float32).astype(
        jnp.bfloat16
    )


def row_update(rep, gain, proj_ref, out_weight, bias_of):
    channels = rep.shape[1]
    half = channels // 2
    heads_per_half = PAIR_HEADS // 2
    normed = normalize(rep, gain)
    f32 = jnp.float32
    query = jnp.dot(normed, proj_ref[0], preferred_element_type=f32)
    query = (query * (LOG2E / math.sqrt(PAIR_HEAD_DIM))).astype(jnp.bfloat16)
    key = project(normed, proj_ref[1])
    value = project(normed, proj_ref[2])
    gate = jax.nn.sigmoid(jnp.dot(normed, proj_ref[3], preferred_element_type=f32))
    head_of_lane = lax.broadcasted_iota(jnp.int32, (1, half), 1) // PAIR_HEAD_DIM
    halves = []
    for side in range(2):
        span = slice(side * half, (side + 1) * half)
        q_half, k_half, v_half = query[:, span], key[:, span], value[:, span]
        top = bottom = None
        for sub in range(heads_per_half):
            head = side * heads_per_half + sub
            mine = head_of_lane == sub
            q_head = jnp.where(mine, q_half, jnp.zeros_like(q_half))
            scores = lax.dot_general(q_head, k_half, NT, preferred_element_type=f32)
            scores = scores + bias_of(head)
            peak = jnp.max(scores, axis=-1, keepdims=True)
            exponent = jnp.exp2(scores - peak).astype(jnp.bfloat16)
            v_ext = jnp.concatenate([v_half, jnp.ones_like(v_half)], axis=1)
            both = jnp.dot(exponent, v_ext, preferred_element_type=f32)
            num, den = both[:, :half], both[:, half:]
            top = num if top is None else jnp.where(mine, num, top)
            bottom = den if bottom is None else jnp.where(mine, den, bottom)
        halves.append(top / bottom)
    attended = jnp.concatenate(halves, axis=1)
    hidden = (gate * attended).astype(jnp.bfloat16)
    return (
        rep.astype(f32) + jnp.dot(hidden, out_weight, preferred_element_type=f32)
    ).astype(jnp.bfloat16)


def slot(ref, *index):
    return ref.at[index]


def window_kernel(
    length_hbm, pair_ref, single_hbm, proj_hbm, out_weight_hbm, single_proj_hbm, single_out_hbm,
    gain_hbm, tri_weight_hbm, bias_gain_hbm, head_weight_hbm, single_gain_hbm,
    pair_out_ref, single_new_ref,
    local, tri_kept, tri_ref, single_ref, proj_ref, out_weight_ref, single_proj_ref, single_out_ref,
    gain_ref, tri_weight_ref, bias_gain_ref, head_weight_ref, single_gain_ref, length_ref,
    rest_ref, local_sem, weight_sem,
    slab, fresh, bands, bias_held, head_kept, head_sent, head_got, head_full,
    s_query, s_key, s_value, s_gate, part_sent, part_got, merged_sent, merged_got,
    in_send, in_recv, out_send, out_recv,
    col_send, col_recv, chip_send, chip_recv, core_send, core_recv,
    head_send, head_recv, part_send, part_recv, merged_send, merged_recv,
):
    f32 = jnp.float32
    slab_rows, cols, cols_here, channels = slab.shape
    rows, _, heads, rows_here, _ = bands.shape
    tokens = cols * cols_here
    chips = rows // 2
    row, col = lax.axis_index("row"), lax.axis_index("col")
    chip, core = row // 2, lax.rem(row, 2)
    partner = chip * 2 + 1 - core
    mesh_id = pl.DeviceIdType.MESH

    def peer(step):
        return lax.rem(col + step, cols)

    def chip_row(step):
        return lax.rem(chip + step, chips) * 2 + core

    def chip_back(step):
        return lax.rem(chip + chips - step, chips) * 2 + core

    def local_copy(part):
        span = pl.ds(part * slab_rows, slab_rows)
        return pltpu.make_async_copy(pair_ref.at[span], local.at[span], local_sem.at[part])

    weight_copies = [
        pltpu.make_async_copy(src, dst, weight_sem.at[i])
        for i, (src, dst) in enumerate(
            (
                (gain_hbm, gain_ref),
                (tri_weight_hbm, tri_weight_ref),
                (length_hbm, length_ref),
                (bias_gain_hbm, bias_gain_ref),
                (head_weight_hbm, head_weight_ref),
                (single_gain_hbm, single_gain_ref),
                (single_hbm, single_ref),
                (single_proj_hbm, single_proj_ref),
                (proj_hbm, proj_ref),
                (out_weight_hbm, out_weight_ref),
                (single_out_hbm, single_out_ref),
            )
        )
    ]
    barrier = pltpu.get_barrier_semaphore()
    for step in range(1, cols):
        pl.semaphore_signal(barrier, inc=1, device_id=(row, peer(step)), device_id_type=mesh_id)
    for step in range(1, chips):
        pl.semaphore_signal(barrier, inc=1, device_id=(chip_row(step), col), device_id_type=mesh_id)
    pl.semaphore_signal(barrier, inc=1, device_id=(partner, col), device_id_type=mesh_id)
    for copy in weight_copies[:2]:
        copy.start()
    for part in range(cols):
        local_copy(part).start()
    for copy in weight_copies[2:]:
        copy.start()
    with jax.named_scope('bar'):
        pl.semaphore_wait(barrier, cols + chips - 1)

    def remote(src, dst, send, recv, to):
        return pltpu.make_async_remote_copy(
            src_ref=src, dst_ref=dst, send_sem=send, recv_sem=recv,
            device_id=to, device_id_type=mesh_id,
        )

    near = cols // 2
    mirror = peer(near)

    def near_peer(step):
        return col // near * near + lax.rem(lax.rem(col, near) + step, near)

    own_steps = range(1, near)
    mirror_steps = range(near + 1, 2 * near)

    def col_copy(step):
        to = mirror if step == 0 else near_peer(step % near)
        src, place = (tri_ref, col) if step < near else (slot(bands, row, mirror), mirror)
        return remote(
            src, slot(bands, row, place), col_send, col_recv.at[min(step, 1)], (row, to)
        )

    def chip_copy(step):
        return remote(
            slot(bands, row), slot(bands, row), chip_send, chip_recv.at[step - 1],
            (chip_row(step), col),
        )

    def core_copy(step):
        band = chip_back(step)
        return remote(
            slot(bands, band), slot(bands, band), core_send, core_recv.at[step],
            (partner, col),
        )

    def in_copy(s, step):
        to = peer(step)
        return remote(
            slot(pair_ref, to * slab_rows + s), slot(slab, s, col),
            in_send, in_recv.at[s], (row, to),
        )

    def own_in(s):
        return pltpu.make_async_copy(
            slot(pair_ref, col * slab_rows + s), slot(slab, s, col), in_recv.at[s]
        )

    def out_copy(s, step):
        to = peer(step)
        return remote(
            slot(fresh, s, to), slot(pair_out_ref, col * slab_rows + s),
            out_send, out_recv, (row, to),
        )

    def own_out(s):
        return pltpu.make_async_copy(
            slot(fresh, s, col), slot(pair_out_ref, col * slab_rows + s), out_recv
        )

    def head_copy(step):
        to = peer(step)
        return remote(
            slot(head_sent, to), slot(head_got, col), head_send, head_recv,
            (row, to),
        )

    lane, half = lax.rem(col, near), col // near

    def part_copy(step):
        return remote(
            slot(part_sent, lax.rem(lane + step, near)), slot(part_got, step),
            part_send, part_recv, (row, near_peer(step)),
        )

    def merged_copy():
        return remote(merged_sent, merged_got, merged_send, merged_recv, (row, mirror))

    def settle(ref, sem):
        pltpu.make_async_copy(ref, ref, sem).wait()

    others = pl.ds(0, cols - 1)

    def bring_row(s):
        own_in(s).start()
        for step in range(1, cols):
            in_copy(s, step).start()

    bring_row(0)
    for copy in weight_copies[:2]:
        copy.wait()
    with jax.named_scope('tri'):
        group = math.gcd(slab_rows, 6)
        for part in range(cols):
            local_copy(part).wait()

            @pl.loop(0, slab_rows // group)
            def _(i):
                for j in range(group):
                    r = part * slab_rows + i * group + j
                    tri_kept[:, r, :] = lax.dot_general(
                        tri_weight_ref[...], normalize(local[r], gain_ref[...]), NT,
                        preferred_element_type=f32,
                    )

    tri_ref[...] = tri_kept[...].astype(jnp.bfloat16)
    for step in (0, *own_steps):
        col_copy(step).start()
    own_block = pltpu.make_async_copy(tri_ref, slot(bands, row, col), col_recv.at[1])
    own_block.start()

    ahead = min(3, slab_rows)
    for s in range(1, ahead):
        bring_row(s)
    with jax.named_scope('waitmirror'):
        col_copy(0).wait_recv()
    for step in mirror_steps:
        col_copy(step).start()

    @pl.loop(ahead, slab_rows)
    def _(s):
        bring_row(s)

    for copy in weight_copies[2:]:
        copy.wait()

    with jax.named_scope('waitcols'):
        settle(slot(bands, row, others), col_recv.at[1])
    for step in range(1, chips):
        chip_copy(step).start()
    core_copy(0).start()

    with jax.named_scope('sproj'):
        s_normed = normalize(single_ref[...], single_gain_ref[...])
        s_key[...] = project_t(s_normed, single_proj_ref[1])
        s_value[...] = project_t(s_normed, single_proj_ref[2])
        width = s_key.shape[1]
        my_rows = pl.ds(pl.multiple_of(row * rows_here, rows_here), rows_here)
        for part in range(cols):

            @pl.when(col == part)
            def _():
                rest_ref[...] = single_ref[my_rows, part * width : (part + 1) * width]

        mine = normalize(
            single_ref[my_rows, :],
            single_gain_ref[...],
        )
        s_query[...] = (
            lax.dot_general(mine, single_proj_ref[0], NT, preferred_element_type=f32)
            * (LOG2E / math.sqrt(SINGLE_HEAD_DIM))
        ).astype(jnp.bfloat16)
        s_gate[...] = jax.nn.sigmoid(
            lax.dot_general(mine, single_proj_ref[3], NT, preferred_element_type=f32)
        )

    def take_band(band):
        start = pl.multiple_of(band * rows_here, rows_here)
        for part in range(cols):
            usable = (
                lax.broadcasted_iota(jnp.int32, (1, 1, cols_here), 2) + part * cols_here
                < length_ref[0]
            )
            piece = bands[band, part].astype(f32) * LOG2E
            bias_held[:, pl.ds(start, rows_here), part * cols_here : (part + 1) * cols_here] = (
                jnp.where(usable, piece, masked_value)
            )

    with jax.named_scope('bands'):
        take_band(row)
        for step in range(1, chips):
            chip_copy(step).wait_recv()
            core_copy(step).start()
            take_band(chip_back(step))
        for step in range(chips):
            core_copy(step).wait_recv()
            take_band(chip_back(step) + 1 - 2 * core)

    early = 2 * slab_rows // 3
    late = slab_rows - slab_rows // 6
    last = slab_rows - slab_rows // 12

    def one_row(s):
        settle(slot(slab, s), in_recv.at[s])
        rep = slab[s].reshape(tokens, channels)
        updated = row_update(
            rep, gain_ref[...], proj_ref, out_weight_ref[...], lambda head: bias_held[head]
        )
        fresh[s] = updated.reshape(cols, cols_here, channels)
        again = normalize(updated, bias_gain_ref[...])
        head_kept[:, s, :] = lax.dot_general(
            head_weight_ref[...], again, NT, preferred_element_type=f32
        )

    def send_row(s):
        own_out(s).start()
        for step in range(1, cols):
            out_copy(s, step).start()

    with jax.named_scope('rows'):
        @pl.loop(0, slab_rows)
        def _(s):
            one_row(s)

            @pl.when(s < early)
            def _():
                send_row(s)

    head_sent[...] = head_kept[...].astype(jnp.bfloat16).reshape(head_sent.shape)
    for step in range(1, cols):
        head_copy(step).start()

    @pl.loop(early, late)
    def _(s):
        send_row(s)

    with jax.named_scope('headwait'):
        settle(slot(head_got, others), head_recv)
    for part in range(cols):
        span = slice(part * slab_rows, (part + 1) * slab_rows)

        @pl.when(col == part)
        def _():
            head_full[:, span, :] = head_sent[part].astype(f32) * LOG2E

        @pl.when(col != part)
        def _():
            head_full[:, span, :] = head_got[part].astype(f32) * LOG2E

    with jax.named_scope('sattn'):
        s_heads = head_full.shape[0]
        usable = lax.broadcasted_iota(jnp.int32, (1, tokens), 1) < length_ref[0]
        head_of_lane = lax.broadcasted_iota(jnp.int32, (1, width), 1) // SINGLE_HEAD_DIM
        blended = jnp.zeros((rows_here, width), f32)
        for head in range(s_heads):
            here = head_of_lane == head
            q_head = jnp.where(here, s_query[...], jnp.zeros_like(s_query[...]))
            scores = lax.dot_general(q_head, s_key[...], NT, preferred_element_type=f32)
            scores = jnp.where(usable, scores + head_full[head], masked_value)
            exponent = jnp.exp2(scores - jnp.max(scores, axis=-1, keepdims=True))
            total = jnp.sum(exponent, axis=-1, keepdims=True)
            weights = (exponent / total).astype(jnp.bfloat16)
            blended = jnp.where(
                here, jnp.dot(weights, s_value[...], preferred_element_type=f32), blended
            )
        s_hidden = (s_gate[...] * blended).astype(jnp.bfloat16)
        share = jnp.dot(s_hidden, single_out_ref[...], preferred_element_type=f32)
        for part in range(cols):
            part_sent[part % near, (half + part // near) % 2] = share[
                :, part * width : (part + 1) * width
            ].astype(jnp.bfloat16)
        for step in own_steps:
            part_copy(step).start()

    @pl.loop(late, last)
    def _(s):
        send_row(s)

    with jax.named_scope('part'):
        nearby = pl.ds(0, near - 1)
        settle(slot(part_got, nearby), part_recv)
        merged = part_sent[lane, 1].astype(f32)
        total = rest_ref[...].astype(f32) + part_sent[lane, 0].astype(f32)
        for step in own_steps:
            merged = merged + part_got[step, 1].astype(f32)
            total = total + part_got[step, 0].astype(f32)
        merged_sent[...] = merged.astype(jnp.bfloat16)
        merged_copy().start()

    @pl.loop(last, slab_rows)
    def _(s):
        send_row(s)

    with jax.named_scope('merge'):
        merged_copy().wait()
        single_new_ref[...] = (total + merged_got[...].astype(f32)).astype(jnp.bfloat16)

    with jax.named_scope('drain'):
        settle(slot(head_sent, others), head_send)
        settle(slot(part_sent, nearby), part_send)
        settle(slot(bands, row, others), col_send)
        settle(slot(bands, pl.ds(0, chips - 1)), chip_send)
        settle(slot(bands, pl.ds(0, chips)), core_send)
        sent = slot(local, pl.ds(0, slab_rows * (cols - 1)))
        settle(sent, in_send)
        settle(sent, out_send)
        settle(pair_out_ref, out_recv)


def store_kernel(pair_ref, single_ref, pair_out_ref, single_out_ref, pair_sem, single_sem):
    rows = pair_ref.shape[0]
    chunks = math.gcd(rows, 8)
    single = pltpu.make_async_copy(single_ref, single_out_ref, single_sem)
    single.start()
    for i in range(chunks):
        span = pl.ds(i * (rows // chunks), rows // chunks)
        pltpu.make_async_copy(pair_ref.at[span], pair_out_ref.at[span], pair_sem).start()
    single.wait()
    pltpu.make_async_copy(pair_ref, pair_out_ref, pair_sem).wait()


def store(pair, single):
    held = pl.BlockSpec(memory_space=pltpu.VMEM)
    away = pl.BlockSpec(memory_space=pltpu.HBM)
    return pl.pallas_call(
        store_kernel,
        in_specs=[held, held],
        out_specs=[away, away],
        out_shape=[jax.ShapeDtypeStruct(x.shape, x.dtype) for x in (pair, single)],
        scratch_shapes=[pltpu.SemaphoreType.DMA, pltpu.SemaphoreType.DMA],
        compiler_params=pltpu.CompilerParams(vmem_limit_bytes=4 * 2**20),
        name="store",
    )(*(pltpu.with_memory_space_constraint(x, pltpu.VMEM) for x in (pair, single)))


def per_device(
    pair_rep,
    single_rep,
    length,
    pair_gain,
    pair_proj,
    bias_weight,
    pair_out_weight,
    single_gain,
    single_proj,
    bias_norm_gain,
    single_bias_weight,
    single_out_weight,
):
    rows_here, cols_here, channels = pair_rep.shape
    rows, cols = lax.axis_size("row"), lax.axis_size("col")
    tokens = rows_here * rows
    slab_rows = rows_here // cols
    chips = rows // 2
    heads = bias_weight.shape[1]
    single_heads = single_bias_weight.shape[1]
    heads_here = single_heads // cols
    width = single_proj.shape[2]
    single_proj_t = single_proj.transpose(0, 2, 1)
    bf16, f32 = jnp.bfloat16, jnp.float32
    dma = pltpu.SemaphoreType.DMA
    anywhere = pl.BlockSpec(memory_space=pl.ANY)
    stay = pl.BlockSpec(memory_space=pltpu.HBM)
    held = pl.BlockSpec(memory_space=pltpu.VMEM)
    pair_out, single_out = pl.pallas_call(
        window_kernel,
        in_specs=[stay] * 12,
        out_specs=[anywhere, held],
        out_shape=[
            pltpu.VMEM(pair_rep.shape, bf16),
            pltpu.VMEM((rows_here, width), bf16),
        ],
        scratch_shapes=[
            pltpu.VMEM(pair_rep.shape, bf16),
            pltpu.VMEM((heads, rows_here, cols_here), f32),
            pltpu.VMEM((heads, rows_here, cols_here), bf16),
            pltpu.VMEM(single_rep.shape, bf16),
            pltpu.VMEM(pair_proj.shape, bf16),
            pltpu.VMEM(pair_out_weight.shape, bf16),
            pltpu.VMEM(single_proj_t.shape, bf16),
            pltpu.VMEM(single_out_weight.shape, bf16),
            pltpu.VMEM(pair_gain.shape, f32),
            pltpu.VMEM((heads, channels), bf16),
            pltpu.VMEM(bias_norm_gain.shape, f32),
            pltpu.VMEM((single_heads, channels), bf16),
            pltpu.VMEM(single_gain.shape, f32),
            pltpu.SMEM(length.shape, jnp.int32),
            pltpu.VMEM((rows_here, width), bf16),
            dma((cols,)),
            dma((11,)),
            pltpu.VMEM((slab_rows, cols, cols_here, channels), bf16),
            pltpu.VMEM((slab_rows, cols, cols_here, channels), bf16),
            pltpu.VMEM((rows, cols, heads, rows_here, cols_here), bf16),
            pltpu.VMEM((heads, tokens, tokens), f32),
            pltpu.VMEM((single_heads, slab_rows, tokens), f32),
            pltpu.VMEM((cols, heads_here, slab_rows, tokens), bf16),
            pltpu.VMEM((cols, heads_here, slab_rows, tokens), bf16),
            pltpu.VMEM((heads_here, rows_here, tokens), f32),
            pltpu.VMEM((rows_here, width), bf16),
            pltpu.VMEM((tokens, width), bf16),
            pltpu.VMEM((tokens, width), bf16),
            pltpu.VMEM((rows_here, width), f32),
            pltpu.VMEM((cols // 2, 2, rows_here, width), bf16),
            pltpu.VMEM((cols // 2, 2, rows_here, width), bf16),
            pltpu.VMEM((rows_here, width), bf16),
            pltpu.VMEM((rows_here, width), bf16),
            dma,
            dma((slab_rows,)),
            dma,
            dma,
            dma,
            dma((2,)),
            dma,
            dma((chips - 1,)),
            dma,
            dma((chips,)),
            dma,
            dma,
            dma,
            dma,
            dma,
            dma,
        ],
        compiler_params=pltpu.CompilerParams(
            collective_id=0, has_side_effects=True, vmem_limit_bytes=56 * 2**20
        ),
        name="window",
    )(
        length, pair_rep, single_rep, pair_proj, pair_out_weight, single_proj_t, single_out_weight,
        pair_gain, bias_weight.T, bias_norm_gain, single_bias_weight.T, single_gain,
    )
    return store(pair_out, single_out)


def solution(mesh):
    in_specs = (
        P("row", "col", None),
        P(),
        P(),
        P(),
        P(),
        P(),
        P(),
        P(),
        P(None, None, "col"),
        P(),
        P(),
        P("col", None),
    )
    out_specs = (P("row", "col", None), P("row", "col"))
    return jax.shard_map(
        per_device, mesh=mesh, in_specs=in_specs, out_specs=out_specs, check_vma=False
    )
```

```python
import math

import jax
import jax.numpy as jnp
from jax import lax
from jax.experimental import pallas as pl
from jax.experimental.pallas import tpu as pltpu
from jax.sharding import PartitionSpec as P

PAIR_HEADS = 8
PAIR_HEAD_DIM = 32
SINGLE_HEAD_DIM = 48
LOG2E = math.log2(math.e)

LANES = 128
masked_value = -1e30
NT = (((1,), (1,)), ((), ()))


def normalize(values, scales):
    floated = values.astype(jnp.float32)
    center = jnp.mean(floated, axis=-1, keepdims=True)
    spread = jnp.mean(jnp.square(floated - center), axis=-1, keepdims=True)
    return ((floated - center) * lax.rsqrt(spread + 1e-05) * scales).astype(jnp.bfloat16)


def project(inputs, matrix):
    return jnp.dot(inputs, matrix, preferred_element_type=jnp.float32).astype(jnp.bfloat16)


def project_t(inputs, matrix):
    return lax.dot_general(inputs, matrix, NT, preferred_element_type=jnp.float32).astype(
        jnp.bfloat16
    )


def row_update(rep, gain, proj_ref, out_weight, bias_of):
    channels = rep.shape[1]
    half = channels // 2
    heads_per_half = PAIR_HEADS // 2
    normed = normalize(rep, gain)
    f32 = jnp.float32
    query = jnp.dot(normed, proj_ref[0], preferred_element_type=f32)
    query = (query * (LOG2E / math.sqrt(PAIR_HEAD_DIM))).astype(jnp.bfloat16)
    key = project(normed, proj_ref[1])
    value = project(normed, proj_ref[2])
    gate = jax.nn.sigmoid(jnp.dot(normed, proj_ref[3], preferred_element_type=f32))
    head_of_lane = lax.broadcasted_iota(jnp.int32, (1, half), 1) // PAIR_HEAD_DIM
    halves = []
    for side in range(2):
        span = slice(side * half, (side + 1) * half)
        q_half, k_half, v_half = query[:, span], key[:, span], value[:, span]
        top = bottom = None
        for sub in range(heads_per_half):
            head = side * heads_per_half + sub
            mine = head_of_lane == sub
            q_head = jnp.where(mine, q_half, jnp.zeros_like(q_half))
            scores = lax.dot_general(q_head, k_half, NT, preferred_element_type=f32)
            scores = scores + bias_of(head)
            peak = jnp.max(scores, axis=-1, keepdims=True)
            exponent = jnp.exp2(scores - peak).astype(jnp.bfloat16)
            v_ext = jnp.concatenate([v_half, jnp.ones_like(v_half)], axis=1)
            both = jnp.dot(exponent, v_ext, preferred_element_type=f32)
            num, den = both[:, :half], both[:, half:]
            top = num if top is None else jnp.where(mine, num, top)
            bottom = den if bottom is None else jnp.where(mine, den, bottom)
        halves.append(top / bottom)
    attended = jnp.concatenate(halves, axis=1)
    hidden = (gate * attended).astype(jnp.bfloat16)
    return (
        rep.astype(f32) + jnp.dot(hidden, out_weight, preferred_element_type=f32)
    ).astype(jnp.bfloat16)


def slot(ref, *index):
    return ref.at[index]


def window_kernel(
    length_hbm, pair_ref, single_hbm, proj_hbm, out_weight_hbm, single_proj_hbm, single_out_hbm,
    gain_hbm, tri_weight_hbm, bias_gain_hbm, head_weight_hbm, single_gain_hbm,
    pair_out_ref, single_new_ref,
    local, tri_kept, tri_ref, single_ref, proj_ref, out_weight_ref, single_proj_ref, single_out_ref,
    gain_ref, tri_weight_ref, bias_gain_ref, head_weight_ref, single_gain_ref, length_ref,
    rest_ref, local_sem, weight_sem,
    slab, fresh, bands, bias_held, head_kept, head_sent, head_got, head_full,
    s_query, s_key, s_value, s_gate, part_sent, part_got, merged_sent, merged_got,
    in_send, in_recv, out_send, out_recv,
    col_send, col_recv, chip_send, chip_recv, core_send, core_recv,
    head_send, head_recv, part_send, part_recv, merged_send, merged_recv,
):
    f32 = jnp.float32
    slab_rows, cols, cols_here, channels = slab.shape
    rows, _, bundles, rows_here, _ = bands.shape
    heads_in = tri_kept.shape[0] // bundles
    tokens = cols * cols_here
    chips = rows // 2
    s_heads = head_full.shape[0]
    row, col = lax.axis_index("row"), lax.axis_index("col")
    chip, core = row // 2, lax.rem(row, 2)
    partner = chip * 2 + 1 - core
    mesh_id = pl.DeviceIdType.MESH

    def peer(step):
        return lax.rem(col + step, cols)

    def chip_row(step):
        return lax.rem(chip + step, chips) * 2 + core

    def chip_back(step):
        return lax.rem(chip + chips - step, chips) * 2 + core

    def local_copy(part):
        span = pl.ds(part * slab_rows, slab_rows)
        return pltpu.make_async_copy(pair_ref.at[span], local.at[span], local_sem.at[part])

    weight_copies = [
        pltpu.make_async_copy(src, dst, weight_sem.at[i])
        for i, (src, dst) in enumerate(
            (
                (gain_hbm, gain_ref),
                (tri_weight_hbm, tri_weight_ref),
                (length_hbm, length_ref),
                (bias_gain_hbm, bias_gain_ref),
                (head_weight_hbm, head_weight_ref),
                (single_gain_hbm, single_gain_ref),
                (single_hbm, single_ref),
                (single_proj_hbm, single_proj_ref),
                (proj_hbm, proj_ref),
                (out_weight_hbm, out_weight_ref),
                (single_out_hbm, single_out_ref),
            )
        )
    ]
    barrier = pltpu.get_barrier_semaphore()
    for step in range(1, cols):
        pl.semaphore_signal(barrier, inc=1, device_id=(row, peer(step)), device_id_type=mesh_id)
    for step in range(1, chips):
        pl.semaphore_signal(barrier, inc=1, device_id=(chip_row(step), col), device_id_type=mesh_id)
    pl.semaphore_signal(barrier, inc=1, device_id=(partner, col), device_id_type=mesh_id)
    for copy in weight_copies[:2]:
        copy.start()
    for part in range(cols):
        local_copy(part).start()
    for copy in weight_copies[2:]:
        copy.start()
    with jax.named_scope('bar'):
        pl.semaphore_wait(barrier, cols + chips - 1)

    def remote(src, dst, send, recv, to):
        return pltpu.make_async_remote_copy(
            src_ref=src, dst_ref=dst, send_sem=send, recv_sem=recv,
            device_id=to, device_id_type=mesh_id,
        )

    near = cols // 2
    mirror = peer(near)

    def near_peer(step):
        return col // near * near + lax.rem(lax.rem(col, near) + step, near)

    own_steps = range(1, near)
    mirror_steps = range(near + 1, 2 * near)

    def col_copy(step):
        to = mirror if step == 0 else near_peer(step % near)
        src, place = (tri_ref, col) if step < near else (slot(bands, row, mirror), mirror)
        return remote(
            src, slot(bands, row, place), col_send, col_recv.at[min(step, 1)], (row, to)
        )

    def chip_copy(step):
        return remote(
            slot(bands, row), slot(bands, row), chip_send, chip_recv.at[step - 1],
            (chip_row(step), col),
        )

    def core_copy(step):
        band = chip_back(step)
        return remote(
            slot(bands, band), slot(bands, band), core_send, core_recv.at[step],
            (partner, col),
        )

    def in_copy(s, step):
        to = peer(step)
        return remote(
            slot(pair_ref, to * slab_rows + s), slot(slab, s, col),
            in_send, in_recv.at[s], (row, to),
        )

    def own_in(s):
        return pltpu.make_async_copy(
            slot(pair_ref, col * slab_rows + s), slot(slab, s, col), in_recv.at[s]
        )

    def out_copy(s, step):
        to = peer(step)
        return remote(
            slot(fresh, s, to), slot(pair_out_ref, col * slab_rows + s),
            out_send, out_recv, (row, to),
        )

    def own_out(s):
        return pltpu.make_async_copy(
            slot(fresh, s, col), slot(pair_out_ref, col * slab_rows + s), out_recv
        )

    def head_copy(step):
        to = peer(step)
        return remote(
            slot(head_sent, to), slot(head_got, col), head_send, head_recv,
            (row, to),
        )

    lane, half = lax.rem(col, near), col // near

    def part_copy(step):
        return remote(
            slot(part_sent, lax.rem(lane + step, near)), slot(part_got, step),
            part_send, part_recv, (row, near_peer(step)),
        )

    def merged_copy():
        return remote(merged_sent, merged_got, merged_send, merged_recv, (row, mirror))

    def settle(ref, sem):
        pltpu.make_async_copy(ref, ref, sem).wait()

    others = pl.ds(0, cols - 1)

    def bring_row(s):
        own_in(s).start()
        for step in range(1, cols):
            in_copy(s, step).start()

    bring_row(0)
    for copy in weight_copies[:2]:
        copy.wait()
    with jax.named_scope('tri'):
        group = math.gcd(slab_rows, 6)
        for part in range(cols):
            local_copy(part).wait()

            @pl.loop(0, slab_rows // group)
            def _(i):
                for j in range(group):
                    r = part * slab_rows + i * group + j
                    tri_kept[:, r, :] = lax.dot_general(
                        tri_weight_ref[...], normalize(local[r], gain_ref[...]), NT,
                        preferred_element_type=f32,
                    )

    for bundle in range(bundles):
        tri_ref[bundle] = jnp.concatenate(
            [tri_kept[bundle * heads_in + i] for i in range(heads_in)], axis=1
        ).astype(jnp.bfloat16)
    for step in (0, *own_steps):
        col_copy(step).start()
    own_block = pltpu.make_async_copy(tri_ref, slot(bands, row, col), col_recv.at[1])
    own_block.start()

    ahead = min(3, slab_rows)
    for s in range(1, ahead):
        bring_row(s)
    with jax.named_scope('waitmirror'):
        col_copy(0).wait_recv()
    for step in mirror_steps:
        col_copy(step).start()

    @pl.loop(ahead, slab_rows)
    def _(s):
        bring_row(s)

    for copy in weight_copies[2:]:
        copy.wait()

    with jax.named_scope('waitcols'):
        settle(slot(bands, row, others), col_recv.at[1])
    for step in range(1, chips):
        chip_copy(step).start()
    core_copy(0).start()

    with jax.named_scope('sproj'):
        s_normed = normalize(single_ref[...], single_gain_ref[...])
        s_key[...] = project_t(s_normed, single_proj_ref[1])
        s_value[...] = project_t(s_normed, single_proj_ref[2])
        width = s_key.shape[1]
        my_rows = pl.ds(pl.multiple_of(row * rows_here, rows_here), rows_here)
        for part in range(cols):

            @pl.when(col == part)
            def _():
                rest_ref[...] = single_ref[my_rows, part * width : (part + 1) * width]

        mine = normalize(
            single_ref[my_rows, :],
            single_gain_ref[...],
        )
        s_query[...] = (
            lax.dot_general(mine, single_proj_ref[0], NT, preferred_element_type=f32)
            * (LOG2E / math.sqrt(SINGLE_HEAD_DIM))
        ).astype(jnp.bfloat16)
        s_gate[...] = jax.nn.sigmoid(
            lax.dot_general(mine, single_proj_ref[3], NT, preferred_element_type=f32)
        )

    def take_band(band):
        start = pl.multiple_of(band * rows_here, rows_here)
        for part in range(cols):
            usable = (
                lax.broadcasted_iota(jnp.int32, (1, cols_here), 1) + part * cols_here
                < length_ref[0]
            )
            place = (pl.ds(start, rows_here), slice(part * cols_here, (part + 1) * cols_here))
            for bundle in range(bundles):
                piece = bands[band, part, bundle].astype(f32) * LOG2E
                for i in range(heads_in):
                    bias_held[bundle * heads_in + i, *place] = jnp.where(
                        usable, piece[:, i * cols_here : (i + 1) * cols_here], masked_value
                    )

    with jax.named_scope('bands'):
        take_band(row)
        for step in range(1, chips):
            chip_copy(step).wait_recv()
            core_copy(step).start()
            take_band(chip_back(step))
        for step in range(chips):
            core_copy(step).wait_recv()
            take_band(chip_back(step) + 1 - 2 * core)

    early = 2 * slab_rows // 3
    late = slab_rows - slab_rows // 6
    last = slab_rows - slab_rows // 12

    def one_row(s):
        settle(slot(slab, s), in_recv.at[s])
        rep = slab[s].reshape(tokens, channels)
        updated = row_update(
            rep, gain_ref[...], proj_ref, out_weight_ref[...], lambda head: bias_held[head]
        )
        fresh[s] = updated.reshape(cols, cols_here, channels)
        again = normalize(updated, bias_gain_ref[...])
        found = lax.dot_general(head_weight_ref[...], again, NT, preferred_element_type=f32)
        for head in range(found.shape[0]):
            line = pl.ds(head % s_heads * slab_rows + s, 1)
            head_kept[head // s_heads, line, :] = found[head : head + 1]

    def send_row(s):
        own_out(s).start()
        for step in range(1, cols):
            out_copy(s, step).start()

    with jax.named_scope('rows'):
        @pl.loop(0, slab_rows)
        def _(s):
            one_row(s)

            @pl.when(s < early)
            def _():
                send_row(s)

    head_sent[...] = head_kept[...].astype(jnp.bfloat16)
    for step in range(1, cols):
        head_copy(step).start()

    @pl.loop(early, late)
    def _(s):
        send_row(s)

    with jax.named_scope('headwait'):
        settle(slot(head_got, others), head_recv)
    for part in range(cols):
        span = slice(part * slab_rows, (part + 1) * slab_rows)

        def fill_head(source):
            block = source[part].astype(f32) * LOG2E
            for head in range(s_heads):
                head_full[head, span, :] = block[head * slab_rows : (head + 1) * slab_rows]

        @pl.when(col == part)
        def _():
            fill_head(head_sent)

        @pl.when(col != part)
        def _():
            fill_head(head_got)

    with jax.named_scope('sattn'):
        usable = lax.broadcasted_iota(jnp.int32, (1, tokens), 1) < length_ref[0]
        head_of_lane = lax.broadcasted_iota(jnp.int32, (1, width), 1) // SINGLE_HEAD_DIM
        blended = jnp.zeros((rows_here, width), f32)
        for head in range(s_heads):
            here = head_of_lane == head
            q_head = jnp.where(here, s_query[...], jnp.zeros_like(s_query[...]))
            scores = lax.dot_general(q_head, s_key[...], NT, preferred_element_type=f32)
            scores = jnp.where(usable, scores + head_full[head], masked_value)
            exponent = jnp.exp2(scores - jnp.max(scores, axis=-1, keepdims=True))
            total = jnp.sum(exponent, axis=-1, keepdims=True)
            weights = (exponent / total).astype(jnp.bfloat16)
            blended = jnp.where(
                here, jnp.dot(weights, s_value[...], preferred_element_type=f32), blended
            )
        s_hidden = (s_gate[...] * blended).astype(jnp.bfloat16)
        share = jnp.dot(s_hidden, single_out_ref[...], preferred_element_type=f32)
        for part in range(cols):
            part_sent[part % near, (half + part // near) % 2] = share[
                :, part * width : (part + 1) * width
            ].astype(jnp.bfloat16)
        for step in own_steps:
            part_copy(step).start()

    @pl.loop(late, last)
    def _(s):
        send_row(s)

    with jax.named_scope('part'):
        nearby = pl.ds(0, near - 1)
        settle(slot(part_got, nearby), part_recv)
        merged = part_sent[lane, 1].astype(f32)
        total = rest_ref[...].astype(f32) + part_sent[lane, 0].astype(f32)
        for step in own_steps:
            merged = merged + part_got[step, 1].astype(f32)
            total = total + part_got[step, 0].astype(f32)
        merged_sent[...] = merged.astype(jnp.bfloat16)
        merged_copy().start()

    @pl.loop(last, slab_rows)
    def _(s):
        send_row(s)

    with jax.named_scope('merge'):
        merged_copy().wait()
        single_new_ref[...] = (total + merged_got[...].astype(f32)).astype(jnp.bfloat16)

    with jax.named_scope('drain'):
        settle(slot(head_sent, others), head_send)
        settle(slot(part_sent, nearby), part_send)
        settle(slot(bands, row, others), col_send)
        settle(slot(bands, pl.ds(0, chips - 1)), chip_send)
        settle(slot(bands, pl.ds(0, chips)), core_send)
        sent = slot(local, pl.ds(0, slab_rows * (cols - 1)))
        settle(sent, in_send)
        settle(sent, out_send)
        settle(pair_out_ref, out_recv)


def store_kernel(pair_ref, single_ref, pair_out_ref, single_out_ref, pair_sem, single_sem):
    rows = pair_ref.shape[0]
    chunks = math.gcd(rows, 8)
    single = pltpu.make_async_copy(single_ref, single_out_ref, single_sem)
    single.start()
    for i in range(chunks):
        span = pl.ds(i * (rows // chunks), rows // chunks)
        pltpu.make_async_copy(pair_ref.at[span], pair_out_ref.at[span], pair_sem).start()
    single.wait()
    pltpu.make_async_copy(pair_ref, pair_out_ref, pair_sem).wait()


def store(pair, single):
    held = pl.BlockSpec(memory_space=pltpu.VMEM)
    away = pl.BlockSpec(memory_space=pltpu.HBM)
    return pl.pallas_call(
        store_kernel,
        in_specs=[held, held],
        out_specs=[away, away],
        out_shape=[jax.ShapeDtypeStruct(x.shape, x.dtype) for x in (pair, single)],
        scratch_shapes=[pltpu.SemaphoreType.DMA, pltpu.SemaphoreType.DMA],
        compiler_params=pltpu.CompilerParams(vmem_limit_bytes=4 * 2**20),
        name="store",
    )(*(pltpu.with_memory_space_constraint(x, pltpu.VMEM) for x in (pair, single)))


def per_device(
    pair_rep,
    single_rep,
    length,
    pair_gain,
    pair_proj,
    bias_weight,
    pair_out_weight,
    single_gain,
    single_proj,
    bias_norm_gain,
    single_bias_weight,
    single_out_weight,
):
    rows_here, cols_here, channels = pair_rep.shape
    rows, cols = lax.axis_size("row"), lax.axis_size("col")
    tokens = rows_here * rows
    slab_rows = rows_here // cols
    chips = rows // 2
    heads = bias_weight.shape[1]
    heads_in = math.gcd(heads, LANES // math.gcd(LANES, cols_here))
    single_heads = single_bias_weight.shape[1]
    heads_here = single_heads // cols
    width = single_proj.shape[2]
    single_proj_t = single_proj.transpose(0, 2, 1)
    bf16, f32 = jnp.bfloat16, jnp.float32
    dma = pltpu.SemaphoreType.DMA
    anywhere = pl.BlockSpec(memory_space=pl.ANY)
    stay = pl.BlockSpec(memory_space=pltpu.HBM)
    held = pl.BlockSpec(memory_space=pltpu.VMEM)
    pair_out, single_out = pl.pallas_call(
        window_kernel,
        in_specs=[stay] * 12,
        out_specs=[anywhere, held],
        out_shape=[
            pltpu.VMEM(pair_rep.shape, bf16),
            pltpu.VMEM((rows_here, width), bf16),
        ],
        scratch_shapes=[
            pltpu.VMEM(pair_rep.shape, bf16),
            pltpu.VMEM((heads, rows_here, cols_here), f32),
            pltpu.VMEM((heads // heads_in, rows_here, heads_in * cols_here), bf16),
            pltpu.VMEM(single_rep.shape, bf16),
            pltpu.VMEM(pair_proj.shape, bf16),
            pltpu.VMEM(pair_out_weight.shape, bf16),
            pltpu.VMEM(single_proj_t.shape, bf16),
            pltpu.VMEM(single_out_weight.shape, bf16),
            pltpu.VMEM(pair_gain.shape, f32),
            pltpu.VMEM((heads, channels), bf16),
            pltpu.VMEM(bias_norm_gain.shape, f32),
            pltpu.VMEM((single_heads, channels), bf16),
            pltpu.VMEM(single_gain.shape, f32),
            pltpu.SMEM(length.shape, jnp.int32),
            pltpu.VMEM((rows_here, width), bf16),
            dma((cols,)),
            dma((11,)),
            pltpu.VMEM((slab_rows, cols, cols_here, channels), bf16),
            pltpu.VMEM((slab_rows, cols, cols_here, channels), bf16),
            pltpu.VMEM((rows, cols, heads // heads_in, rows_here, heads_in * cols_here), bf16),
            pltpu.VMEM((heads, tokens, tokens), f32),
            pltpu.VMEM((cols, heads_here * slab_rows, tokens), f32),
            pltpu.VMEM((cols, heads_here * slab_rows, tokens), bf16),
            pltpu.VMEM((cols, heads_here * slab_rows, tokens), bf16),
            pltpu.VMEM((heads_here, rows_here, tokens), f32),
            pltpu.VMEM((rows_here, width), bf16),
            pltpu.VMEM((tokens, width), bf16),
            pltpu.VMEM((tokens, width), bf16),
            pltpu.VMEM((rows_here, width), f32),
            pltpu.VMEM((cols // 2, 2, rows_here, width), bf16),
            pltpu.VMEM((cols // 2, 2, rows_here, width), bf16),
            pltpu.VMEM((rows_here, width), bf16),
            pltpu.VMEM((rows_here, width), bf16),
            dma,
            dma((slab_rows,)),
            dma,
            dma,
            dma,
            dma((2,)),
            dma,
            dma((chips - 1,)),
            dma,
            dma((chips,)),
            dma,
            dma,
            dma,
            dma,
            dma,
            dma,
        ],
        compiler_params=pltpu.CompilerParams(
            collective_id=0, has_side_effects=True, vmem_limit_bytes=56 * 2**20
        ),
        name="window",
    )(
        length, pair_rep, single_rep, pair_proj, pair_out_weight, single_proj_t, single_out_weight,
        pair_gain, bias_weight.T, bias_norm_gain, single_bias_weight.T, single_gain,
    )
    return store(pair_out, single_out)


def solution(mesh):
    in_specs = (
        P("row", "col", None),
        P(),
        P(),
        P(),
        P(),
        P(),
        P(),
        P(),
        P(None, None, "col"),
        P(),
        P(),
        P("col", None),
    )
    out_specs = (P("row", "col", None), P("row", "col"))
    return jax.shard_map(
        per_device, mesh=mesh, in_specs=in_specs, out_specs=out_specs, check_vma=False
    )
```

```python
import math

import jax
import jax.numpy as jnp
from jax import lax
from jax.experimental import pallas as pl
from jax.experimental.pallas import tpu as pltpu
from jax.sharding import PartitionSpec as P

PAIR_HEADS = 8
PAIR_HEAD_DIM = 32
SINGLE_HEAD_DIM = 48
LOG2E = math.log2(math.e)

LANES = 128
masked_value = -1e30
NT = (((1,), (1,)), ((), ()))


def normalize(values, scales):
    floated = values.astype(jnp.float32)
    center = jnp.mean(floated, axis=-1, keepdims=True)
    spread = jnp.mean(jnp.square(floated - center), axis=-1, keepdims=True)
    return ((floated - center) * lax.rsqrt(spread + 1e-05) * scales).astype(jnp.bfloat16)


def project(inputs, matrix):
    return jnp.dot(inputs, matrix, preferred_element_type=jnp.float32).astype(jnp.bfloat16)


def project_t(inputs, matrix):
    return lax.dot_general(inputs, matrix, NT, preferred_element_type=jnp.float32).astype(
        jnp.bfloat16
    )


def row_update(rep, gain, proj_ref, out_weight, bias_of):
    channels = rep.shape[1]
    half = channels // 2
    heads_per_half = PAIR_HEADS // 2
    normed = normalize(rep, gain)
    f32 = jnp.float32
    query = jnp.dot(normed, proj_ref[0], preferred_element_type=f32)
    query = (query * (LOG2E / math.sqrt(PAIR_HEAD_DIM))).astype(jnp.bfloat16)
    key = project(normed, proj_ref[1])
    value = project(normed, proj_ref[2])
    gate = jax.nn.sigmoid(jnp.dot(normed, proj_ref[3], preferred_element_type=f32))
    head_of_lane = lax.broadcasted_iota(jnp.int32, (1, half), 1) // PAIR_HEAD_DIM
    halves = []
    for side in range(2):
        span = slice(side * half, (side + 1) * half)
        q_half, k_half, v_half = query[:, span], key[:, span], value[:, span]
        top = bottom = None
        for sub in range(heads_per_half):
            head = side * heads_per_half + sub
            mine = head_of_lane == sub
            q_head = jnp.where(mine, q_half, jnp.zeros_like(q_half))
            scores = lax.dot_general(q_head, k_half, NT, preferred_element_type=f32)
            scores = scores + bias_of(head)
            peak = jnp.max(scores, axis=-1, keepdims=True)
            exponent = jnp.exp2(scores - peak).astype(jnp.bfloat16)
            v_ext = jnp.concatenate([v_half, jnp.ones_like(v_half)], axis=1)
            both = jnp.dot(exponent, v_ext, preferred_element_type=f32)
            num, den = both[:, :half], both[:, half:]
            top = num if top is None else jnp.where(mine, num, top)
            bottom = den if bottom is None else jnp.where(mine, den, bottom)
        halves.append(top / bottom)
    attended = jnp.concatenate(halves, axis=1)
    hidden = (gate * attended).astype(jnp.bfloat16)
    return (
        rep.astype(f32) + jnp.dot(hidden, out_weight, preferred_element_type=f32)
    ).astype(jnp.bfloat16)


def folded(rows, width):
    full, odd = width // LANES * LANES, width % LANES
    if full and odd and 2 * odd == LANES:
        return (rows * (full // LANES) + rows // 2, LANES)
    return (rows, width)


def fold(value, ref):
    rows, width = value.shape
    if ref.shape == value.shape:
        ref[...] = value.astype(ref.dtype)
        return
    full = width // LANES
    for i in range(full):
        ref[i * rows : (i + 1) * rows] = value[:, i * LANES : (i + 1) * LANES].astype(ref.dtype)
    odd = value[:, full * LANES :]
    ref[full * rows :] = jnp.concatenate(
        [odd[: rows // 2], odd[rows // 2 :]], axis=1
    ).astype(ref.dtype)


def unfold(ref, shape):
    value = ref[...].astype(jnp.float32)
    if ref.shape == shape:
        return value
    rows, width = shape
    full = width // LANES
    odd = value[full * rows :]
    cut = width - full * LANES
    pieces = [value[i * rows : (i + 1) * rows] for i in range(full)]
    return jnp.concatenate(
        pieces + [jnp.concatenate([odd[:, :cut], odd[:, cut:]], axis=0)], axis=1
    )


def slot(ref, *index):
    return ref.at[index]


def window_kernel(
    length_hbm, pair_ref, single_hbm, proj_hbm, out_weight_hbm, single_proj_hbm, single_out_hbm,
    gain_hbm, tri_weight_hbm, bias_gain_hbm, head_weight_hbm, single_gain_hbm,
    pair_out_ref, single_new_ref,
    local, tri_kept, tri_ref, single_ref, proj_ref, out_weight_ref, single_proj_ref, single_out_ref,
    gain_ref, tri_weight_ref, bias_gain_ref, head_weight_ref, single_gain_ref, length_ref,
    rest_ref, local_sem, weight_sem,
    slab, fresh, bands, bias_held, head_kept, head_sent, head_got, head_full,
    cross_kept, cross_sent, cross_got, early_kept, early_sent, early_got,
    s_query, s_key, s_value, s_gate, part_sent, part_got, merged_sent, merged_got,
    in_send, in_recv, out_send, out_recv,
    col_send, col_recv, chip_send, chip_recv, core_send, core_recv,
    head_send, head_recv, cross_send, cross_recv, early_send, early_recv,
    part_send, part_recv, merged_send, merged_recv,
):
    f32 = jnp.float32
    slab_rows, cols, cols_here, channels = slab.shape
    rows, _, bundles, rows_here, _ = bands.shape
    heads_in = tri_kept.shape[0] // bundles
    tokens = cols * cols_here
    chips = rows // 2
    s_heads = head_full.shape[0]
    row, col = lax.axis_index("row"), lax.axis_index("col")
    chip, core = row // 2, lax.rem(row, 2)
    partner = chip * 2 + 1 - core
    mesh_id = pl.DeviceIdType.MESH

    def peer(step):
        return lax.rem(col + step, cols)

    def chip_row(step):
        return lax.rem(chip + step, chips) * 2 + core

    def chip_back(step):
        return lax.rem(chip + chips - step, chips) * 2 + core

    def local_copy(part):
        span = pl.ds(part * slab_rows, slab_rows)
        return pltpu.make_async_copy(pair_ref.at[span], local.at[span], local_sem.at[part])

    weight_copies = [
        pltpu.make_async_copy(src, dst, weight_sem.at[i])
        for i, (src, dst) in enumerate(
            (
                (gain_hbm, gain_ref),
                (tri_weight_hbm, tri_weight_ref),
                (length_hbm, length_ref),
                (bias_gain_hbm, bias_gain_ref),
                (head_weight_hbm, head_weight_ref),
                (single_gain_hbm, single_gain_ref),
                (single_hbm, single_ref),
                (single_proj_hbm, single_proj_ref),
                (proj_hbm, proj_ref),
                (out_weight_hbm, out_weight_ref),
                (single_out_hbm, single_out_ref),
            )
        )
    ]
    barrier = pltpu.get_barrier_semaphore()
    for step in range(1, cols):
        pl.semaphore_signal(barrier, inc=1, device_id=(row, peer(step)), device_id_type=mesh_id)
    for step in range(1, chips):
        pl.semaphore_signal(barrier, inc=1, device_id=(chip_row(step), col), device_id_type=mesh_id)
    pl.semaphore_signal(barrier, inc=1, device_id=(partner, col), device_id_type=mesh_id)
    for copy in weight_copies[:2]:
        copy.start()
    for part in range(cols):
        local_copy(part).start()
    for copy in weight_copies[2:]:
        copy.start()
    with jax.named_scope('bar'):
        pl.semaphore_wait(barrier, cols + chips - 1)

    def remote(src, dst, send, recv, to):
        return pltpu.make_async_remote_copy(
            src_ref=src, dst_ref=dst, send_sem=send, recv_sem=recv,
            device_id=to, device_id_type=mesh_id,
        )

    near = cols // 2
    mirror = peer(near)

    def near_peer(step):
        return col // near * near + lax.rem(lax.rem(col, near) + step, near)

    own_steps = range(1, near)
    mirror_steps = range(near + 1, 2 * near)

    def col_copy(step):
        to = mirror if step == 0 else near_peer(step % near)
        src, place = (tri_ref, col) if step < near else (slot(bands, row, mirror), mirror)
        return remote(
            src, slot(bands, row, place), col_send, col_recv.at[min(step, 1)], (row, to)
        )

    def chip_copy(step):
        return remote(
            slot(bands, row), slot(bands, row), chip_send, chip_recv.at[step - 1],
            (chip_row(step), col),
        )

    def core_copy(step):
        band = chip_back(step)
        return remote(
            slot(bands, band), slot(bands, band), core_send, core_recv.at[step],
            (partner, col),
        )

    def in_copy(s, step):
        to = peer(step)
        return remote(
            slot(pair_ref, to * slab_rows + s), slot(slab, s, col),
            in_send, in_recv.at[s], (row, to),
        )

    def own_in(s):
        return pltpu.make_async_copy(
            slot(pair_ref, col * slab_rows + s), slot(slab, s, col), in_recv.at[s]
        )

    lane, half = lax.rem(col, near), col // near
    early = 2 * slab_rows // 3

    def out_copy(s, step):
        to = peer(step)
        kind = jnp.where(jnp.logical_and(to // near != half, s < early), 1 + s, 0)
        return remote(
            slot(fresh, s, to), slot(pair_out_ref, col * slab_rows + s),
            out_send, out_recv.at[kind], (row, to),
        )

    def own_out(s):
        return pltpu.make_async_copy(
            slot(fresh, s, col), slot(pair_out_ref, col * slab_rows + s), out_recv.at[0]
        )

    def head_copy(step):
        to = near_peer(step)
        return remote(slot(head_sent, to), slot(head_got, lane), head_send, head_recv, (row, to))

    def cross_copy(step):
        place = lax.rem(lane + step, near)
        to = (1 - half) * near + place
        return remote(
            slot(cross_sent, place), slot(cross_got, lane), cross_send, cross_recv, (row, to)
        )

    def early_copy(step):
        to = near_peer(step)
        return remote(
            slot(early_sent, lax.rem(to, near)), slot(early_got, lane),
            early_send, early_recv, (row, to),
        )

    def part_copy(step):
        return remote(
            slot(part_sent, lax.rem(lane + step, near)), slot(part_got, step),
            part_send, part_recv, (row, near_peer(step)),
        )

    def merged_copy():
        return remote(merged_sent, merged_got, merged_send, merged_recv, (row, mirror))

    def settle(ref, sem):
        pltpu.make_async_copy(ref, ref, sem).wait()

    others = pl.ds(0, cols - 1)

    def bring_row(s):
        own_in(s).start()
        for step in range(1, cols):
            in_copy(s, step).start()

    bring_row(0)
    for copy in weight_copies[:2]:
        copy.wait()
    with jax.named_scope('tri'):
        group = math.gcd(slab_rows, 6)
        for part in range(cols):
            local_copy(part).wait()

            @pl.loop(0, slab_rows // group)
            def _(i):
                for j in range(group):
                    r = part * slab_rows + i * group + j
                    tri_kept[:, r, :] = lax.dot_general(
                        tri_weight_ref[...], normalize(local[r], gain_ref[...]), NT,
                        preferred_element_type=f32,
                    )

    for bundle in range(bundles):
        tri_ref[bundle] = jnp.concatenate(
            [tri_kept[bundle * heads_in + i] for i in range(heads_in)], axis=1
        ).astype(jnp.bfloat16)
    for step in (0, *own_steps):
        col_copy(step).start()
    own_block = pltpu.make_async_copy(tri_ref, slot(bands, row, col), col_recv.at[1])
    own_block.start()

    ahead = min(3, slab_rows)
    for s in range(1, ahead):
        bring_row(s)
    with jax.named_scope('waitmirror'):
        col_copy(0).wait_recv()
    for step in mirror_steps:
        col_copy(step).start()

    @pl.loop(ahead, slab_rows)
    def _(s):
        bring_row(s)

    for copy in weight_copies[2:]:
        copy.wait()

    with jax.named_scope('waitcols'):
        settle(slot(bands, row, others), col_recv.at[1])
    for step in range(1, chips):
        chip_copy(step).start()
    core_copy(0).start()

    with jax.named_scope('sproj'):
        s_normed = normalize(single_ref[...], single_gain_ref[...])
        s_key[...] = project_t(s_normed, single_proj_ref[1])
        s_value[...] = project_t(s_normed, single_proj_ref[2])
        width = s_key.shape[1]
        my_rows = pl.ds(pl.multiple_of(row * rows_here, rows_here), rows_here)
        for part in range(cols):

            @pl.when(col == part)
            def _():
                rest_ref[...] = single_ref[my_rows, part * width : (part + 1) * width]

        mine = normalize(
            single_ref[my_rows, :],
            single_gain_ref[...],
        )
        s_query[...] = (
            lax.dot_general(mine, single_proj_ref[0], NT, preferred_element_type=f32)
            * (LOG2E / math.sqrt(SINGLE_HEAD_DIM))
        ).astype(jnp.bfloat16)
        s_gate[...] = jax.nn.sigmoid(
            lax.dot_general(mine, single_proj_ref[3], NT, preferred_element_type=f32)
        )

    def take_band(band):
        start = pl.multiple_of(band * rows_here, rows_here)
        for part in range(cols):
            usable = (
                lax.broadcasted_iota(jnp.int32, (1, cols_here), 1) + part * cols_here
                < length_ref[0]
            )
            place = (pl.ds(start, rows_here), slice(part * cols_here, (part + 1) * cols_here))
            for bundle in range(bundles):
                piece = bands[band, part, bundle].astype(f32) * LOG2E
                for i in range(heads_in):
                    bias_held[bundle * heads_in + i, *place] = jnp.where(
                        usable, piece[:, i * cols_here : (i + 1) * cols_here], masked_value
                    )

    with jax.named_scope('bands'):
        take_band(row)
        for step in range(1, chips):
            chip_copy(step).wait_recv()
            core_copy(step).start()
            take_band(chip_back(step))
        for step in range(chips):
            core_copy(step).wait_recv()
            take_band(chip_back(step) + 1 - 2 * core)

    middle = early + slab_rows // 12
    late = slab_rows - slab_rows // 6
    last = slab_rows - slab_rows // 12

    def one_row(s):
        settle(slot(slab, s), in_recv.at[s])
        rep = slab[s].reshape(tokens, channels)
        updated = row_update(
            rep, gain_ref[...], proj_ref, out_weight_ref[...], lambda head: bias_held[head]
        )
        fresh[s] = updated.reshape(cols, cols_here, channels)
        again = normalize(updated, bias_gain_ref[...])
        found = lax.dot_general(head_weight_ref[...], again, NT, preferred_element_type=f32)
        for head in range(found.shape[0]):
            line = pl.ds(head % s_heads * slab_rows + s, 1)
            head_kept[head // s_heads, line, :] = found[head : head + 1]

    def send_row(s):
        own_out(s).start()
        for step in range(1, cols):
            out_copy(s, step).start()

    with jax.named_scope('rows'):
        @pl.loop(0, slab_rows)
        def _(s):
            one_row(s)

            @pl.when(s < early)
            def _():
                send_row(s)

    head_sent[...] = head_kept[...].astype(jnp.bfloat16)
    wide = near * cols_here
    rest = slab_rows - early
    top_heads = s_heads // 2
    for part in range(cols):
        mine = slice((1 - part // near) * wide, (2 - part // near) * wide)

        @pl.when(half != part // near)
        def _():
            for head in range(s_heads):
                begin = head * slab_rows
                up = head % top_heads * early
                side = head // top_heads * wide
                cross_kept[up : up + early, side : side + wide] = head_kept[
                    part, begin : begin + early, mine
                ]
                down = top_heads * early + head * rest
                cross_kept[down : down + rest, :] = head_kept[
                    part, begin + early : begin + slab_rows, :
                ]
            cross_sent[part % near] = cross_kept[...].astype(jnp.bfloat16)

    for step in range(near):
        cross_copy(step).start()
    for step in own_steps:
        head_copy(step).start()
    head_got[lane] = head_sent[col]

    @pl.loop(early, middle)
    def _(s):
        send_row(s)

    with jax.named_scope('recompute'):

        @pl.loop(0, early)
        def _(s):
            settle(slot(pair_out_ref, pl.ds(0, near)), out_recv.at[1 + s])
            for other in range(near):
                line = ((1 - half) * near + other) * slab_rows + s
                again = normalize(pair_out_ref[line], bias_gain_ref[...])
                found = lax.dot_general(head_weight_ref[...], again, NT, preferred_element_type=f32)
                for head in range(found.shape[0]):
                    at = (head % s_heads * near + other) * early + s
                    early_kept[head // s_heads, pl.ds(at, 1), :] = found[head : head + 1]

        for place in range(near):
            early_sent[place] = early_kept[half * near + place].astype(jnp.bfloat16)
        for step in own_steps:
            early_copy(step).start()
        early_got[lane] = early_sent[lane]

    @pl.loop(middle, late)
    def _(s):
        send_row(s)

    nearby = pl.ds(0, near - 1)
    with jax.named_scope('headwait'):
        settle(slot(head_got, nearby), head_recv)
        settle(cross_got, cross_recv)
        settle(slot(early_got, nearby), early_recv)
    for part in range(cols):
        first = part * slab_rows
        place, side = part % near, part // near

        @pl.when(half == side)
        def _():
            block = head_got[place].astype(f32) * LOG2E
            for head in range(s_heads):
                head_full[head, first : first + slab_rows, :] = block[
                    head * slab_rows : (head + 1) * slab_rows
                ]

        @pl.when(half != side)
        def _():
            block = cross_got[place].astype(f32) * LOG2E
            for head in range(s_heads):
                up = head % top_heads * early
                from_side = head // top_heads * wide
                head_full[head, first : first + early, side * wide : (side + 1) * wide] = block[
                    up : up + early, from_side : from_side + wide
                ]
                down = top_heads * early + head * rest
                head_full[head, first + early : first + slab_rows, :] = block[down : down + rest]
                at = (head * near + place) * early
                for source in range(near):
                    begin = ((1 - side) * near + source) * cols_here
                    head_full[head, first : first + early, begin : begin + cols_here] = (
                        early_got[source, at : at + early, :].astype(f32) * LOG2E
                    )

    with jax.named_scope('sattn'):
        usable = lax.broadcasted_iota(jnp.int32, (1, tokens), 1) < length_ref[0]
        head_of_lane = lax.broadcasted_iota(jnp.int32, (1, width), 1) // SINGLE_HEAD_DIM
        blended = jnp.zeros((rows_here, width), f32)
        for head in range(s_heads):
            here = head_of_lane == head
            q_head = jnp.where(here, s_query[...], jnp.zeros_like(s_query[...]))
            scores = lax.dot_general(q_head, s_key[...], NT, preferred_element_type=f32)
            scores = jnp.where(usable, scores + head_full[head], masked_value)
            exponent = jnp.exp2(scores - jnp.max(scores, axis=-1, keepdims=True))
            total = jnp.sum(exponent, axis=-1, keepdims=True)
            weights = (exponent / total).astype(jnp.bfloat16)
            blended = jnp.where(
                here, jnp.dot(weights, s_value[...], preferred_element_type=f32), blended
            )
        s_hidden = (s_gate[...] * blended).astype(jnp.bfloat16)
        share = jnp.dot(s_hidden, single_out_ref[...], preferred_element_type=f32)
        for part in range(cols):
            part_sent[part % near, (half + part // near) % 2] = share[
                :, part * width : (part + 1) * width
            ].astype(jnp.bfloat16)
        for step in own_steps:
            part_copy(step).start()

    @pl.loop(late, last)
    def _(s):
        send_row(s)

    with jax.named_scope('part'):
        settle(slot(part_got, nearby), part_recv)
        merged = part_sent[lane, 1].astype(f32)
        total = rest_ref[...].astype(f32) + part_sent[lane, 0].astype(f32)
        for step in own_steps:
            merged = merged + part_got[step, 1].astype(f32)
            total = total + part_got[step, 0].astype(f32)
        fold(merged, merged_sent)
        merged_copy().start()

    @pl.loop(last, slab_rows)
    def _(s):
        send_row(s)

    with jax.named_scope('merge'):
        merged_copy().wait()
        single_new_ref[...] = (total + unfold(merged_got, total.shape)).astype(jnp.bfloat16)

    with jax.named_scope('drain'):
        settle(slot(head_sent, nearby), head_send)
        settle(cross_sent, cross_send)
        settle(slot(early_sent, nearby), early_send)
        settle(slot(part_sent, nearby), part_send)
        settle(slot(bands, row, others), col_send)
        settle(slot(bands, pl.ds(0, chips - 1)), chip_send)
        settle(slot(bands, pl.ds(0, chips)), core_send)
        sent = slot(local, pl.ds(0, slab_rows * (cols - 1)))
        settle(sent, in_send)
        settle(sent, out_send)
        settle(slot(pair_out_ref, pl.ds(0, rows_here - near * early)), out_recv.at[0])


def store_kernel(pair_ref, single_ref, pair_out_ref, single_out_ref, pair_sem, single_sem):
    rows = pair_ref.shape[0]
    chunks = math.gcd(rows, 8)
    single = pltpu.make_async_copy(single_ref, single_out_ref, single_sem)
    single.start()
    for i in range(chunks):
        span = pl.ds(i * (rows // chunks), rows // chunks)
        pltpu.make_async_copy(pair_ref.at[span], pair_out_ref.at[span], pair_sem).start()
    single.wait()
    pltpu.make_async_copy(pair_ref, pair_out_ref, pair_sem).wait()


def store(pair, single):
    held = pl.BlockSpec(memory_space=pltpu.VMEM)
    away = pl.BlockSpec(memory_space=pltpu.HBM)
    return pl.pallas_call(
        store_kernel,
        in_specs=[held, held],
        out_specs=[away, away],
        out_shape=[jax.ShapeDtypeStruct(x.shape, x.dtype) for x in (pair, single)],
        scratch_shapes=[pltpu.SemaphoreType.DMA, pltpu.SemaphoreType.DMA],
        compiler_params=pltpu.CompilerParams(vmem_limit_bytes=4 * 2**20),
        name="store",
    )(*(pltpu.with_memory_space_constraint(x, pltpu.VMEM) for x in (pair, single)))


def per_device(
    pair_rep,
    single_rep,
    length,
    pair_gain,
    pair_proj,
    bias_weight,
    pair_out_weight,
    single_gain,
    single_proj,
    bias_norm_gain,
    single_bias_weight,
    single_out_weight,
):
    rows_here, cols_here, channels = pair_rep.shape
    rows, cols = lax.axis_size("row"), lax.axis_size("col")
    tokens = rows_here * rows
    slab_rows = rows_here // cols
    chips = rows // 2
    heads = bias_weight.shape[1]
    heads_in = math.gcd(heads, LANES // math.gcd(LANES, cols_here))
    single_heads = single_bias_weight.shape[1]
    heads_here = single_heads // cols
    width = single_proj.shape[2]
    near = cols // 2
    early = 2 * slab_rows // 3
    cross_rows = heads_here // 2 * early + heads_here * (slab_rows - early)
    single_proj_t = single_proj.transpose(0, 2, 1)
    bf16, f32 = jnp.bfloat16, jnp.float32
    dma = pltpu.SemaphoreType.DMA
    anywhere = pl.BlockSpec(memory_space=pl.ANY)
    stay = pl.BlockSpec(memory_space=pltpu.HBM)
    held = pl.BlockSpec(memory_space=pltpu.VMEM)
    pair_out, single_out = pl.pallas_call(
        window_kernel,
        in_specs=[stay] * 12,
        out_specs=[held, held],
        out_shape=[
            pltpu.VMEM(pair_rep.shape, bf16),
            pltpu.VMEM((rows_here, width), bf16),
        ],
        scratch_shapes=[
            pltpu.VMEM(pair_rep.shape, bf16),
            pltpu.VMEM((heads, rows_here, cols_here), f32),
            pltpu.VMEM((heads // heads_in, rows_here, heads_in * cols_here), bf16),
            pltpu.VMEM(single_rep.shape, bf16),
            pltpu.VMEM(pair_proj.shape, bf16),
            pltpu.VMEM(pair_out_weight.shape, bf16),
            pltpu.VMEM(single_proj_t.shape, bf16),
            pltpu.VMEM(single_out_weight.shape, bf16),
            pltpu.VMEM(pair_gain.shape, f32),
            pltpu.VMEM((heads, channels), bf16),
            pltpu.VMEM(bias_norm_gain.shape, f32),
            pltpu.VMEM((single_heads, channels), bf16),
            pltpu.VMEM(single_gain.shape, f32),
            pltpu.SMEM(length.shape, jnp.int32),
            pltpu.VMEM((rows_here, width), bf16),
            dma((cols,)),
            dma((11,)),
            pltpu.VMEM((slab_rows, cols, cols_here, channels), bf16),
            pltpu.VMEM((slab_rows, cols, cols_here, channels), bf16),
            pltpu.VMEM((rows, cols, heads // heads_in, rows_here, heads_in * cols_here), bf16),
            pltpu.VMEM((heads, tokens, tokens), f32),
            pltpu.VMEM((cols, heads_here * slab_rows, tokens), f32),
            pltpu.VMEM((cols, heads_here * slab_rows, tokens), bf16),
            pltpu.VMEM((near, heads_here * slab_rows, tokens), bf16),
            pltpu.VMEM((heads_here, rows_here, tokens), f32),
            pltpu.VMEM((cross_rows, tokens), f32),
            pltpu.VMEM((near, cross_rows, tokens), bf16),
            pltpu.VMEM((near, cross_rows, tokens), bf16),
            pltpu.VMEM((cols, heads_here * near * early, cols_here), f32),
            pltpu.VMEM((near, heads_here * near * early, cols_here), bf16),
            pltpu.VMEM((near, heads_here * near * early, cols_here), bf16),
            pltpu.VMEM((rows_here, width), bf16),
            pltpu.VMEM((tokens, width), bf16),
            pltpu.VMEM((tokens, width), bf16),
            pltpu.VMEM((rows_here, width), f32),
            pltpu.VMEM((cols // 2, 2, rows_here, width), bf16),
            pltpu.VMEM((cols // 2, 2, rows_here, width), bf16),
            pltpu.VMEM(folded(rows_here, width), bf16),
            pltpu.VMEM(folded(rows_here, width), bf16),
            dma,
            dma((slab_rows,)),
            dma,
            dma((1 + early,)),
            dma,
            dma((2,)),
            dma,
            dma((chips - 1,)),
            dma,
            dma((chips,)),
            dma,
            dma,
            dma,
            dma,
            dma,
            dma,
            dma,
            dma,
            dma,
            dma,
        ],
        compiler_params=pltpu.CompilerParams(
            collective_id=0, has_side_effects=True, vmem_limit_bytes=56 * 2**20
        ),
        name="window",
    )(
        length, pair_rep, single_rep, pair_proj, pair_out_weight, single_proj_t, single_out_weight,
        pair_gain, bias_weight.T, bias_norm_gain, single_bias_weight.T, single_gain,
    )
    return store(pair_out, single_out)


def solution(mesh):
    in_specs = (
        P("row", "col", None),
        P(),
        P(),
        P(),
        P(),
        P(),
        P(),
        P(),
        P(None, None, "col"),
        P(),
        P(),
        P("col", None),
    )
    out_specs = (P("row", "col", None), P("row", "col"))
    return jax.shard_map(
        per_device, mesh=mesh, in_specs=in_specs, out_specs=out_specs, check_vma=False
    )
```

```python
import math

import jax
import jax.numpy as jnp
from jax import lax
from jax.experimental import pallas as pl
from jax.experimental.pallas import tpu as pltpu
from jax.sharding import PartitionSpec as P

PAIR_HEADS = 8
PAIR_HEAD_DIM = 32
SINGLE_HEAD_DIM = 48
LOG2E = math.log2(math.e)

LANES = 128
masked_value = -1e30
NT = (((1,), (1,)), ((), ()))


def normalize(values, scales):
    floated = values.astype(jnp.float32)
    center = jnp.mean(floated, axis=-1, keepdims=True)
    spread = jnp.mean(jnp.square(floated - center), axis=-1, keepdims=True)
    return ((floated - center) * lax.rsqrt(spread + 1e-05) * scales).astype(jnp.bfloat16)


def project(inputs, matrix):
    return jnp.dot(inputs, matrix, preferred_element_type=jnp.float32).astype(jnp.bfloat16)


def project_t(inputs, matrix):
    return lax.dot_general(inputs, matrix, NT, preferred_element_type=jnp.float32).astype(
        jnp.bfloat16
    )


def row_update(rep, gain, proj_ref, out_weight, bias_of):
    channels = rep.shape[1]
    half = channels // 2
    heads_per_half = PAIR_HEADS // 2
    normed = normalize(rep, gain)
    f32 = jnp.float32
    query = jnp.dot(normed, proj_ref[0], preferred_element_type=f32)
    query = (query * (LOG2E / math.sqrt(PAIR_HEAD_DIM))).astype(jnp.bfloat16)
    key = project(normed, proj_ref[1])
    value = project(normed, proj_ref[2])
    gate = jax.nn.sigmoid(jnp.dot(normed, proj_ref[3], preferred_element_type=f32))
    head_of_lane = lax.broadcasted_iota(jnp.int32, (1, half), 1) // PAIR_HEAD_DIM
    halves = []
    for side in range(2):
        span = slice(side * half, (side + 1) * half)
        q_half, k_half, v_half = query[:, span], key[:, span], value[:, span]
        top = bottom = None
        for sub in range(heads_per_half):
            head = side * heads_per_half + sub
            mine = head_of_lane == sub
            q_head = jnp.where(mine, q_half, jnp.zeros_like(q_half))
            scores = lax.dot_general(q_head, k_half, NT, preferred_element_type=f32)
            scores = scores + bias_of(head)
            peak = jnp.max(scores, axis=-1, keepdims=True)
            exponent = jnp.exp2(scores - peak).astype(jnp.bfloat16)
            v_ext = jnp.concatenate([v_half, jnp.ones_like(v_half)], axis=1)
            both = jnp.dot(exponent, v_ext, preferred_element_type=f32)
            num, den = both[:, :half], both[:, half:]
            top = num if top is None else jnp.where(mine, num, top)
            bottom = den if bottom is None else jnp.where(mine, den, bottom)
        halves.append(top / bottom)
    attended = jnp.concatenate(halves, axis=1)
    hidden = (gate * attended).astype(jnp.bfloat16)
    return (
        rep.astype(f32) + jnp.dot(hidden, out_weight, preferred_element_type=f32)
    ).astype(jnp.bfloat16)


def folded(rows, width):
    full, odd = width // LANES * LANES, width % LANES
    if full and odd and 2 * odd == LANES:
        return (rows * (full // LANES) + rows // 2, LANES)
    return (rows, width)


def fold(value, ref):
    rows, width = value.shape
    if ref.shape == value.shape:
        ref[...] = value.astype(ref.dtype)
        return
    full = width // LANES
    for i in range(full):
        ref[i * rows : (i + 1) * rows] = value[:, i * LANES : (i + 1) * LANES].astype(ref.dtype)
    odd = value[:, full * LANES :]
    ref[full * rows :] = jnp.concatenate(
        [odd[: rows // 2], odd[rows // 2 :]], axis=1
    ).astype(ref.dtype)


def unfold(ref, shape):
    value = ref[...].astype(jnp.float32)
    if ref.shape == shape:
        return value
    rows, width = shape
    full = width // LANES
    odd = value[full * rows :]
    cut = width - full * LANES
    pieces = [value[i * rows : (i + 1) * rows] for i in range(full)]
    return jnp.concatenate(
        pieces + [jnp.concatenate([odd[:, :cut], odd[:, cut:]], axis=0)], axis=1
    )


def slot(ref, *index):
    return ref.at[index]


def window_kernel(
    length_hbm, pair_ref, single_hbm, proj_hbm, out_weight_hbm, single_proj_hbm, single_out_hbm,
    gain_hbm, tri_weight_hbm, bias_gain_hbm, head_weight_hbm, single_gain_hbm,
    pair_out_ref, single_new_ref,
    local, tri_kept, tri_ref, single_ref, proj_ref, out_weight_ref, single_proj_ref, single_out_ref,
    gain_ref, tri_weight_ref, bias_gain_ref, head_weight_ref, single_gain_ref, length_ref,
    rest_ref, local_sem, weight_sem,
    slab, fresh, bands, bias_held, head_kept, head_sent, head_got, head_full,
    cross_kept, cross_sent, cross_got, early_kept, early_sent, early_got,
    s_query, s_key, s_value, s_gate, part_sent, part_got, merged_sent, merged_got,
    in_send, in_recv, out_send, out_recv,
    col_send, col_recv, chip_send, chip_recv, core_send, core_recv,
    head_send, head_recv, cross_send, cross_recv, early_send, early_recv,
    part_send, part_recv, merged_send, merged_recv, opened, met, entered,
):
    f32 = jnp.float32
    slab_rows, cols, cols_here, channels = slab.shape
    rows, _, bundles, rows_here, _ = bands.shape
    heads_in = tri_kept.shape[0] // bundles
    tokens = cols * cols_here
    chips = rows // 2
    s_heads = head_full.shape[0]
    row, col = lax.axis_index("row"), lax.axis_index("col")
    chip, core = row // 2, lax.rem(row, 2)
    partner = chip * 2 + 1 - core
    mesh_id = pl.DeviceIdType.MESH

    def peer(step):
        return lax.rem(col + step, cols)

    def chip_row(step):
        return lax.rem(chip + step, chips) * 2 + core

    def chip_back(step):
        return lax.rem(chip + chips - step, chips) * 2 + core

    def local_copy(part):
        span = pl.ds(part * slab_rows, slab_rows)
        return pltpu.make_async_copy(pair_ref.at[span], local.at[span], local_sem.at[part])

    weight_copies = [
        pltpu.make_async_copy(src, dst, weight_sem.at[i])
        for i, (src, dst) in enumerate(
            (
                (gain_hbm, gain_ref),
                (tri_weight_hbm, tri_weight_ref),
                (length_hbm, length_ref),
                (bias_gain_hbm, bias_gain_ref),
                (head_weight_hbm, head_weight_ref),
                (single_gain_hbm, single_gain_ref),
                (single_hbm, single_ref),
                (single_proj_hbm, single_proj_ref),
                (proj_hbm, proj_ref),
                (out_weight_hbm, out_weight_ref),
                (single_out_hbm, single_out_ref),
            )
        )
    ]
    barrier = pltpu.get_barrier_semaphore()
    left, right = cols // 2 - 1, cols // 2
    inner = jnp.logical_or(col == left, col == right)
    outer = jnp.logical_not(inner)
    guide = jnp.logical_or(col == 0, col == cols - 1)
    follower = jnp.where(col == 0, left, right)
    pair = cols - 1 - col

    def signal(sem, to_row, to_col):
        pl.semaphore_signal(sem, inc=1, device_id=(to_row, to_col), device_id_type=mesh_id)

    def signal_rows(sem):
        for step in range(1, chips):
            signal(sem, chip_row(step), col)
        signal(sem, partner, col)

    for step in range(1, cols):
        to = peer(step)
        to_outer = jnp.logical_and(to != left, to != right)

        @pl.when(jnp.logical_or(to_outer, jnp.logical_and(inner, to == pair)))
        def _():
            signal(barrier, row, to)

    @pl.when(outer)
    def _():
        signal_rows(barrier)

    for copy in weight_copies[:2]:
        copy.start()
    for part in range(cols):
        local_copy(part).start()
    for copy in weight_copies[2:]:
        copy.start()
    with jax.named_scope('bar'):
        @pl.when(inner)
        def _():
            pl.semaphore_wait(barrier, 1)

        @pl.when(outer)
        def _():
            pl.semaphore_wait(barrier, cols + chips - 1)

    @pl.when(guide)
    def _():
        signal(opened, row, follower)
        signal_rows(met)

    def remote(src, dst, send, recv, to):
        return pltpu.make_async_remote_copy(
            src_ref=src, dst_ref=dst, send_sem=send, recv_sem=recv,
            device_id=to, device_id_type=mesh_id,
        )

    near = cols // 2
    mirror = peer(near)

    def near_peer(step):
        return col // near * near + lax.rem(lax.rem(col, near) + step, near)

    own_steps = range(1, near)
    mirror_steps = range(near + 1, 2 * near)

    def col_copy(step):
        to = mirror if step == 0 else near_peer(step % near)
        src, place = (tri_ref, col) if step < near else (slot(bands, row, mirror), mirror)
        return remote(
            src, slot(bands, row, place), col_send, col_recv.at[min(step, 1)], (row, to)
        )

    def chip_copy(step):
        return remote(
            slot(bands, row), slot(bands, row), chip_send, chip_recv.at[step - 1],
            (chip_row(step), col),
        )

    def core_copy(step):
        band = chip_back(step)
        return remote(
            slot(bands, band), slot(bands, band), core_send, core_recv.at[step],
            (partner, col),
        )

    def in_copy(s, to):
        return remote(
            slot(pair_ref, to * slab_rows + s), slot(slab, s, col),
            in_send, in_recv.at[s], (row, to),
        )

    def own_in(s):
        return pltpu.make_async_copy(
            slot(pair_ref, col * slab_rows + s), slot(slab, s, col), in_recv.at[s]
        )

    lane, half = lax.rem(col, near), col // near
    early = 2 * slab_rows // 3

    def out_copy(s, step):
        to = peer(step)
        kind = jnp.where(jnp.logical_and(to // near != half, s < early), 1 + s, 0)
        return remote(
            slot(fresh, s, to), slot(pair_out_ref, col * slab_rows + s),
            out_send, out_recv.at[kind], (row, to),
        )

    def own_out(s):
        return pltpu.make_async_copy(
            slot(fresh, s, col), slot(pair_out_ref, col * slab_rows + s), out_recv.at[0]
        )

    def head_copy(step):
        to = near_peer(step)
        return remote(slot(head_sent, to), slot(head_got, lane), head_send, head_recv, (row, to))

    def cross_copy(step):
        place = lax.rem(lane + step, near)
        to = (1 - half) * near + place
        return remote(
            slot(cross_sent, place), slot(cross_got, lane), cross_send, cross_recv, (row, to)
        )

    def early_copy(step):
        to = near_peer(step)
        return remote(
            slot(early_sent, lax.rem(to, near)), slot(early_got, lane),
            early_send, early_recv, (row, to),
        )

    def part_copy(step):
        return remote(
            slot(part_sent, lax.rem(lane + step, near)), slot(part_got, step),
            part_send, part_recv, (row, near_peer(step)),
        )

    def merged_copy():
        return remote(merged_sent, merged_got, merged_send, merged_recv, (row, mirror))

    def settle(ref, sem):
        pltpu.make_async_copy(ref, ref, sem).wait()

    others = pl.ds(0, cols - 1)

    def bring_row(s):
        own_in(s).start()
        for step in range(1, cols):
            in_copy(s, peer(step)).start()

    def bring_rest(s):
        own_in(s).start()
        for step in range(1, cols):

            @pl.when(peer(step) != pair)
            def _():
                in_copy(s, peer(step)).start()

    first_rows = min(2, slab_rows)

    @pl.when(inner)
    def _():
        for s in range(first_rows):
            in_copy(s, pair).start()

    @pl.when(outer)
    def _():
        bring_row(0)

    for copy in weight_copies[:2]:
        copy.wait()
    with jax.named_scope('tri'):
        group = math.gcd(slab_rows, 6)
        for part in range(cols):
            local_copy(part).wait()

            @pl.loop(0, slab_rows // group)
            def _(i):
                for j in range(group):
                    r = part * slab_rows + i * group + j
                    tri_kept[:, r, :] = lax.dot_general(
                        tri_weight_ref[...], normalize(local[r], gain_ref[...]), NT,
                        preferred_element_type=f32,
                    )

    for bundle in range(bundles):
        tri_ref[bundle] = jnp.concatenate(
            [tri_kept[bundle * heads_in + i] for i in range(heads_in)], axis=1
        ).astype(jnp.bfloat16)
    @pl.when(inner)
    def _():
        pl.semaphore_wait(opened, 1)

    for step in (0, *own_steps):
        col_copy(step).start()
    own_block = pltpu.make_async_copy(tri_ref, slot(bands, row, col), col_recv.at[1])
    own_block.start()

    ahead = min(3, slab_rows)

    @pl.when(inner)
    def _():
        for s in range(first_rows):
            bring_rest(s)

    @pl.when(outer)
    def _():
        for s in range(1, first_rows):
            bring_row(s)

    for s in range(first_rows, ahead):
        bring_row(s)

    @pl.when(guide)
    def _():
        pl.semaphore_wait(met, chips)
        signal(entered, row, follower)

    with jax.named_scope('waitmirror'):
        col_copy(0).wait_recv()
    for step in mirror_steps:
        col_copy(step).start()

    @pl.loop(ahead, slab_rows)
    def _(s):
        bring_row(s)

    for copy in weight_copies[2:]:
        copy.wait()

    with jax.named_scope('waitcols'):
        settle(slot(bands, row, others), col_recv.at[1])
    @pl.when(inner)
    def _():
        pl.semaphore_wait(entered, 1)

    for step in range(1, chips):
        chip_copy(step).start()
    core_copy(0).start()

    with jax.named_scope('sproj'):
        s_normed = normalize(single_ref[...], single_gain_ref[...])
        s_key[...] = project_t(s_normed, single_proj_ref[1])
        s_value[...] = project_t(s_normed, single_proj_ref[2])
        width = s_key.shape[1]
        my_rows = pl.ds(pl.multiple_of(row * rows_here, rows_here), rows_here)
        for part in range(cols):

            @pl.when(col == part)
            def _():
                rest_ref[...] = single_ref[my_rows, part * width : (part + 1) * width]

        mine = normalize(
            single_ref[my_rows, :],
            single_gain_ref[...],
        )
        s_query[...] = (
            lax.dot_general(mine, single_proj_ref[0], NT, preferred_element_type=f32)
            * (LOG2E / math.sqrt(SINGLE_HEAD_DIM))
        ).astype(jnp.bfloat16)
        s_gate[...] = jax.nn.sigmoid(
            lax.dot_general(mine, single_proj_ref[3], NT, preferred_element_type=f32)
        )

    def take_band(band):
        start = pl.multiple_of(band * rows_here, rows_here)
        for part in range(cols):
            usable = (
                lax.broadcasted_iota(jnp.int32, (1, cols_here), 1) + part * cols_here
                < length_ref[0]
            )
            place = (pl.ds(start, rows_here), slice(part * cols_here, (part + 1) * cols_here))
            for bundle in range(bundles):
                piece = bands[band, part, bundle].astype(f32) * LOG2E
                for i in range(heads_in):
                    bias_held[bundle * heads_in + i, *place] = jnp.where(
                        usable, piece[:, i * cols_here : (i + 1) * cols_here], masked_value
                    )

    with jax.named_scope('bands'):
        take_band(row)
        for step in range(1, chips):
            chip_copy(step).wait_recv()
            core_copy(step).start()
            take_band(chip_back(step))
        for step in range(chips):
            core_copy(step).wait_recv()
            take_band(chip_back(step) + 1 - 2 * core)

    middle = early + slab_rows // 12
    late = slab_rows - slab_rows // 6
    last = slab_rows - slab_rows // 12

    def one_row(s):
        settle(slot(slab, s), in_recv.at[s])
        rep = slab[s].reshape(tokens, channels)
        updated = row_update(
            rep, gain_ref[...], proj_ref, out_weight_ref[...], lambda head: bias_held[head]
        )
        fresh[s] = updated.reshape(cols, cols_here, channels)
        again = normalize(updated, bias_gain_ref[...])
        found = lax.dot_general(head_weight_ref[...], again, NT, preferred_element_type=f32)
        for head in range(found.shape[0]):
            line = pl.ds(head % s_heads * slab_rows + s, 1)
            head_kept[head // s_heads, line, :] = found[head : head + 1]

    def send_row(s):
        own_out(s).start()
        for step in range(1, cols):
            out_copy(s, step).start()

    with jax.named_scope('rows'):
        @pl.loop(0, slab_rows)
        def _(s):
            one_row(s)

            @pl.when(s < early)
            def _():
                send_row(s)

    head_sent[...] = head_kept[...].astype(jnp.bfloat16)
    wide = near * cols_here
    rest = slab_rows - early
    top_heads = s_heads // 2
    for part in range(cols):
        mine = slice((1 - part // near) * wide, (2 - part // near) * wide)

        @pl.when(half != part // near)
        def _():
            for head in range(s_heads):
                begin = head * slab_rows
                up = head % top_heads * early
                side = head // top_heads * wide
                cross_kept[up : up + early, side : side + wide] = head_kept[
                    part, begin : begin + early, mine
                ]
                down = top_heads * early + head * rest
                cross_kept[down : down + rest, :] = head_kept[
                    part, begin + early : begin + slab_rows, :
                ]
            cross_sent[part % near] = cross_kept[...].astype(jnp.bfloat16)

    for step in range(near):
        cross_copy(step).start()
    for step in own_steps:
        head_copy(step).start()
    head_got[lane] = head_sent[col]

    @pl.loop(early, middle)
    def _(s):
        send_row(s)

    with jax.named_scope('recompute'):

        @pl.loop(0, early)
        def _(s):
            settle(slot(pair_out_ref, pl.ds(0, near)), out_recv.at[1 + s])
            for other in range(near):
                line = ((1 - half) * near + other) * slab_rows + s
                again = normalize(pair_out_ref[line], bias_gain_ref[...])
                found = lax.dot_general(head_weight_ref[...], again, NT, preferred_element_type=f32)
                for head in range(found.shape[0]):
                    at = (head % s_heads * near + other) * early + s
                    early_kept[head // s_heads, pl.ds(at, 1), :] = found[head : head + 1]

        for place in range(near):
            early_sent[place] = early_kept[half * near + place].astype(jnp.bfloat16)
        for step in own_steps:
            early_copy(step).start()
        early_got[lane] = early_sent[lane]

    @pl.loop(middle, late)
    def _(s):
        send_row(s)

    nearby = pl.ds(0, near - 1)
    with jax.named_scope('headwait'):
        settle(slot(head_got, nearby), head_recv)
        settle(cross_got, cross_recv)
        settle(slot(early_got, nearby), early_recv)
    for part in range(cols):
        first = part * slab_rows
        place, side = part % near, part // near

        @pl.when(half == side)
        def _():
            block = head_got[place].astype(f32) * LOG2E
            for head in range(s_heads):
                head_full[head, first : first + slab_rows, :] = block[
                    head * slab_rows : (head + 1) * slab_rows
                ]

        @pl.when(half != side)
        def _():
            block = cross_got[place].astype(f32) * LOG2E
            for head in range(s_heads):
                up = head % top_heads * early
                from_side = head // top_heads * wide
                head_full[head, first : first + early, side * wide : (side + 1) * wide] = block[
                    up : up + early, from_side : from_side + wide
                ]
                down = top_heads * early + head * rest
                head_full[head, first + early : first + slab_rows, :] = block[down : down + rest]
                at = (head * near + place) * early
                for source in range(near):
                    begin = ((1 - side) * near + source) * cols_here
                    head_full[head, first : first + early, begin : begin + cols_here] = (
                        early_got[source, at : at + early, :].astype(f32) * LOG2E
                    )

    with jax.named_scope('sattn'):
        usable = lax.broadcasted_iota(jnp.int32, (1, tokens), 1) < length_ref[0]
        head_of_lane = lax.broadcasted_iota(jnp.int32, (1, width), 1) // SINGLE_HEAD_DIM
        blended = jnp.zeros((rows_here, width), f32)
        for head in range(s_heads):
            here = head_of_lane == head
            q_head = jnp.where(here, s_query[...], jnp.zeros_like(s_query[...]))
            scores = lax.dot_general(q_head, s_key[...], NT, preferred_element_type=f32)
            scores = jnp.where(usable, scores + head_full[head], masked_value)
            exponent = jnp.exp2(scores - jnp.max(scores, axis=-1, keepdims=True))
            total = jnp.sum(exponent, axis=-1, keepdims=True)
            weights = (exponent / total).astype(jnp.bfloat16)
            blended = jnp.where(
                here, jnp.dot(weights, s_value[...], preferred_element_type=f32), blended
            )
        s_hidden = (s_gate[...] * blended).astype(jnp.bfloat16)
        share = jnp.dot(s_hidden, single_out_ref[...], preferred_element_type=f32)
        for part in range(cols):
            part_sent[part % near, (half + part // near) % 2] = share[
                :, part * width : (part + 1) * width
            ].astype(jnp.bfloat16)
        for step in own_steps:
            part_copy(step).start()

    @pl.loop(late, last)
    def _(s):
        send_row(s)

    with jax.named_scope('part'):
        settle(slot(part_got, nearby), part_recv)
        merged = part_sent[lane, 1].astype(f32)
        total = rest_ref[...].astype(f32) + part_sent[lane, 0].astype(f32)
        for step in own_steps:
            merged = merged + part_got[step, 1].astype(f32)
            total = total + part_got[step, 0].astype(f32)
        fold(merged, merged_sent)
        merged_copy().start()

    @pl.loop(last, slab_rows)
    def _(s):
        send_row(s)

    with jax.named_scope('merge'):
        merged_copy().wait()
        single_new_ref[...] = (total + unfold(merged_got, total.shape)).astype(jnp.bfloat16)

    with jax.named_scope('drain'):
        settle(slot(head_sent, nearby), head_send)
        settle(cross_sent, cross_send)
        settle(slot(early_sent, nearby), early_send)
        settle(slot(part_sent, nearby), part_send)
        settle(slot(bands, row, others), col_send)
        settle(slot(bands, pl.ds(0, chips - 1)), chip_send)
        settle(slot(bands, pl.ds(0, chips)), core_send)
        sent = slot(local, pl.ds(0, slab_rows * (cols - 1)))
        settle(sent, in_send)
        settle(sent, out_send)
        settle(slot(pair_out_ref, pl.ds(0, rows_here - near * early)), out_recv.at[0])


def store_kernel(pair_ref, single_ref, pair_out_ref, single_out_ref, pair_sem, single_sem):
    rows = pair_ref.shape[0]
    chunks = math.gcd(rows, 8)
    single = pltpu.make_async_copy(single_ref, single_out_ref, single_sem)
    single.start()
    for i in range(chunks):
        span = pl.ds(i * (rows // chunks), rows // chunks)
        pltpu.make_async_copy(pair_ref.at[span], pair_out_ref.at[span], pair_sem).start()
    single.wait()
    pltpu.make_async_copy(pair_ref, pair_out_ref, pair_sem).wait()


def store(pair, single):
    held = pl.BlockSpec(memory_space=pltpu.VMEM)
    away = pl.BlockSpec(memory_space=pltpu.HBM)
    return pl.pallas_call(
        store_kernel,
        in_specs=[held, held],
        out_specs=[away, away],
        out_shape=[jax.ShapeDtypeStruct(x.shape, x.dtype) for x in (pair, single)],
        scratch_shapes=[pltpu.SemaphoreType.DMA, pltpu.SemaphoreType.DMA],
        compiler_params=pltpu.CompilerParams(vmem_limit_bytes=4 * 2**20),
        name="store",
    )(*(pltpu.with_memory_space_constraint(x, pltpu.VMEM) for x in (pair, single)))


def per_device(
    pair_rep,
    single_rep,
    length,
    pair_gain,
    pair_proj,
    bias_weight,
    pair_out_weight,
    single_gain,
    single_proj,
    bias_norm_gain,
    single_bias_weight,
    single_out_weight,
):
    rows_here, cols_here, channels = pair_rep.shape
    rows, cols = lax.axis_size("row"), lax.axis_size("col")
    tokens = rows_here * rows
    slab_rows = rows_here // cols
    chips = rows // 2
    heads = bias_weight.shape[1]
    heads_in = math.gcd(heads, LANES // math.gcd(LANES, cols_here))
    single_heads = single_bias_weight.shape[1]
    heads_here = single_heads // cols
    width = single_proj.shape[2]
    near = cols // 2
    early = 2 * slab_rows // 3
    cross_rows = heads_here // 2 * early + heads_here * (slab_rows - early)
    single_proj_t = single_proj.transpose(0, 2, 1)
    bf16, f32 = jnp.bfloat16, jnp.float32
    dma = pltpu.SemaphoreType.DMA
    anywhere = pl.BlockSpec(memory_space=pl.ANY)
    stay = pl.BlockSpec(memory_space=pltpu.HBM)
    held = pl.BlockSpec(memory_space=pltpu.VMEM)
    pair_out, single_out = pl.pallas_call(
        window_kernel,
        in_specs=[stay] * 12,
        out_specs=[held, held],
        out_shape=[
            pltpu.VMEM(pair_rep.shape, bf16),
            pltpu.VMEM((rows_here, width), bf16),
        ],
        scratch_shapes=[
            pltpu.VMEM(pair_rep.shape, bf16),
            pltpu.VMEM((heads, rows_here, cols_here), f32),
            pltpu.VMEM((heads // heads_in, rows_here, heads_in * cols_here), bf16),
            pltpu.VMEM(single_rep.shape, bf16),
            pltpu.VMEM(pair_proj.shape, bf16),
            pltpu.VMEM(pair_out_weight.shape, bf16),
            pltpu.VMEM(single_proj_t.shape, bf16),
            pltpu.VMEM(single_out_weight.shape, bf16),
            pltpu.VMEM(pair_gain.shape, f32),
            pltpu.VMEM((heads, channels), bf16),
            pltpu.VMEM(bias_norm_gain.shape, f32),
            pltpu.VMEM((single_heads, channels), bf16),
            pltpu.VMEM(single_gain.shape, f32),
            pltpu.SMEM(length.shape, jnp.int32),
            pltpu.VMEM((rows_here, width), bf16),
            dma((cols,)),
            dma((11,)),
            pltpu.VMEM((slab_rows, cols, cols_here, channels), bf16),
            pltpu.VMEM((slab_rows, cols, cols_here, channels), bf16),
            pltpu.VMEM((rows, cols, heads // heads_in, rows_here, heads_in * cols_here), bf16),
            pltpu.VMEM((heads, tokens, tokens), f32),
            pltpu.VMEM((cols, heads_here * slab_rows, tokens), f32),
            pltpu.VMEM((cols, heads_here * slab_rows, tokens), bf16),
            pltpu.VMEM((near, heads_here * slab_rows, tokens), bf16),
            pltpu.VMEM((heads_here, rows_here, tokens), f32),
            pltpu.VMEM((cross_rows, tokens), f32),
            pltpu.VMEM((near, cross_rows, tokens), bf16),
            pltpu.VMEM((near, cross_rows, tokens), bf16),
            pltpu.VMEM((cols, heads_here * near * early, cols_here), f32),
            pltpu.VMEM((near, heads_here * near * early, cols_here), bf16),
            pltpu.VMEM((near, heads_here * near * early, cols_here), bf16),
            pltpu.VMEM((rows_here, width), bf16),
            pltpu.VMEM((tokens, width), bf16),
            pltpu.VMEM((tokens, width), bf16),
            pltpu.VMEM((rows_here, width), f32),
            pltpu.VMEM((cols // 2, 2, rows_here, width), bf16),
            pltpu.VMEM((cols // 2, 2, rows_here, width), bf16),
            pltpu.VMEM(folded(rows_here, width), bf16),
            pltpu.VMEM(folded(rows_here, width), bf16),
            dma,
            dma((slab_rows,)),
            dma,
            dma((1 + early,)),
            dma,
            dma((2,)),
            dma,
            dma((chips - 1,)),
            dma,
            dma((chips,)),
            dma,
            dma,
            dma,
            dma,
            dma,
            dma,
            dma,
            dma,
            dma,
            dma,
            pltpu.SemaphoreType.REGULAR,
            pltpu.SemaphoreType.REGULAR,
            pltpu.SemaphoreType.REGULAR,
        ],
        compiler_params=pltpu.CompilerParams(
            collective_id=0, has_side_effects=True, vmem_limit_bytes=56 * 2**20
        ),
        name="window",
    )(
        length, pair_rep, single_rep, pair_proj, pair_out_weight, single_proj_t, single_out_weight,
        pair_gain, bias_weight.T, bias_norm_gain, single_bias_weight.T, single_gain,
    )
    return store(pair_out, single_out)


def solution(mesh):
    in_specs = (
        P("row", "col", None),
        P(),
        P(),
        P(),
        P(),
        P(),
        P(),
        P(),
        P(None, None, "col"),
        P(),
        P(),
        P("col", None),
    )
    out_specs = (P("row", "col", None), P("row", "col"))
    return jax.shard_map(
        per_device, mesh=mesh, in_specs=in_specs, out_specs=out_specs, check_vma=False
    )
```

```python
import math

import jax
import jax.numpy as jnp
from jax import lax
from jax.experimental import pallas as pl
from jax.experimental.pallas import tpu as pltpu
from jax.sharding import PartitionSpec as P

PAIR_HEADS = 8
PAIR_HEAD_DIM = 32
SINGLE_HEAD_DIM = 48
LOG2E = math.log2(math.e)

LANES = 128
masked_value = -1e30
NT = (((1,), (1,)), ((), ()))


def normalize(values, scales):
    floated = values.astype(jnp.float32)
    center = jnp.mean(floated, axis=-1, keepdims=True)
    spread = jnp.mean(jnp.square(floated - center), axis=-1, keepdims=True)
    return ((floated - center) * lax.rsqrt(spread + 1e-05) * scales).astype(jnp.bfloat16)


def project(inputs, matrix):
    return jnp.dot(inputs, matrix, preferred_element_type=jnp.float32).astype(jnp.bfloat16)


def project_t(inputs, matrix):
    return lax.dot_general(inputs, matrix, NT, preferred_element_type=jnp.float32).astype(
        jnp.bfloat16
    )


def row_update(rep, gain, proj_ref, out_weight, bias_of):
    channels = rep.shape[1]
    half = channels // 2
    heads_per_half = PAIR_HEADS // 2
    normed = normalize(rep, gain)
    f32 = jnp.float32
    query = jnp.dot(normed, proj_ref[0], preferred_element_type=f32)
    query = (query * (LOG2E / math.sqrt(PAIR_HEAD_DIM))).astype(jnp.bfloat16)
    key = project(normed, proj_ref[1])
    value = project(normed, proj_ref[2])
    gate = jax.nn.sigmoid(jnp.dot(normed, proj_ref[3], preferred_element_type=f32))
    head_of_lane = lax.broadcasted_iota(jnp.int32, (1, half), 1) // PAIR_HEAD_DIM
    halves = []
    for side in range(2):
        span = slice(side * half, (side + 1) * half)
        q_half, k_half, v_half = query[:, span], key[:, span], value[:, span]
        top = bottom = None
        for sub in range(heads_per_half):
            head = side * heads_per_half + sub
            mine = head_of_lane == sub
            q_head = jnp.where(mine, q_half, jnp.zeros_like(q_half))
            scores = lax.dot_general(q_head, k_half, NT, preferred_element_type=f32)
            scores = scores + bias_of(head)
            peak = jnp.max(scores, axis=-1, keepdims=True)
            exponent = jnp.exp2(scores - peak).astype(jnp.bfloat16)
            v_ext = jnp.concatenate([v_half, jnp.ones_like(v_half)], axis=1)
            both = jnp.dot(exponent, v_ext, preferred_element_type=f32)
            num, den = both[:, :half], both[:, half:]
            top = num if top is None else jnp.where(mine, num, top)
            bottom = den if bottom is None else jnp.where(mine, den, bottom)
        halves.append(top / bottom)
    attended = jnp.concatenate(halves, axis=1)
    hidden = (gate * attended).astype(jnp.bfloat16)
    return (
        rep.astype(f32) + jnp.dot(hidden, out_weight, preferred_element_type=f32)
    ).astype(jnp.bfloat16)


def folded(rows, width):
    full, odd = width // LANES * LANES, width % LANES
    if full and odd and 2 * odd == LANES:
        return (rows * (full // LANES) + rows // 2, LANES)
    return (rows, width)


def fold(value, ref):
    rows, width = value.shape
    if ref.shape == value.shape:
        ref[...] = value.astype(ref.dtype)
        return
    full = width // LANES
    for i in range(full):
        ref[i * rows : (i + 1) * rows] = value[:, i * LANES : (i + 1) * LANES].astype(ref.dtype)
    odd = value[:, full * LANES :]
    ref[full * rows :] = jnp.concatenate(
        [odd[: rows // 2], odd[rows // 2 :]], axis=1
    ).astype(ref.dtype)


def unfold(ref, shape):
    value = ref[...].astype(jnp.float32)
    if ref.shape == shape:
        return value
    rows, width = shape
    full = width // LANES
    odd = value[full * rows :]
    cut = width - full * LANES
    pieces = [value[i * rows : (i + 1) * rows] for i in range(full)]
    return jnp.concatenate(
        pieces + [jnp.concatenate([odd[:, :cut], odd[:, cut:]], axis=0)], axis=1
    )


def slot(ref, *index):
    return ref.at[index]


def window_kernel(
    length_hbm, pair_ref, single_hbm, proj_hbm, out_weight_hbm, single_proj_hbm, single_out_hbm,
    gain_hbm, tri_weight_hbm, bias_gain_hbm, head_weight_hbm, single_gain_hbm,
    pair_out_ref, single_new_ref,
    local, tri_kept, tri_ref, single_ref, proj_ref, out_weight_ref, single_proj_ref, single_out_ref,
    gain_ref, tri_weight_ref, bias_gain_ref, head_weight_ref, single_gain_ref, length_ref,
    rest_ref, local_sem, weight_sem,
    slab, fresh, bands, bias_held, head_kept, head_sent, head_got, head_full,
    cross_kept, cross_sent, cross_got, early_kept, early_sent, early_got,
    s_query, s_key, s_value, s_gate, part_sent, part_got, merged_sent, merged_got,
    in_send, in_recv, out_send, out_recv,
    col_send, col_recv, chip_send, chip_recv, core_send, core_recv,
    head_send, head_recv, cross_send, cross_recv, early_send, early_recv,
    part_send, part_recv, merged_send, merged_recv, opened, met, entered,
):
    f32 = jnp.float32
    slab_rows, cols, cols_here, channels = slab.shape
    rows, _, bundles, rows_here, _ = bands.shape
    heads_in = tri_kept.shape[0] // bundles
    tokens = cols * cols_here
    chips = rows // 2
    s_heads = head_full.shape[0]
    row, col = lax.axis_index("row"), lax.axis_index("col")
    chip, core = row // 2, lax.rem(row, 2)
    partner = chip * 2 + 1 - core
    mesh_id = pl.DeviceIdType.MESH

    def peer(step):
        return lax.rem(col + step, cols)

    def chip_row(step):
        return lax.rem(chip + step, chips) * 2 + core

    def chip_back(step):
        return lax.rem(chip + chips - step, chips) * 2 + core

    def local_copy(part):
        span = pl.ds(part * slab_rows, slab_rows)
        return pltpu.make_async_copy(pair_ref.at[span], local.at[span], local_sem.at[part])

    weight_copies = [
        pltpu.make_async_copy(src, dst, weight_sem.at[i])
        for i, (src, dst) in enumerate(
            (
                (gain_hbm, gain_ref),
                (tri_weight_hbm, tri_weight_ref),
                (length_hbm, length_ref),
                (bias_gain_hbm, bias_gain_ref),
                (head_weight_hbm, head_weight_ref),
                (single_gain_hbm, single_gain_ref),
                (single_hbm, single_ref),
                (single_proj_hbm, single_proj_ref),
                (proj_hbm, proj_ref),
                (out_weight_hbm, out_weight_ref),
                (single_out_hbm, single_out_ref),
            )
        )
    ]
    barrier = pltpu.get_barrier_semaphore()
    left, right = cols // 2 - 1, cols // 2
    inner = jnp.logical_or(col == left, col == right)
    outer = jnp.logical_not(inner)
    guide = jnp.logical_or(col == 0, col == cols - 1)
    follower = jnp.where(col == 0, left, right)
    pair = cols - 1 - col

    def signal(sem, to_row, to_col):
        pl.semaphore_signal(sem, inc=1, device_id=(to_row, to_col), device_id_type=mesh_id)

    def signal_rows(sem):
        for step in range(1, chips):
            signal(sem, chip_row(step), col)
        signal(sem, partner, col)

    for step in range(1, cols):
        to = peer(step)
        to_outer = jnp.logical_and(to != left, to != right)

        @pl.when(jnp.logical_or(to_outer, jnp.logical_and(inner, to == pair)))
        def _():
            signal(barrier, row, to)

    @pl.when(outer)
    def _():
        signal_rows(barrier)

    for copy in weight_copies[:2]:
        copy.start()
    for part in range(cols):
        local_copy(part).start()
    for copy in weight_copies[2:]:
        copy.start()
    with jax.named_scope('bar'):
        @pl.when(inner)
        def _():
            pl.semaphore_wait(barrier, 1)

        @pl.when(outer)
        def _():
            pl.semaphore_wait(barrier, cols + chips - 1)

    @pl.when(guide)
    def _():
        signal(opened, row, follower)
        signal_rows(met)

    def remote(src, dst, send, recv, to):
        return pltpu.make_async_remote_copy(
            src_ref=src, dst_ref=dst, send_sem=send, recv_sem=recv,
            device_id=to, device_id_type=mesh_id,
        )

    near = cols // 2
    mirror = peer(near)

    def near_peer(step):
        return col // near * near + lax.rem(lax.rem(col, near) + step, near)

    own_steps = range(1, near)
    mirror_steps = range(near + 1, 2 * near)

    def col_copy(step):
        to = mirror if step == 0 else near_peer(step % near)
        src, place = (tri_ref, col) if step < near else (slot(bands, row, mirror), mirror)
        return remote(
            src, slot(bands, row, place), col_send, col_recv.at[min(step, 1)], (row, to)
        )

    def chip_copy(step):
        return remote(
            slot(bands, row), slot(bands, row), chip_send, chip_recv.at[step - 1],
            (chip_row(step), col),
        )

    def core_copy(step):
        band = chip_back(step)
        return remote(
            slot(bands, band), slot(bands, band), core_send, core_recv.at[step],
            (partner, col),
        )

    def in_copy(s, to):
        return remote(
            slot(pair_ref, to * slab_rows + s), slot(slab, s, col),
            in_send, in_recv.at[s], (row, to),
        )

    def own_in(s):
        return pltpu.make_async_copy(
            slot(pair_ref, col * slab_rows + s), slot(slab, s, col), in_recv.at[s]
        )

    lane, half = lax.rem(col, near), col // near
    early = 2 * slab_rows // 3

    def out_copy(s, step):
        to = peer(step)
        kind = jnp.where(jnp.logical_and(to // near != half, s < early), 1 + s, 0)
        return remote(
            slot(fresh, s, to), slot(pair_out_ref, col * slab_rows + s),
            out_send, out_recv.at[kind], (row, to),
        )

    def own_out(s):
        return pltpu.make_async_copy(
            slot(fresh, s, col), slot(pair_out_ref, col * slab_rows + s), out_recv.at[0]
        )

    def head_copy(step):
        to = near_peer(step)
        return remote(slot(head_sent, to), slot(head_got, lane), head_send, head_recv, (row, to))

    def cross_copy(step):
        place = lax.rem(lane + step, near)
        to = (1 - half) * near + place
        return remote(
            slot(cross_sent, place), slot(cross_got, lane), cross_send, cross_recv, (row, to)
        )

    def early_copy(step):
        to = near_peer(step)
        return remote(
            slot(early_sent, lax.rem(to, near)), slot(early_got, lane),
            early_send, early_recv, (row, to),
        )

    def part_copy(step):
        return remote(
            slot(part_sent, lax.rem(lane + step, near)), slot(part_got, step),
            part_send, part_recv, (row, near_peer(step)),
        )

    def merged_copy():
        return remote(merged_sent, merged_got, merged_send, merged_recv, (row, mirror))

    def settle(ref, sem):
        pltpu.make_async_copy(ref, ref, sem).wait()

    others = pl.ds(0, cols - 1)

    def bring_row(s):
        own_in(s).start()
        for step in range(1, cols):
            in_copy(s, peer(step)).start()

    def bring_rest(s):
        own_in(s).start()
        for step in range(1, cols):

            @pl.when(peer(step) != pair)
            def _():
                in_copy(s, peer(step)).start()

    first_rows = min(2, slab_rows)

    @pl.when(inner)
    def _():
        for s in range(first_rows):
            in_copy(s, pair).start()

    @pl.when(outer)
    def _():
        bring_row(0)

    for copy in weight_copies[:2]:
        copy.wait()
    with jax.named_scope('tri'):
        group = math.gcd(slab_rows, 6)
        for part in range(cols):
            local_copy(part).wait()

            @pl.loop(0, slab_rows // group)
            def _(i):
                for j in range(group):
                    r = part * slab_rows + i * group + j
                    tri_kept[:, r, :] = lax.dot_general(
                        tri_weight_ref[...], normalize(local[r], gain_ref[...]), NT,
                        preferred_element_type=f32,
                    )

    for bundle in range(bundles):
        tri_ref[bundle] = jnp.concatenate(
            [tri_kept[bundle * heads_in + i] for i in range(heads_in)], axis=1
        ).astype(jnp.bfloat16)
    @pl.when(inner)
    def _():
        pl.semaphore_wait(opened, 1)

    for step in (0, *own_steps):
        col_copy(step).start()
    own_block = pltpu.make_async_copy(tri_ref, slot(bands, row, col), col_recv.at[1])
    own_block.start()

    ahead = min(3, slab_rows)

    @pl.when(inner)
    def _():
        for s in range(first_rows):
            bring_rest(s)

    @pl.when(outer)
    def _():
        for s in range(1, first_rows):
            bring_row(s)

    for s in range(first_rows, ahead):
        bring_row(s)

    @pl.when(guide)
    def _():
        pl.semaphore_wait(met, chips)
        signal(entered, row, follower)

    with jax.named_scope('waitmirror'):
        col_copy(0).wait_recv()
    for step in mirror_steps:
        col_copy(step).start()

    @pl.loop(ahead, slab_rows)
    def _(s):
        bring_row(s)

    for copy in weight_copies[2:]:
        copy.wait()

    with jax.named_scope('waitcols'):
        settle(slot(bands, row, others), col_recv.at[1])
    @pl.when(inner)
    def _():
        pl.semaphore_wait(entered, 1)

    for step in range(1, chips):
        chip_copy(step).start()
    core_copy(0).start()

    with jax.named_scope('sproj'):
        s_normed = normalize(single_ref[...], single_gain_ref[...])
        s_key[...] = project_t(s_normed, single_proj_ref[1])
        s_value[...] = project_t(s_normed, single_proj_ref[2])
        width = s_key.shape[1]
        my_rows = pl.ds(pl.multiple_of(row * rows_here, rows_here), rows_here)
        for part in range(cols):

            @pl.when(col == part)
            def _():
                rest_ref[...] = single_ref[my_rows, part * width : (part + 1) * width]

        mine = normalize(
            single_ref[my_rows, :],
            single_gain_ref[...],
        )
        s_query[...] = (
            lax.dot_general(mine, single_proj_ref[0], NT, preferred_element_type=f32)
            * (LOG2E / math.sqrt(SINGLE_HEAD_DIM))
        ).astype(jnp.bfloat16)
        s_gate[...] = jax.nn.sigmoid(
            lax.dot_general(mine, single_proj_ref[3], NT, preferred_element_type=f32)
        )

    def take_band(band):
        start = pl.multiple_of(band * rows_here, rows_here)
        for part in range(cols):
            usable = (
                lax.broadcasted_iota(jnp.int32, (1, cols_here), 1) + part * cols_here
                < length_ref[0]
            )
            place = (pl.ds(start, rows_here), slice(part * cols_here, (part + 1) * cols_here))
            for bundle in range(bundles):
                piece = bands[band, part, bundle].astype(f32) * LOG2E
                for i in range(heads_in):
                    bias_held[bundle * heads_in + i, *place] = jnp.where(
                        usable, piece[:, i * cols_here : (i + 1) * cols_here], masked_value
                    )

    with jax.named_scope('bands'):
        take_band(row)
        for step in range(1, chips):
            chip_copy(step).wait_recv()
            core_copy(step).start()
            take_band(chip_back(step))
        for step in range(chips):
            core_copy(step).wait_recv()
            take_band(chip_back(step) + 1 - 2 * core)

    middle = early + slab_rows // 12
    late = slab_rows - slab_rows // 6
    last = slab_rows - slab_rows // 12

    def one_row(s):
        settle(slot(slab, s), in_recv.at[s])
        rep = slab[s].reshape(tokens, channels)
        updated = row_update(
            rep, gain_ref[...], proj_ref, out_weight_ref[...], lambda head: bias_held[head]
        )
        fresh[s] = updated.reshape(cols, cols_here, channels)
        again = normalize(updated, bias_gain_ref[...])
        found = lax.dot_general(head_weight_ref[...], again, NT, preferred_element_type=f32)
        for head in range(found.shape[0]):
            line = pl.ds(head % s_heads * slab_rows + s, 1)
            head_kept[head // s_heads, line, :] = found[head : head + 1]

    def send_part(s, to_inner):
        for step in range(1, cols):
            to = peer(step)

            @pl.when(jnp.logical_or(to == left, to == right) == to_inner)
            def _():
                out_copy(s, step).start()

    def send_row(s):
        own_out(s).start()
        for step in range(1, cols):
            out_copy(s, step).start()

    with jax.named_scope('rows'):
        @pl.loop(0, slab_rows)
        def _(s):
            one_row(s)

            @pl.when(s < early)
            def _():
                send_row(s)

    head_sent[...] = head_kept[...].astype(jnp.bfloat16)
    wide = near * cols_here
    rest = slab_rows - early
    top_heads = s_heads // 2
    for part in range(cols):
        mine = slice((1 - part // near) * wide, (2 - part // near) * wide)

        @pl.when(half != part // near)
        def _():
            for head in range(s_heads):
                begin = head * slab_rows
                up = head % top_heads * early
                side = head // top_heads * wide
                cross_kept[up : up + early, side : side + wide] = head_kept[
                    part, begin : begin + early, mine
                ]
                down = top_heads * early + head * rest
                cross_kept[down : down + rest, :] = head_kept[
                    part, begin + early : begin + slab_rows, :
                ]
            cross_sent[part % near] = cross_kept[...].astype(jnp.bfloat16)

    for step in range(near):
        cross_copy(step).start()
    for step in own_steps:
        head_copy(step).start()
    head_got[lane] = head_sent[col]

    @pl.loop(early, middle)
    def _(s):
        send_row(s)

    with jax.named_scope('recompute'):

        @pl.loop(0, early)
        def _(s):
            settle(slot(pair_out_ref, pl.ds(0, near)), out_recv.at[1 + s])
            for other in range(near):
                line = ((1 - half) * near + other) * slab_rows + s
                again = normalize(pair_out_ref[line], bias_gain_ref[...])
                found = lax.dot_general(head_weight_ref[...], again, NT, preferred_element_type=f32)
                for head in range(found.shape[0]):
                    at = (head % s_heads * near + other) * early + s
                    early_kept[head // s_heads, pl.ds(at, 1), :] = found[head : head + 1]

        for place in range(near):
            early_sent[place] = early_kept[half * near + place].astype(jnp.bfloat16)
        for step in own_steps:
            early_copy(step).start()
        early_got[lane] = early_sent[lane]

    @pl.loop(middle, late)
    def _(s):
        send_row(s)

    nearby = pl.ds(0, near - 1)
    with jax.named_scope('headwait'):
        settle(slot(head_got, nearby), head_recv)
        settle(cross_got, cross_recv)
        settle(slot(early_got, nearby), early_recv)
    for part in range(cols):
        first = part * slab_rows
        place, side = part % near, part // near

        @pl.when(half == side)
        def _():
            block = head_got[place].astype(f32) * LOG2E
            for head in range(s_heads):
                head_full[head, first : first + slab_rows, :] = block[
                    head * slab_rows : (head + 1) * slab_rows
                ]

        @pl.when(half != side)
        def _():
            block = cross_got[place].astype(f32) * LOG2E
            for head in range(s_heads):
                up = head % top_heads * early
                from_side = head // top_heads * wide
                head_full[head, first : first + early, side * wide : (side + 1) * wide] = block[
                    up : up + early, from_side : from_side + wide
                ]
                down = top_heads * early + head * rest
                head_full[head, first + early : first + slab_rows, :] = block[down : down + rest]
                at = (head * near + place) * early
                for source in range(near):
                    begin = ((1 - side) * near + source) * cols_here
                    head_full[head, first : first + early, begin : begin + cols_here] = (
                        early_got[source, at : at + early, :].astype(f32) * LOG2E
                    )

    with jax.named_scope('sattn'):
        usable = lax.broadcasted_iota(jnp.int32, (1, tokens), 1) < length_ref[0]
        head_of_lane = lax.broadcasted_iota(jnp.int32, (1, width), 1) // SINGLE_HEAD_DIM
        blended = jnp.zeros((rows_here, width), f32)
        for head in range(s_heads):
            here = head_of_lane == head
            q_head = jnp.where(here, s_query[...], jnp.zeros_like(s_query[...]))
            scores = lax.dot_general(q_head, s_key[...], NT, preferred_element_type=f32)
            scores = jnp.where(usable, scores + head_full[head], masked_value)
            exponent = jnp.exp2(scores - jnp.max(scores, axis=-1, keepdims=True))
            total = jnp.sum(exponent, axis=-1, keepdims=True)
            weights = (exponent / total).astype(jnp.bfloat16)
            blended = jnp.where(
                here, jnp.dot(weights, s_value[...], preferred_element_type=f32), blended
            )
        s_hidden = (s_gate[...] * blended).astype(jnp.bfloat16)
        share = jnp.dot(s_hidden, single_out_ref[...], preferred_element_type=f32)
        for part in range(cols):
            part_sent[part % near, (half + part // near) % 2] = share[
                :, part * width : (part + 1) * width
            ].astype(jnp.bfloat16)
        for step in own_steps:
            part_copy(step).start()

    @pl.loop(late, slab_rows)
    def _(s):
        own_out(s).start()
        send_part(s, False)

    @pl.loop(late, last)
    def _(s):
        send_part(s, True)

    with jax.named_scope('part'):
        settle(slot(part_got, nearby), part_recv)
        merged = part_sent[lane, 1].astype(f32)
        total = rest_ref[...].astype(f32) + part_sent[lane, 0].astype(f32)
        for step in own_steps:
            merged = merged + part_got[step, 1].astype(f32)
            total = total + part_got[step, 0].astype(f32)
        fold(merged, merged_sent)
        merged_copy().start()

    @pl.loop(last, slab_rows)
    def _(s):
        send_part(s, True)

    with jax.named_scope('merge'):
        merged_copy().wait()
        single_new_ref[...] = (total + unfold(merged_got, total.shape)).astype(jnp.bfloat16)

    with jax.named_scope('drain'):
        settle(slot(head_sent, nearby), head_send)
        settle(cross_sent, cross_send)
        settle(slot(early_sent, nearby), early_send)
        settle(slot(part_sent, nearby), part_send)
        settle(slot(bands, row, others), col_send)
        settle(slot(bands, pl.ds(0, chips - 1)), chip_send)
        settle(slot(bands, pl.ds(0, chips)), core_send)
        sent = slot(local, pl.ds(0, slab_rows * (cols - 1)))
        settle(sent, in_send)
        settle(sent, out_send)
        settle(slot(pair_out_ref, pl.ds(0, rows_here - near * early)), out_recv.at[0])


def store_kernel(pair_ref, single_ref, pair_out_ref, single_out_ref, pair_sem, single_sem):
    rows = pair_ref.shape[0]
    chunks = math.gcd(rows, 8)
    single = pltpu.make_async_copy(single_ref, single_out_ref, single_sem)
    single.start()
    for i in range(chunks):
        span = pl.ds(i * (rows // chunks), rows // chunks)
        pltpu.make_async_copy(pair_ref.at[span], pair_out_ref.at[span], pair_sem).start()
    single.wait()
    pltpu.make_async_copy(pair_ref, pair_out_ref, pair_sem).wait()


def store(pair, single):
    held = pl.BlockSpec(memory_space=pltpu.VMEM)
    away = pl.BlockSpec(memory_space=pltpu.HBM)
    return pl.pallas_call(
        store_kernel,
        in_specs=[held, held],
        out_specs=[away, away],
        out_shape=[jax.ShapeDtypeStruct(x.shape, x.dtype) for x in (pair, single)],
        scratch_shapes=[pltpu.SemaphoreType.DMA, pltpu.SemaphoreType.DMA],
        compiler_params=pltpu.CompilerParams(vmem_limit_bytes=4 * 2**20),
        name="store",
    )(*(pltpu.with_memory_space_constraint(x, pltpu.VMEM) for x in (pair, single)))


def per_device(
    pair_rep,
    single_rep,
    length,
    pair_gain,
    pair_proj,
    bias_weight,
    pair_out_weight,
    single_gain,
    single_proj,
    bias_norm_gain,
    single_bias_weight,
    single_out_weight,
):
    rows_here, cols_here, channels = pair_rep.shape
    rows, cols = lax.axis_size("row"), lax.axis_size("col")
    tokens = rows_here * rows
    slab_rows = rows_here // cols
    chips = rows // 2
    heads = bias_weight.shape[1]
    heads_in = math.gcd(heads, LANES // math.gcd(LANES, cols_here))
    single_heads = single_bias_weight.shape[1]
    heads_here = single_heads // cols
    width = single_proj.shape[2]
    near = cols // 2
    early = 2 * slab_rows // 3
    cross_rows = heads_here // 2 * early + heads_here * (slab_rows - early)
    single_proj_t = single_proj.transpose(0, 2, 1)
    bf16, f32 = jnp.bfloat16, jnp.float32
    dma = pltpu.SemaphoreType.DMA
    anywhere = pl.BlockSpec(memory_space=pl.ANY)
    stay = pl.BlockSpec(memory_space=pltpu.HBM)
    held = pl.BlockSpec(memory_space=pltpu.VMEM)
    pair_out, single_out = pl.pallas_call(
        window_kernel,
        in_specs=[stay] * 12,
        out_specs=[held, held],
        out_shape=[
            pltpu.VMEM(pair_rep.shape, bf16),
            pltpu.VMEM((rows_here, width), bf16),
        ],
        scratch_shapes=[
            pltpu.VMEM(pair_rep.shape, bf16),
            pltpu.VMEM((heads, rows_here, cols_here), f32),
            pltpu.VMEM((heads // heads_in, rows_here, heads_in * cols_here), bf16),
            pltpu.VMEM(single_rep.shape, bf16),
            pltpu.VMEM(pair_proj.shape, bf16),
            pltpu.VMEM(pair_out_weight.shape, bf16),
            pltpu.VMEM(single_proj_t.shape, bf16),
            pltpu.VMEM(single_out_weight.shape, bf16),
            pltpu.VMEM(pair_gain.shape, f32),
            pltpu.VMEM((heads, channels), bf16),
            pltpu.VMEM(bias_norm_gain.shape, f32),
            pltpu.VMEM((single_heads, channels), bf16),
            pltpu.VMEM(single_gain.shape, f32),
            pltpu.SMEM(length.shape, jnp.int32),
            pltpu.VMEM((rows_here, width), bf16),
            dma((cols,)),
            dma((11,)),
            pltpu.VMEM((slab_rows, cols, cols_here, channels), bf16),
            pltpu.VMEM((slab_rows, cols, cols_here, channels), bf16),
            pltpu.VMEM((rows, cols, heads // heads_in, rows_here, heads_in * cols_here), bf16),
            pltpu.VMEM((heads, tokens, tokens), f32),
            pltpu.VMEM((cols, heads_here * slab_rows, tokens), f32),
            pltpu.VMEM((cols, heads_here * slab_rows, tokens), bf16),
            pltpu.VMEM((near, heads_here * slab_rows, tokens), bf16),
            pltpu.VMEM((heads_here, rows_here, tokens), f32),
            pltpu.VMEM((cross_rows, tokens), f32),
            pltpu.VMEM((near, cross_rows, tokens), bf16),
            pltpu.VMEM((near, cross_rows, tokens), bf16),
            pltpu.VMEM((cols, heads_here * near * early, cols_here), f32),
            pltpu.VMEM((near, heads_here * near * early, cols_here), bf16),
            pltpu.VMEM((near, heads_here * near * early, cols_here), bf16),
            pltpu.VMEM((rows_here, width), bf16),
            pltpu.VMEM((tokens, width), bf16),
            pltpu.VMEM((tokens, width), bf16),
            pltpu.VMEM((rows_here, width), f32),
            pltpu.VMEM((cols // 2, 2, rows_here, width), bf16),
            pltpu.VMEM((cols // 2, 2, rows_here, width), bf16),
            pltpu.VMEM(folded(rows_here, width), bf16),
            pltpu.VMEM(folded(rows_here, width), bf16),
            dma,
            dma((slab_rows,)),
            dma,
            dma((1 + early,)),
            dma,
            dma((2,)),
            dma,
            dma((chips - 1,)),
            dma,
            dma((chips,)),
            dma,
            dma,
            dma,
            dma,
            dma,
            dma,
            dma,
            dma,
            dma,
            dma,
            pltpu.SemaphoreType.REGULAR,
            pltpu.SemaphoreType.REGULAR,
            pltpu.SemaphoreType.REGULAR,
        ],
        compiler_params=pltpu.CompilerParams(
            collective_id=0, has_side_effects=True, vmem_limit_bytes=56 * 2**20
        ),
        name="window",
    )(
        length, pair_rep, single_rep, pair_proj, pair_out_weight, single_proj_t, single_out_weight,
        pair_gain, bias_weight.T, bias_norm_gain, single_bias_weight.T, single_gain,
    )
    return store(pair_out, single_out)


def solution(mesh):
    in_specs = (
        P("row", "col", None),
        P(),
        P(),
        P(),
        P(),
        P(),
        P(),
        P(),
        P(None, None, "col"),
        P(),
        P(),
        P("col", None),
    )
    out_specs = (P("row", "col", None), P("row", "col"))
    return jax.shard_map(
        per_device, mesh=mesh, in_specs=in_specs, out_specs=out_specs, check_vma=False
    )
```

```python
import math

import jax
import jax.numpy as jnp
from jax import lax
from jax.experimental import pallas as pl
from jax.experimental.pallas import tpu as pltpu
from jax.sharding import PartitionSpec as P

PAIR_HEADS = 8
PAIR_HEAD_DIM = 32
SINGLE_HEAD_DIM = 48
LOG2E = math.log2(math.e)

LANES = 128
masked_value = -1e30
NT = (((1,), (1,)), ((), ()))


def normalize(values, scales):
    floated = values.astype(jnp.float32)
    center = jnp.mean(floated, axis=-1, keepdims=True)
    spread = jnp.mean(jnp.square(floated - center), axis=-1, keepdims=True)
    return ((floated - center) * lax.rsqrt(spread + 1e-05) * scales).astype(jnp.bfloat16)


def project(inputs, matrix):
    return jnp.dot(inputs, matrix, preferred_element_type=jnp.float32).astype(jnp.bfloat16)


def project_t(inputs, matrix):
    return lax.dot_general(inputs, matrix, NT, preferred_element_type=jnp.float32).astype(
        jnp.bfloat16
    )


def row_update(rep, gain, proj_ref, out_weight, bias_of):
    channels = rep.shape[1]
    half = channels // 2
    heads_per_half = PAIR_HEADS // 2
    normed = normalize(rep, gain)
    f32 = jnp.float32
    query = jnp.dot(normed, proj_ref[0], preferred_element_type=f32)
    query = (query * (LOG2E / math.sqrt(PAIR_HEAD_DIM))).astype(jnp.bfloat16)
    key = project(normed, proj_ref[1])
    value = project(normed, proj_ref[2])
    gate = jax.nn.sigmoid(jnp.dot(normed, proj_ref[3], preferred_element_type=f32))
    head_of_lane = lax.broadcasted_iota(jnp.int32, (1, half), 1) // PAIR_HEAD_DIM
    halves = []
    for side in range(2):
        span = slice(side * half, (side + 1) * half)
        q_half, k_half, v_half = query[:, span], key[:, span], value[:, span]
        top = bottom = None
        for sub in range(heads_per_half):
            head = side * heads_per_half + sub
            mine = head_of_lane == sub
            q_head = jnp.where(mine, q_half, jnp.zeros_like(q_half))
            scores = lax.dot_general(q_head, k_half, NT, preferred_element_type=f32)
            scores = scores + bias_of(head)
            peak = jnp.max(scores, axis=-1, keepdims=True)
            exponent = jnp.exp2(scores - peak).astype(jnp.bfloat16)
            v_ext = jnp.concatenate([v_half, jnp.ones_like(v_half)], axis=1)
            both = jnp.dot(exponent, v_ext, preferred_element_type=f32)
            num, den = both[:, :half], both[:, half:]
            top = num if top is None else jnp.where(mine, num, top)
            bottom = den if bottom is None else jnp.where(mine, den, bottom)
        halves.append(top / bottom)
    attended = jnp.concatenate(halves, axis=1)
    hidden = (gate * attended).astype(jnp.bfloat16)
    return (
        rep.astype(f32) + jnp.dot(hidden, out_weight, preferred_element_type=f32)
    ).astype(jnp.bfloat16)


def folded(rows, width):
    full, odd = width // LANES * LANES, width % LANES
    if full and odd and 2 * odd == LANES:
        return (rows * (full // LANES) + rows // 2, LANES)
    return (rows, width)


def fold(value, ref):
    rows, width = value.shape
    if ref.shape == value.shape:
        ref[...] = value.astype(ref.dtype)
        return
    full = width // LANES
    for i in range(full):
        ref[i * rows : (i + 1) * rows] = value[:, i * LANES : (i + 1) * LANES].astype(ref.dtype)
    odd = value[:, full * LANES :]
    ref[full * rows :] = jnp.concatenate(
        [odd[: rows // 2], odd[rows // 2 :]], axis=1
    ).astype(ref.dtype)


def unfold(ref, shape):
    value = ref[...].astype(jnp.float32)
    if ref.shape == shape:
        return value
    rows, width = shape
    full = width // LANES
    odd = value[full * rows :]
    cut = width - full * LANES
    pieces = [value[i * rows : (i + 1) * rows] for i in range(full)]
    return jnp.concatenate(
        pieces + [jnp.concatenate([odd[:, :cut], odd[:, cut:]], axis=0)], axis=1
    )


def slot(ref, *index):
    return ref.at[index]


def window_kernel(
    length_hbm, pair_ref, single_hbm, proj_hbm, out_weight_hbm, single_proj_hbm, single_out_hbm,
    gain_hbm, tri_weight_hbm, bias_gain_hbm, head_weight_hbm, single_gain_hbm,
    pair_out_ref, single_new_ref,
    local, tri_kept, tri_ref, single_ref, proj_ref, out_weight_ref, single_proj_ref, single_out_ref,
    gain_ref, tri_weight_ref, bias_gain_ref, head_weight_ref, single_gain_ref, length_ref,
    rest_ref, local_sem, weight_sem,
    slab, fresh, bands, bias_held, head_kept, head_sent, head_got, head_full,
    cross_kept, cross_sent, cross_got, early_kept, early_sent, early_got,
    s_query, s_key, s_value, s_gate, part_sent, part_got, merged_sent, merged_got,
    in_send, in_recv, out_send, out_recv,
    col_send, col_recv, chip_send, chip_recv, core_send, core_recv,
    head_send, head_recv, cross_send, cross_recv, early_send, early_recv,
    part_send, part_recv, merged_send, merged_recv, opened, met, entered,
):
    f32 = jnp.float32
    slab_rows, cols, cols_here, channels = slab.shape
    rows, _, bundles, rows_here, _ = bands.shape
    heads_in = tri_kept.shape[0] // bundles
    tokens = cols * cols_here
    chips = rows // 2
    s_heads = head_full.shape[0]
    row, col = lax.axis_index("row"), lax.axis_index("col")
    chip, core = row // 2, lax.rem(row, 2)
    partner = chip * 2 + 1 - core
    mesh_id = pl.DeviceIdType.MESH

    def peer(step):
        return lax.rem(col + step, cols)

    def chip_row(step):
        return lax.rem(chip + step, chips) * 2 + core

    def chip_back(step):
        return lax.rem(chip + chips - step, chips) * 2 + core

    def local_copy(part):
        span = pl.ds(part * slab_rows, slab_rows)
        return pltpu.make_async_copy(pair_ref.at[span], local.at[span], local_sem.at[part])

    weight_copies = [
        pltpu.make_async_copy(src, dst, weight_sem.at[i])
        for i, (src, dst) in enumerate(
            (
                (gain_hbm, gain_ref),
                (tri_weight_hbm, tri_weight_ref),
                (length_hbm, length_ref),
                (bias_gain_hbm, bias_gain_ref),
                (head_weight_hbm, head_weight_ref),
                (single_gain_hbm, single_gain_ref),
                (single_hbm, single_ref),
                (single_proj_hbm, single_proj_ref),
                (proj_hbm, proj_ref),
                (out_weight_hbm, out_weight_ref),
                (single_out_hbm, single_out_ref),
            )
        )
    ]
    barrier = pltpu.get_barrier_semaphore()
    left, right = cols // 2 - 1, cols // 2
    inner = jnp.logical_or(col == left, col == right)
    outer = jnp.logical_not(inner)
    guide = jnp.logical_or(col == 0, col == cols - 1)
    follower = jnp.where(col == 0, left, right)
    pair = cols - 1 - col

    def signal(sem, to_row, to_col):
        pl.semaphore_signal(sem, inc=1, device_id=(to_row, to_col), device_id_type=mesh_id)

    def signal_rows(sem):
        for step in range(1, chips):
            signal(sem, chip_row(step), col)
        signal(sem, partner, col)

    for step in range(1, cols):
        to = peer(step)
        to_outer = jnp.logical_and(to != left, to != right)

        @pl.when(jnp.logical_or(to_outer, jnp.logical_and(inner, to == pair)))
        def _():
            signal(barrier, row, to)

    @pl.when(outer)
    def _():
        signal_rows(barrier)

    for copy in weight_copies[:2]:
        copy.start()
    for part in range(cols):
        local_copy(part).start()
    for copy in weight_copies[2:]:
        copy.start()
    with jax.named_scope('bar'):
        @pl.when(inner)
        def _():
            pl.semaphore_wait(barrier, 1)

        @pl.when(outer)
        def _():
            pl.semaphore_wait(barrier, cols + chips - 1)

    @pl.when(guide)
    def _():
        signal(opened, row, follower)
        signal_rows(met)

    def remote(src, dst, send, recv, to):
        return pltpu.make_async_remote_copy(
            src_ref=src, dst_ref=dst, send_sem=send, recv_sem=recv,
            device_id=to, device_id_type=mesh_id,
        )

    near = cols // 2
    mirror = peer(near)

    def near_peer(step):
        return col // near * near + lax.rem(lax.rem(col, near) + step, near)

    own_steps = range(1, near)
    mirror_steps = range(near + 1, 2 * near)

    def col_copy(step):
        to = mirror if step == 0 else near_peer(step % near)
        src, place = (tri_ref, col) if step < near else (slot(bands, row, mirror), mirror)
        return remote(
            src, slot(bands, row, place), col_send, col_recv.at[min(step, 1)], (row, to)
        )

    def chip_copy(step):
        return remote(
            slot(bands, row), slot(bands, row), chip_send, chip_recv.at[step - 1],
            (chip_row(step), col),
        )

    def core_copy(step):
        band = chip_back(step)
        return remote(
            slot(bands, band), slot(bands, band), core_send, core_recv.at[step],
            (partner, col),
        )

    def in_copy(s, to):
        return remote(
            slot(pair_ref, to * slab_rows + s), slot(slab, s, col),
            in_send, in_recv.at[s], (row, to),
        )

    def own_in(s):
        return pltpu.make_async_copy(
            slot(pair_ref, col * slab_rows + s), slot(slab, s, col), in_recv.at[s]
        )

    lane, half = lax.rem(col, near), col // near
    early = 2 * slab_rows // 3

    def out_copy(s, step):
        to = peer(step)
        kind = jnp.where(jnp.logical_and(to // near != half, s < early), 1 + s, 0)
        return remote(
            slot(fresh, s, to), slot(pair_out_ref, col * slab_rows + s),
            out_send, out_recv.at[kind], (row, to),
        )

    def own_out(s):
        return pltpu.make_async_copy(
            slot(fresh, s, col), slot(pair_out_ref, col * slab_rows + s), out_recv.at[0]
        )

    def head_copy(step):
        to = near_peer(step)
        return remote(slot(head_sent, to), slot(head_got, lane), head_send, head_recv, (row, to))

    def cross_copy(step):
        place = lax.rem(lane + step, near)
        to = (1 - half) * near + place
        return remote(
            slot(cross_sent, place), slot(cross_got, lane), cross_send, cross_recv, (row, to)
        )

    def early_copy(step):
        to = near_peer(step)
        return remote(
            slot(early_sent, lax.rem(to, near)), slot(early_got, lane),
            early_send, early_recv, (row, to),
        )

    def part_copy(step):
        return remote(
            slot(part_sent, lax.rem(lane + step, near)), slot(part_got, step),
            part_send, part_recv, (row, near_peer(step)),
        )

    def merged_copy():
        return remote(merged_sent, merged_got, merged_send, merged_recv, (row, mirror))

    def settle(ref, sem):
        pltpu.make_async_copy(ref, ref, sem).wait()

    others = pl.ds(0, cols - 1)

    def bring_row(s):
        own_in(s).start()
        for step in range(1, cols):
            in_copy(s, peer(step)).start()

    def bring_rest(s):
        own_in(s).start()
        for step in range(1, cols):

            @pl.when(peer(step) != pair)
            def _():
                in_copy(s, peer(step)).start()

    first_rows = min(2, slab_rows)

    @pl.when(inner)
    def _():
        for s in range(first_rows):
            in_copy(s, pair).start()

    @pl.when(outer)
    def _():
        bring_row(0)

    for copy in weight_copies[:2]:
        copy.wait()
    with jax.named_scope('tri'):
        group = math.gcd(slab_rows, 6)
        for part in range(cols):
            local_copy(part).wait()

            @pl.loop(0, slab_rows // group)
            def _(i):
                for j in range(group):
                    r = part * slab_rows + i * group + j
                    tri_kept[:, r, :] = lax.dot_general(
                        tri_weight_ref[...], normalize(local[r], gain_ref[...]), NT,
                        preferred_element_type=f32,
                    )

    for bundle in range(bundles):
        tri_ref[bundle] = jnp.concatenate(
            [tri_kept[bundle * heads_in + i] for i in range(heads_in)], axis=1
        ).astype(jnp.bfloat16)
    @pl.when(inner)
    def _():
        pl.semaphore_wait(opened, 1)

    for step in (0, *own_steps):
        col_copy(step).start()
    own_block = pltpu.make_async_copy(tri_ref, slot(bands, row, col), col_recv.at[1])
    own_block.start()

    ahead = min(3, slab_rows)

    @pl.when(inner)
    def _():
        for s in range(first_rows):
            bring_rest(s)

    @pl.when(outer)
    def _():
        for s in range(1, first_rows):
            bring_row(s)

    for s in range(first_rows, ahead):
        bring_row(s)

    @pl.when(guide)
    def _():
        pl.semaphore_wait(met, chips)
        signal(entered, row, follower)

    with jax.named_scope('waitmirror'):
        col_copy(0).wait_recv()
    for step in mirror_steps:
        col_copy(step).start()

    @pl.loop(ahead, slab_rows)
    def _(s):
        bring_row(s)

    for copy in weight_copies[2:]:
        copy.wait()

    with jax.named_scope('waitcols'):
        settle(slot(bands, row, others), col_recv.at[1])
    @pl.when(inner)
    def _():
        pl.semaphore_wait(entered, 1)

    for step in range(1, chips):
        chip_copy(step).start()
    core_copy(0).start()

    with jax.named_scope('sproj'):
        s_normed = normalize(single_ref[...], single_gain_ref[...])
        s_key[...] = project_t(s_normed, single_proj_ref[1])
        s_value[...] = project_t(s_normed, single_proj_ref[2])
        width = s_key.shape[1]
        my_rows = pl.ds(pl.multiple_of(row * rows_here, rows_here), rows_here)
        for part in range(cols):

            @pl.when(col == part)
            def _():
                rest_ref[...] = single_ref[my_rows, part * width : (part + 1) * width]

        mine = normalize(
            single_ref[my_rows, :],
            single_gain_ref[...],
        )
        s_query[...] = (
            lax.dot_general(mine, single_proj_ref[0], NT, preferred_element_type=f32)
            * (LOG2E / math.sqrt(SINGLE_HEAD_DIM))
        ).astype(jnp.bfloat16)
        s_gate[...] = jax.nn.sigmoid(
            lax.dot_general(mine, single_proj_ref[3], NT, preferred_element_type=f32)
        )

    def take_band(band):
        start = pl.multiple_of(band * rows_here, rows_here)
        for part in range(cols):
            usable = (
                lax.broadcasted_iota(jnp.int32, (1, cols_here), 1) + part * cols_here
                < length_ref[0]
            )
            place = (pl.ds(start, rows_here), slice(part * cols_here, (part + 1) * cols_here))
            for bundle in range(bundles):
                piece = bands[band, part, bundle].astype(f32) * LOG2E
                for i in range(heads_in):
                    bias_held[bundle * heads_in + i, *place] = jnp.where(
                        usable, piece[:, i * cols_here : (i + 1) * cols_here], masked_value
                    )

    with jax.named_scope('bands'):
        take_band(row)
        for step in range(1, chips):
            chip_copy(step).wait_recv()
            core_copy(step).start()
            take_band(chip_back(step))
        for step in range(chips):
            core_copy(step).wait_recv()
            take_band(chip_back(step) + 1 - 2 * core)

    middle = early + slab_rows // 12
    late = slab_rows - slab_rows // 6
    last = slab_rows - slab_rows // 12

    def one_row(s):
        settle(slot(slab, s), in_recv.at[s])
        rep = slab[s].reshape(tokens, channels)
        updated = row_update(
            rep, gain_ref[...], proj_ref, out_weight_ref[...], lambda head: bias_held[head]
        )
        fresh[s] = updated.reshape(cols, cols_here, channels)
        again = normalize(updated, bias_gain_ref[...])
        found = lax.dot_general(head_weight_ref[...], again, NT, preferred_element_type=f32)
        for head in range(found.shape[0]):
            line = pl.ds(head % s_heads * slab_rows + s, 1)
            head_kept[head // s_heads, line, :] = found[head : head + 1]

    def send_part(s, to_inner):
        for step in range(1, cols):
            to = peer(step)

            @pl.when(jnp.logical_or(to == left, to == right) == to_inner)
            def _():
                out_copy(s, step).start()

    def send_row(s):
        own_out(s).start()
        for step in range(1, cols):
            out_copy(s, step).start()

    with jax.named_scope('rows'):
        @pl.loop(0, slab_rows)
        def _(s):
            one_row(s)

            @pl.when(s < early)
            def _():
                send_row(s)

    head_sent[...] = head_kept[...].astype(jnp.bfloat16)
    wide = near * cols_here
    rest = slab_rows - early
    top_heads = s_heads // 2
    for part in range(cols):
        mine = slice((1 - part // near) * wide, (2 - part // near) * wide)

        @pl.when(half != part // near)
        def _():
            for head in range(s_heads):
                begin = head * slab_rows
                up = head % top_heads * early
                side = head // top_heads * wide
                cross_kept[up : up + early, side : side + wide] = head_kept[
                    part, begin : begin + early, mine
                ]
                down = top_heads * early + head * rest
                cross_kept[down : down + rest, :] = head_kept[
                    part, begin + early : begin + slab_rows, :
                ]
            cross_sent[part % near] = cross_kept[...].astype(jnp.bfloat16)

    for step in range(near):
        cross_copy(step).start()
    for step in own_steps:
        head_copy(step).start()
    head_got[lane] = head_sent[col]

    @pl.loop(early, middle)
    def _(s):
        send_row(s)

    with jax.named_scope('recompute'):

        @pl.loop(0, early)
        def _(s):
            settle(slot(pair_out_ref, pl.ds(0, near)), out_recv.at[1 + s])
            for other in range(near):
                line = ((1 - half) * near + other) * slab_rows + s
                again = normalize(pair_out_ref[line], bias_gain_ref[...])
                found = lax.dot_general(head_weight_ref[...], again, NT, preferred_element_type=f32)
                for head in range(found.shape[0]):
                    at = (head % s_heads * near + other) * early + s
                    early_kept[head // s_heads, pl.ds(at, 1), :] = found[head : head + 1]

        for place in range(near):
            early_sent[place] = early_kept[half * near + place].astype(jnp.bfloat16)
        for step in own_steps:
            early_copy(step).start()
        early_got[lane] = early_sent[lane]

    @pl.loop(middle, late)
    def _(s):
        send_row(s)

    nearby = pl.ds(0, near - 1)
    with jax.named_scope('headwait'):
        settle(slot(head_got, nearby), head_recv)
        settle(cross_got, cross_recv)
        settle(slot(early_got, nearby), early_recv)
    for part in range(cols):
        first = part * slab_rows
        place, side = part % near, part // near

        @pl.when(half == side)
        def _():
            block = head_got[place].astype(f32) * LOG2E
            for head in range(s_heads):
                head_full[head, first : first + slab_rows, :] = block[
                    head * slab_rows : (head + 1) * slab_rows
                ]

        @pl.when(half != side)
        def _():
            block = cross_got[place].astype(f32) * LOG2E
            for head in range(s_heads):
                up = head % top_heads * early
                from_side = head // top_heads * wide
                head_full[head, first : first + early, side * wide : (side + 1) * wide] = block[
                    up : up + early, from_side : from_side + wide
                ]
                down = top_heads * early + head * rest
                head_full[head, first + early : first + slab_rows, :] = block[down : down + rest]
                at = (head * near + place) * early
                for source in range(near):
                    begin = ((1 - side) * near + source) * cols_here
                    head_full[head, first : first + early, begin : begin + cols_here] = (
                        early_got[source, at : at + early, :].astype(f32) * LOG2E
                    )

    with jax.named_scope('sattn'):
        usable = lax.broadcasted_iota(jnp.int32, (1, tokens), 1) < length_ref[0]
        head_of_lane = lax.broadcasted_iota(jnp.int32, (1, width), 1) // SINGLE_HEAD_DIM
        blended = jnp.zeros((rows_here, width), f32)
        for head in range(s_heads):
            here = head_of_lane == head
            q_head = jnp.where(here, s_query[...], jnp.zeros_like(s_query[...]))
            scores = lax.dot_general(q_head, s_key[...], NT, preferred_element_type=f32)
            scores = jnp.where(usable, scores + head_full[head], masked_value)
            exponent = jnp.exp2(scores - jnp.max(scores, axis=-1, keepdims=True))
            total = jnp.sum(exponent, axis=-1, keepdims=True)
            weights = (exponent / total).astype(jnp.bfloat16)
            blended = jnp.where(
                here, jnp.dot(weights, s_value[...], preferred_element_type=f32), blended
            )
        s_hidden = (s_gate[...] * blended).astype(jnp.bfloat16)
        share = jnp.dot(s_hidden, single_out_ref[...], preferred_element_type=f32)
        for part in range(cols):
            part_sent[part % near, (half + part // near) % 2] = share[
                :, part * width : (part + 1) * width
            ].astype(jnp.bfloat16)
        for step in own_steps:
            part_copy(step).start()

    @pl.loop(late, slab_rows)
    def _(s):
        own_out(s).start()
        send_part(s, False)

    @pl.when(outer)
    def _():
        @pl.loop(late, last)
        def _(s):
            send_part(s, True)

    with jax.named_scope('part'):
        settle(slot(part_got, nearby), part_recv)
        merged = part_sent[lane, 1].astype(f32)
        total = rest_ref[...].astype(f32) + part_sent[lane, 0].astype(f32)
        for step in own_steps:
            merged = merged + part_got[step, 1].astype(f32)
            total = total + part_got[step, 0].astype(f32)
        fold(merged, merged_sent)
        merged_copy().start()

    @pl.when(inner)
    def _():
        @pl.loop(late, last)
        def _(s):
            send_part(s, True)

    @pl.loop(last, slab_rows)
    def _(s):
        send_part(s, True)

    with jax.named_scope('merge'):
        merged_copy().wait()
        single_new_ref[...] = (total + unfold(merged_got, total.shape)).astype(jnp.bfloat16)

    with jax.named_scope('drain'):
        settle(slot(head_sent, nearby), head_send)
        settle(cross_sent, cross_send)
        settle(slot(early_sent, nearby), early_send)
        settle(slot(part_sent, nearby), part_send)
        settle(slot(bands, row, others), col_send)
        settle(slot(bands, pl.ds(0, chips - 1)), chip_send)
        settle(slot(bands, pl.ds(0, chips)), core_send)
        sent = slot(local, pl.ds(0, slab_rows * (cols - 1)))
        settle(sent, in_send)
        settle(sent, out_send)
        settle(slot(pair_out_ref, pl.ds(0, rows_here - near * early)), out_recv.at[0])


def store_kernel(pair_ref, single_ref, pair_out_ref, single_out_ref, pair_sem, single_sem):
    rows = pair_ref.shape[0]
    chunks = math.gcd(rows, 8)
    single = pltpu.make_async_copy(single_ref, single_out_ref, single_sem)
    single.start()
    for i in range(chunks):
        span = pl.ds(i * (rows // chunks), rows // chunks)
        pltpu.make_async_copy(pair_ref.at[span], pair_out_ref.at[span], pair_sem).start()
    single.wait()
    pltpu.make_async_copy(pair_ref, pair_out_ref, pair_sem).wait()


def store(pair, single):
    held = pl.BlockSpec(memory_space=pltpu.VMEM)
    away = pl.BlockSpec(memory_space=pltpu.HBM)
    return pl.pallas_call(
        store_kernel,
        in_specs=[held, held],
        out_specs=[away, away],
        out_shape=[jax.ShapeDtypeStruct(x.shape, x.dtype) for x in (pair, single)],
        scratch_shapes=[pltpu.SemaphoreType.DMA, pltpu.SemaphoreType.DMA],
        compiler_params=pltpu.CompilerParams(vmem_limit_bytes=4 * 2**20),
        name="store",
    )(*(pltpu.with_memory_space_constraint(x, pltpu.VMEM) for x in (pair, single)))


def per_device(
    pair_rep,
    single_rep,
    length,
    pair_gain,
    pair_proj,
    bias_weight,
    pair_out_weight,
    single_gain,
    single_proj,
    bias_norm_gain,
    single_bias_weight,
    single_out_weight,
):
    rows_here, cols_here, channels = pair_rep.shape
    rows, cols = lax.axis_size("row"), lax.axis_size("col")
    tokens = rows_here * rows
    slab_rows = rows_here // cols
    chips = rows // 2
    heads = bias_weight.shape[1]
    heads_in = math.gcd(heads, LANES // math.gcd(LANES, cols_here))
    single_heads = single_bias_weight.shape[1]
    heads_here = single_heads // cols
    width = single_proj.shape[2]
    near = cols // 2
    early = 2 * slab_rows // 3
    cross_rows = heads_here // 2 * early + heads_here * (slab_rows - early)
    single_proj_t = single_proj.transpose(0, 2, 1)
    bf16, f32 = jnp.bfloat16, jnp.float32
    dma = pltpu.SemaphoreType.DMA
    anywhere = pl.BlockSpec(memory_space=pl.ANY)
    stay = pl.BlockSpec(memory_space=pltpu.HBM)
    held = pl.BlockSpec(memory_space=pltpu.VMEM)
    pair_out, single_out = pl.pallas_call(
        window_kernel,
        in_specs=[stay] * 12,
        out_specs=[held, held],
        out_shape=[
            pltpu.VMEM(pair_rep.shape, bf16),
            pltpu.VMEM((rows_here, width), bf16),
        ],
        scratch_shapes=[
            pltpu.VMEM(pair_rep.shape, bf16),
            pltpu.VMEM((heads, rows_here, cols_here), f32),
            pltpu.VMEM((heads // heads_in, rows_here, heads_in * cols_here), bf16),
            pltpu.VMEM(single_rep.shape, bf16),
            pltpu.VMEM(pair_proj.shape, bf16),
            pltpu.VMEM(pair_out_weight.shape, bf16),
            pltpu.VMEM(single_proj_t.shape, bf16),
            pltpu.VMEM(single_out_weight.shape, bf16),
            pltpu.VMEM(pair_gain.shape, f32),
            pltpu.VMEM((heads, channels), bf16),
            pltpu.VMEM(bias_norm_gain.shape, f32),
            pltpu.VMEM((single_heads, channels), bf16),
            pltpu.VMEM(single_gain.shape, f32),
            pltpu.SMEM(length.shape, jnp.int32),
            pltpu.VMEM((rows_here, width), bf16),
            dma((cols,)),
            dma((11,)),
            pltpu.VMEM((slab_rows, cols, cols_here, channels), bf16),
            pltpu.VMEM((slab_rows, cols, cols_here, channels), bf16),
            pltpu.VMEM((rows, cols, heads // heads_in, rows_here, heads_in * cols_here), bf16),
            pltpu.VMEM((heads, tokens, tokens), f32),
            pltpu.VMEM((cols, heads_here * slab_rows, tokens), f32),
            pltpu.VMEM((cols, heads_here * slab_rows, tokens), bf16),
            pltpu.VMEM((near, heads_here * slab_rows, tokens), bf16),
            pltpu.VMEM((heads_here, rows_here, tokens), f32),
            pltpu.VMEM((cross_rows, tokens), f32),
            pltpu.VMEM((near, cross_rows, tokens), bf16),
            pltpu.VMEM((near, cross_rows, tokens), bf16),
            pltpu.VMEM((cols, heads_here * near * early, cols_here), f32),
            pltpu.VMEM((near, heads_here * near * early, cols_here), bf16),
            pltpu.VMEM((near, heads_here * near * early, cols_here), bf16),
            pltpu.VMEM((rows_here, width), bf16),
            pltpu.VMEM((tokens, width), bf16),
            pltpu.VMEM((tokens, width), bf16),
            pltpu.VMEM((rows_here, width), f32),
            pltpu.VMEM((cols // 2, 2, rows_here, width), bf16),
            pltpu.VMEM((cols // 2, 2, rows_here, width), bf16),
            pltpu.VMEM(folded(rows_here, width), bf16),
            pltpu.VMEM(folded(rows_here, width), bf16),
            dma,
            dma((slab_rows,)),
            dma,
            dma((1 + early,)),
            dma,
            dma((2,)),
            dma,
            dma((chips - 1,)),
            dma,
            dma((chips,)),
            dma,
            dma,
            dma,
            dma,
            dma,
            dma,
            dma,
            dma,
            dma,
            dma,
            pltpu.SemaphoreType.REGULAR,
            pltpu.SemaphoreType.REGULAR,
            pltpu.SemaphoreType.REGULAR,
        ],
        compiler_params=pltpu.CompilerParams(
            collective_id=0, has_side_effects=True, vmem_limit_bytes=56 * 2**20
        ),
        name="window",
    )(
        length, pair_rep, single_rep, pair_proj, pair_out_weight, single_proj_t, single_out_weight,
        pair_gain, bias_weight.T, bias_norm_gain, single_bias_weight.T, single_gain,
    )
    return store(pair_out, single_out)


def solution(mesh):
    in_specs = (
        P("row", "col", None),
        P(),
        P(),
        P(),
        P(),
        P(),
        P(),
        P(),
        P(None, None, "col"),
        P(),
        P(),
        P("col", None),
    )
    out_specs = (P("row", "col", None), P("row", "col"))
    return jax.shard_map(
        per_device, mesh=mesh, in_specs=in_specs, out_specs=out_specs, check_vma=False
    )
```

```python
import math

import jax
import jax.numpy as jnp
from jax import lax
from jax.experimental import pallas as pl
from jax.experimental.pallas import tpu as pltpu
from jax.sharding import PartitionSpec as P

PAIR_HEADS = 8
PAIR_HEAD_DIM = 32
SINGLE_HEAD_DIM = 48
LOG2E = math.log2(math.e)

LANES = 128
masked_value = -1e30
NT = (((1,), (1,)), ((), ()))


def normalize(values, scales):
    floated = values.astype(jnp.float32)
    center = jnp.mean(floated, axis=-1, keepdims=True)
    spread = jnp.mean(jnp.square(floated - center), axis=-1, keepdims=True)
    return ((floated - center) * lax.rsqrt(spread + 1e-05) * scales).astype(jnp.bfloat16)


def project(inputs, matrix):
    return jnp.dot(inputs, matrix, preferred_element_type=jnp.float32).astype(jnp.bfloat16)


def project_t(inputs, matrix):
    return lax.dot_general(inputs, matrix, NT, preferred_element_type=jnp.float32).astype(
        jnp.bfloat16
    )


def row_update(rep, gain, proj_ref, out_weight, bias_of):
    channels = rep.shape[1]
    half = channels // 2
    heads_per_half = PAIR_HEADS // 2
    normed = normalize(rep, gain)
    f32 = jnp.float32
    query = jnp.dot(normed, proj_ref[0], preferred_element_type=f32)
    query = (query * (LOG2E / math.sqrt(PAIR_HEAD_DIM))).astype(jnp.bfloat16)
    key = project(normed, proj_ref[1])
    value = project(normed, proj_ref[2])
    gate = jax.nn.sigmoid(jnp.dot(normed, proj_ref[3], preferred_element_type=f32))
    head_of_lane = lax.broadcasted_iota(jnp.int32, (1, half), 1) // PAIR_HEAD_DIM
    halves = []
    for side in range(2):
        span = slice(side * half, (side + 1) * half)
        q_half, k_half, v_half = query[:, span], key[:, span], value[:, span]
        top = bottom = None
        for sub in range(heads_per_half):
            head = side * heads_per_half + sub
            mine = head_of_lane == sub
            q_head = jnp.where(mine, q_half, jnp.zeros_like(q_half))
            scores = lax.dot_general(q_head, k_half, NT, preferred_element_type=f32)
            scores = scores + bias_of(head)
            peak = jnp.max(scores, axis=-1, keepdims=True)
            exponent = jnp.exp2(scores - peak).astype(jnp.bfloat16)
            v_ext = jnp.concatenate([v_half, jnp.ones_like(v_half)], axis=1)
            both = jnp.dot(exponent, v_ext, preferred_element_type=f32)
            num, den = both[:, :half], both[:, half:]
            top = num if top is None else jnp.where(mine, num, top)
            bottom = den if bottom is None else jnp.where(mine, den, bottom)
        halves.append(top / bottom)
    attended = jnp.concatenate(halves, axis=1)
    hidden = (gate * attended).astype(jnp.bfloat16)
    return (
        rep.astype(f32) + jnp.dot(hidden, out_weight, preferred_element_type=f32)
    ).astype(jnp.bfloat16)


def folded(rows, width):
    full, odd = width // LANES * LANES, width % LANES
    if full and odd and 2 * odd == LANES:
        return (rows * (full // LANES) + rows // 2, LANES)
    return (rows, width)


def fold(value, ref):
    rows, width = value.shape
    if ref.shape == value.shape:
        ref[...] = value.astype(ref.dtype)
        return
    full = width // LANES
    for i in range(full):
        ref[i * rows : (i + 1) * rows] = value[:, i * LANES : (i + 1) * LANES].astype(ref.dtype)
    odd = value[:, full * LANES :]
    ref[full * rows :] = jnp.concatenate(
        [odd[: rows // 2], odd[rows // 2 :]], axis=1
    ).astype(ref.dtype)


def unfold(ref, shape):
    value = ref[...].astype(jnp.float32)
    if ref.shape == shape:
        return value
    rows, width = shape
    full = width // LANES
    odd = value[full * rows :]
    cut = width - full * LANES
    pieces = [value[i * rows : (i + 1) * rows] for i in range(full)]
    return jnp.concatenate(
        pieces + [jnp.concatenate([odd[:, :cut], odd[:, cut:]], axis=0)], axis=1
    )


def slot(ref, *index):
    return ref.at[index]


def window_kernel(
    length_hbm, pair_ref, single_hbm, proj_hbm, out_weight_hbm, single_proj_hbm, single_out_hbm,
    gain_hbm, tri_weight_hbm, bias_gain_hbm, head_weight_hbm, single_gain_hbm,
    pair_out_ref, single_new_ref,
    local, tri_kept, tri_ref, single_ref, proj_ref, out_weight_ref, single_proj_ref, single_out_ref,
    gain_ref, tri_weight_ref, bias_gain_ref, head_weight_ref, single_gain_ref, length_ref,
    rest_ref, local_sem, weight_sem,
    slab, fresh, bands, bias_held, head_kept, head_sent, head_got, head_full,
    cross_kept, cross_sent, cross_got, early_kept, early_sent, early_got,
    s_query, s_key, s_value, s_gate, part_sent, part_got, merged_sent, merged_got,
    in_send, in_recv, out_send, out_recv,
    col_send, col_recv, chip_send, chip_recv, core_send, core_recv,
    head_send, head_recv, cross_send, cross_recv, early_send, early_recv,
    part_send, part_recv, merged_send, merged_recv, opened, met, entered,
):
    f32 = jnp.float32
    slab_rows, cols, cols_here, channels = slab.shape
    rows, _, bundles, rows_here, _ = bands.shape
    heads_in = tri_kept.shape[0] // bundles
    tokens = cols * cols_here
    chips = rows // 2
    s_heads = head_full.shape[0]
    batch = slab_rows // in_recv.shape[0]
    row, col = lax.axis_index("row"), lax.axis_index("col")
    chip, core = row // 2, lax.rem(row, 2)
    partner = chip * 2 + 1 - core
    mesh_id = pl.DeviceIdType.MESH

    def peer(step):
        return lax.rem(col + step, cols)

    def chip_row(step):
        return lax.rem(chip + step, chips) * 2 + core

    def chip_back(step):
        return lax.rem(chip + chips - step, chips) * 2 + core

    def local_copy(part):
        span = pl.ds(part * slab_rows, slab_rows)
        return pltpu.make_async_copy(pair_ref.at[span], local.at[span], local_sem.at[part])

    weight_copies = [
        pltpu.make_async_copy(src, dst, weight_sem.at[i])
        for i, (src, dst) in enumerate(
            (
                (gain_hbm, gain_ref),
                (tri_weight_hbm, tri_weight_ref),
                (length_hbm, length_ref),
                (bias_gain_hbm, bias_gain_ref),
                (head_weight_hbm, head_weight_ref),
                (single_gain_hbm, single_gain_ref),
                (single_hbm, single_ref),
                (single_proj_hbm, single_proj_ref),
                (proj_hbm, proj_ref),
                (out_weight_hbm, out_weight_ref),
                (single_out_hbm, single_out_ref),
            )
        )
    ]
    barrier = pltpu.get_barrier_semaphore()
    left, right = cols // 2 - 1, cols // 2
    inner = jnp.logical_or(col == left, col == right)
    outer = jnp.logical_not(inner)
    guide = jnp.logical_or(col == 0, col == cols - 1)
    follower = jnp.where(col == 0, left, right)
    pair = cols - 1 - col

    def signal(sem, to_row, to_col):
        pl.semaphore_signal(sem, inc=1, device_id=(to_row, to_col), device_id_type=mesh_id)

    def signal_rows(sem):
        for step in range(1, chips):
            signal(sem, chip_row(step), col)
        signal(sem, partner, col)

    for step in range(1, cols):
        to = peer(step)
        to_outer = jnp.logical_and(to != left, to != right)

        @pl.when(jnp.logical_or(to_outer, jnp.logical_and(inner, to == pair)))
        def _():
            signal(barrier, row, to)

    @pl.when(outer)
    def _():
        signal_rows(barrier)

    for copy in weight_copies[:2]:
        copy.start()
    for part in range(cols):
        local_copy(part).start()
    for copy in weight_copies[2:]:
        copy.start()
    with jax.named_scope('bar'):
        @pl.when(inner)
        def _():
            pl.semaphore_wait(barrier, 1)

        @pl.when(outer)
        def _():
            pl.semaphore_wait(barrier, cols + chips - 1)

    @pl.when(guide)
    def _():
        signal(opened, row, follower)
        signal_rows(met)

    def remote(src, dst, send, recv, to):
        return pltpu.make_async_remote_copy(
            src_ref=src, dst_ref=dst, send_sem=send, recv_sem=recv,
            device_id=to, device_id_type=mesh_id,
        )

    near = cols // 2
    mirror = peer(near)

    def near_peer(step):
        return col // near * near + lax.rem(lax.rem(col, near) + step, near)

    own_steps = range(1, near)
    mirror_steps = range(near + 1, 2 * near)

    def col_copy(step):
        to = mirror if step == 0 else near_peer(step % near)
        src, place = (tri_ref, col) if step < near else (slot(bands, row, mirror), mirror)
        return remote(
            src, slot(bands, row, place), col_send, col_recv.at[min(step, 1)], (row, to)
        )

    def chip_copy(step):
        return remote(
            slot(bands, row), slot(bands, row), chip_send, chip_recv.at[step - 1],
            (chip_row(step), col),
        )

    def core_copy(step):
        band = chip_back(step)
        return remote(
            slot(bands, band), slot(bands, band), core_send, core_recv.at[step],
            (partner, col),
        )

    def in_copy(s, to):
        return remote(
            slot(pair_ref, to * slab_rows + s), slot(slab, s, col),
            in_send, in_recv.at[s // batch], (row, to),
        )

    def own_in(s):
        return pltpu.make_async_copy(
            slot(pair_ref, col * slab_rows + s), slot(slab, s, col), in_recv.at[s // batch]
        )

    lane, half = lax.rem(col, near), col // near
    early = 2 * slab_rows // 3

    def out_copy(s, step):
        to = peer(step)
        kind = jnp.where(jnp.logical_and(to // near != half, s < early), 1 + s, 0)
        return remote(
            slot(fresh, s, to), slot(pair_out_ref, col * slab_rows + s),
            out_send, out_recv.at[kind], (row, to),
        )

    def own_out(s):
        return pltpu.make_async_copy(
            slot(fresh, s, col), slot(pair_out_ref, col * slab_rows + s), out_recv.at[0]
        )

    def head_copy(step):
        to = near_peer(step)
        return remote(slot(head_sent, to), slot(head_got, lane), head_send, head_recv, (row, to))

    def cross_copy(step):
        place = lax.rem(lane + step, near)
        to = (1 - half) * near + place
        return remote(
            slot(cross_sent, place), slot(cross_got, lane), cross_send, cross_recv, (row, to)
        )

    def early_copy(step):
        to = near_peer(step)
        return remote(
            slot(early_sent, lax.rem(to, near)), slot(early_got, lane),
            early_send, early_recv, (row, to),
        )

    def part_copy(step):
        return remote(
            slot(part_sent, lax.rem(lane + step, near)), slot(part_got, step),
            part_send, part_recv, (row, near_peer(step)),
        )

    def merged_copy():
        return remote(merged_sent, merged_got, merged_send, merged_recv, (row, mirror))

    def settle(ref, sem):
        pltpu.make_async_copy(ref, ref, sem).wait()

    others = pl.ds(0, cols - 1)

    def bring_row(s):
        own_in(s).start()
        for step in range(1, cols):
            in_copy(s, peer(step)).start()

    def bring_rest(s):
        own_in(s).start()
        for step in range(1, cols):

            @pl.when(peer(step) != pair)
            def _():
                in_copy(s, peer(step)).start()

    first_rows = min(2, slab_rows)

    @pl.when(inner)
    def _():
        for s in range(first_rows):
            in_copy(s, pair).start()

    @pl.when(outer)
    def _():
        bring_row(0)

    for copy in weight_copies[:2]:
        copy.wait()
    with jax.named_scope('tri'):
        group = math.gcd(slab_rows, 6)
        for part in range(cols):
            local_copy(part).wait()

            @pl.loop(0, slab_rows // group)
            def _(i):
                for j in range(group):
                    r = part * slab_rows + i * group + j
                    tri_kept[:, r, :] = lax.dot_general(
                        tri_weight_ref[...], normalize(local[r], gain_ref[...]), NT,
                        preferred_element_type=f32,
                    )

    for bundle in range(bundles):
        tri_ref[bundle] = jnp.concatenate(
            [tri_kept[bundle * heads_in + i] for i in range(heads_in)], axis=1
        ).astype(jnp.bfloat16)
    @pl.when(inner)
    def _():
        pl.semaphore_wait(opened, 1)

    for step in (0, *own_steps):
        col_copy(step).start()
    own_block = pltpu.make_async_copy(tri_ref, slot(bands, row, col), col_recv.at[1])
    own_block.start()

    ahead = min(3, slab_rows)

    @pl.when(inner)
    def _():
        for s in range(first_rows):
            bring_rest(s)

    @pl.when(outer)
    def _():
        for s in range(1, first_rows):
            bring_row(s)

    for s in range(first_rows, ahead):
        bring_row(s)

    @pl.when(guide)
    def _():
        pl.semaphore_wait(met, chips)
        signal(entered, row, follower)

    with jax.named_scope('waitmirror'):
        col_copy(0).wait_recv()
    for step in mirror_steps:
        col_copy(step).start()

    @pl.loop(ahead, slab_rows)
    def _(s):
        bring_row(s)

    for copy in weight_copies[2:]:
        copy.wait()

    with jax.named_scope('waitcols'):
        settle(slot(bands, row, others), col_recv.at[1])
    @pl.when(inner)
    def _():
        pl.semaphore_wait(entered, 1)

    for step in range(1, chips):
        chip_copy(step).start()
    core_copy(0).start()

    with jax.named_scope('sproj'):
        s_normed = normalize(single_ref[...], single_gain_ref[...])
        s_key[...] = project_t(s_normed, single_proj_ref[1])
        s_value[...] = project_t(s_normed, single_proj_ref[2])
        width = s_key.shape[1]
        my_rows = pl.ds(pl.multiple_of(row * rows_here, rows_here), rows_here)
        for part in range(cols):

            @pl.when(col == part)
            def _():
                rest_ref[...] = single_ref[my_rows, part * width : (part + 1) * width]

        mine = normalize(
            single_ref[my_rows, :],
            single_gain_ref[...],
        )
        s_query[...] = (
            lax.dot_general(mine, single_proj_ref[0], NT, preferred_element_type=f32)
            * (LOG2E / math.sqrt(SINGLE_HEAD_DIM))
        ).astype(jnp.bfloat16)
        s_gate[...] = jax.nn.sigmoid(
            lax.dot_general(mine, single_proj_ref[3], NT, preferred_element_type=f32)
        )

    def take_band(band):
        start = pl.multiple_of(band * rows_here, rows_here)
        for part in range(cols):
            usable = (
                lax.broadcasted_iota(jnp.int32, (1, cols_here), 1) + part * cols_here
                < length_ref[0]
            )
            place = (pl.ds(start, rows_here), slice(part * cols_here, (part + 1) * cols_here))
            for bundle in range(bundles):
                piece = bands[band, part, bundle].astype(f32) * LOG2E
                for i in range(heads_in):
                    bias_held[bundle * heads_in + i, *place] = jnp.where(
                        usable, piece[:, i * cols_here : (i + 1) * cols_here], masked_value
                    )

    with jax.named_scope('bands'):
        take_band(row)
        for step in range(1, chips):
            chip_copy(step).wait_recv()
            core_copy(step).start()
            take_band(chip_back(step))
        for step in range(chips):
            core_copy(step).wait_recv()
            take_band(chip_back(step) + 1 - 2 * core)

    middle = early + slab_rows // 12
    late = slab_rows - slab_rows // 6
    last = slab_rows - slab_rows // 12

    def one_row(s):
        @pl.when(lax.rem(s, batch) == 0)
        def _():
            settle(slot(slab, pl.ds(s, batch)), in_recv.at[s // batch])

        rep = slab[s].reshape(tokens, channels)
        updated = row_update(
            rep, gain_ref[...], proj_ref, out_weight_ref[...], lambda head: bias_held[head]
        )
        fresh[s] = updated.reshape(cols, cols_here, channels)
        again = normalize(updated, bias_gain_ref[...])
        found = lax.dot_general(head_weight_ref[...], again, NT, preferred_element_type=f32)
        for head in range(found.shape[0]):
            line = pl.ds(head % s_heads * slab_rows + s, 1)
            head_kept[head // s_heads, line, :] = found[head : head + 1]

    def send_part(s, to_inner):
        for step in range(1, cols):
            to = peer(step)

            @pl.when(jnp.logical_or(to == left, to == right) == to_inner)
            def _():
                out_copy(s, step).start()

    def send_row(s):
        own_out(s).start()
        for step in range(1, cols):
            out_copy(s, step).start()

    with jax.named_scope('rows'):
        @pl.loop(0, slab_rows)
        def _(s):
            one_row(s)

            @pl.when(s < early)
            def _():
                send_row(s)

    head_sent[...] = head_kept[...].astype(jnp.bfloat16)
    wide = near * cols_here
    rest = slab_rows - early
    top_heads = s_heads // 2
    for part in range(cols):
        mine = slice((1 - part // near) * wide, (2 - part // near) * wide)

        @pl.when(half != part // near)
        def _():
            for head in range(s_heads):
                begin = head * slab_rows
                up = head % top_heads * early
                side = head // top_heads * wide
                cross_kept[up : up + early, side : side + wide] = head_kept[
                    part, begin : begin + early, mine
                ]
                down = top_heads * early + head * rest
                cross_kept[down : down + rest, :] = head_kept[
                    part, begin + early : begin + slab_rows, :
                ]
            cross_sent[part % near] = cross_kept[...].astype(jnp.bfloat16)

    for step in range(near):
        cross_copy(step).start()
    for step in own_steps:
        head_copy(step).start()
    head_got[lane] = head_sent[col]

    @pl.loop(early, middle)
    def _(s):
        send_row(s)

    with jax.named_scope('recompute'):

        @pl.loop(0, early)
        def _(s):
            settle(slot(pair_out_ref, pl.ds(0, near)), out_recv.at[1 + s])
            for other in range(near):
                line = ((1 - half) * near + other) * slab_rows + s
                again = normalize(pair_out_ref[line], bias_gain_ref[...])
                found = lax.dot_general(head_weight_ref[...], again, NT, preferred_element_type=f32)
                for head in range(found.shape[0]):
                    at = (head % s_heads * near + other) * early + s
                    early_kept[head // s_heads, pl.ds(at, 1), :] = found[head : head + 1]

        for place in range(near):
            early_sent[place] = early_kept[half * near + place].astype(jnp.bfloat16)
        for step in own_steps:
            early_copy(step).start()
        early_got[lane] = early_sent[lane]

    @pl.loop(middle, late)
    def _(s):
        send_row(s)

    nearby = pl.ds(0, near - 1)
    with jax.named_scope('headwait'):
        settle(slot(head_got, nearby), head_recv)
        settle(cross_got, cross_recv)
        settle(slot(early_got, nearby), early_recv)
    for part in range(cols):
        first = part * slab_rows
        place, side = part % near, part // near

        @pl.when(half == side)
        def _():
            block = head_got[place].astype(f32) * LOG2E
            for head in range(s_heads):
                head_full[head, first : first + slab_rows, :] = block[
                    head * slab_rows : (head + 1) * slab_rows
                ]

        @pl.when(half != side)
        def _():
            block = cross_got[place].astype(f32) * LOG2E
            for head in range(s_heads):
                up = head % top_heads * early
                from_side = head // top_heads * wide
                head_full[head, first : first + early, side * wide : (side + 1) * wide] = block[
                    up : up + early, from_side : from_side + wide
                ]
                down = top_heads * early + head * rest
                head_full[head, first + early : first + slab_rows, :] = block[down : down + rest]
                at = (head * near + place) * early
                for source in range(near):
                    begin = ((1 - side) * near + source) * cols_here
                    head_full[head, first : first + early, begin : begin + cols_here] = (
                        early_got[source, at : at + early, :].astype(f32) * LOG2E
                    )

    with jax.named_scope('sattn'):
        usable = lax.broadcasted_iota(jnp.int32, (1, tokens), 1) < length_ref[0]
        head_of_lane = lax.broadcasted_iota(jnp.int32, (1, width), 1) // SINGLE_HEAD_DIM
        blended = jnp.zeros((rows_here, width), f32)
        for head in range(s_heads):
            here = head_of_lane == head
            q_head = jnp.where(here, s_query[...], jnp.zeros_like(s_query[...]))
            scores = lax.dot_general(q_head, s_key[...], NT, preferred_element_type=f32)
            scores = jnp.where(usable, scores + head_full[head], masked_value)
            exponent = jnp.exp2(scores - jnp.max(scores, axis=-1, keepdims=True))
            total = jnp.sum(exponent, axis=-1, keepdims=True)
            weights = (exponent / total).astype(jnp.bfloat16)
            blended = jnp.where(
                here, jnp.dot(weights, s_value[...], preferred_element_type=f32), blended
            )
        s_hidden = (s_gate[...] * blended).astype(jnp.bfloat16)
        share = jnp.dot(s_hidden, single_out_ref[...], preferred_element_type=f32)
        for part in range(cols):
            part_sent[part % near, (half + part // near) % 2] = share[
                :, part * width : (part + 1) * width
            ].astype(jnp.bfloat16)
        for step in own_steps:
            part_copy(step).start()

    @pl.loop(late, slab_rows)
    def _(s):
        own_out(s).start()
        send_part(s, False)

    @pl.when(outer)
    def _():
        @pl.loop(late, last)
        def _(s):
            send_part(s, True)

    with jax.named_scope('part'):
        settle(slot(part_got, nearby), part_recv)
        merged = part_sent[lane, 1].astype(f32)
        total = rest_ref[...].astype(f32) + part_sent[lane, 0].astype(f32)
        for step in own_steps:
            merged = merged + part_got[step, 1].astype(f32)
            total = total + part_got[step, 0].astype(f32)
        fold(merged, merged_sent)
        merged_copy().start()

    @pl.when(inner)
    def _():
        @pl.loop(late, last)
        def _(s):
            send_part(s, True)

    @pl.loop(last, slab_rows)
    def _(s):
        send_part(s, True)

    with jax.named_scope('merge'):
        merged_copy().wait()
        single_new_ref[...] = (total + unfold(merged_got, total.shape)).astype(jnp.bfloat16)

    with jax.named_scope('drain'):
        settle(slot(head_sent, nearby), head_send)
        settle(cross_sent, cross_send)
        settle(slot(early_sent, nearby), early_send)
        settle(slot(part_sent, nearby), part_send)
        settle(slot(bands, row, others), col_send)
        settle(slot(bands, pl.ds(0, chips - 1)), chip_send)
        settle(slot(bands, pl.ds(0, chips)), core_send)
        sent = slot(local, pl.ds(0, slab_rows * (cols - 1)))
        settle(sent, in_send)
        settle(sent, out_send)
        settle(slot(pair_out_ref, pl.ds(0, rows_here - near * early)), out_recv.at[0])


def store_kernel(pair_ref, single_ref, pair_out_ref, single_out_ref, pair_sem, single_sem):
    rows = pair_ref.shape[0]
    chunks = math.gcd(rows, 8)
    single = pltpu.make_async_copy(single_ref, single_out_ref, single_sem)
    single.start()
    for i in range(chunks):
        span = pl.ds(i * (rows // chunks), rows // chunks)
        pltpu.make_async_copy(pair_ref.at[span], pair_out_ref.at[span], pair_sem).start()
    single.wait()
    pltpu.make_async_copy(pair_ref, pair_out_ref, pair_sem).wait()


def store(pair, single):
    held = pl.BlockSpec(memory_space=pltpu.VMEM)
    away = pl.BlockSpec(memory_space=pltpu.HBM)
    return pl.pallas_call(
        store_kernel,
        in_specs=[held, held],
        out_specs=[away, away],
        out_shape=[jax.ShapeDtypeStruct(x.shape, x.dtype) for x in (pair, single)],
        scratch_shapes=[pltpu.SemaphoreType.DMA, pltpu.SemaphoreType.DMA],
        compiler_params=pltpu.CompilerParams(vmem_limit_bytes=4 * 2**20),
        name="store",
    )(*(pltpu.with_memory_space_constraint(x, pltpu.VMEM) for x in (pair, single)))


def per_device(
    pair_rep,
    single_rep,
    length,
    pair_gain,
    pair_proj,
    bias_weight,
    pair_out_weight,
    single_gain,
    single_proj,
    bias_norm_gain,
    single_bias_weight,
    single_out_weight,
):
    rows_here, cols_here, channels = pair_rep.shape
    rows, cols = lax.axis_size("row"), lax.axis_size("col")
    tokens = rows_here * rows
    slab_rows = rows_here // cols
    chips = rows // 2
    heads = bias_weight.shape[1]
    heads_in = math.gcd(heads, LANES // math.gcd(LANES, cols_here))
    single_heads = single_bias_weight.shape[1]
    heads_here = single_heads // cols
    width = single_proj.shape[2]
    near = cols // 2
    early = 2 * slab_rows // 3
    cross_rows = heads_here // 2 * early + heads_here * (slab_rows - early)
    single_proj_t = single_proj.transpose(0, 2, 1)
    bf16, f32 = jnp.bfloat16, jnp.float32
    dma = pltpu.SemaphoreType.DMA
    anywhere = pl.BlockSpec(memory_space=pl.ANY)
    stay = pl.BlockSpec(memory_space=pltpu.HBM)
    held = pl.BlockSpec(memory_space=pltpu.VMEM)
    pair_out, single_out = pl.pallas_call(
        window_kernel,
        in_specs=[stay] * 12,
        out_specs=[held, held],
        out_shape=[
            pltpu.VMEM(pair_rep.shape, bf16),
            pltpu.VMEM((rows_here, width), bf16),
        ],
        scratch_shapes=[
            pltpu.VMEM(pair_rep.shape, bf16),
            pltpu.VMEM((heads, rows_here, cols_here), f32),
            pltpu.VMEM((heads // heads_in, rows_here, heads_in * cols_here), bf16),
            pltpu.VMEM(single_rep.shape, bf16),
            pltpu.VMEM(pair_proj.shape, bf16),
            pltpu.VMEM(pair_out_weight.shape, bf16),
            pltpu.VMEM(single_proj_t.shape, bf16),
            pltpu.VMEM(single_out_weight.shape, bf16),
            pltpu.VMEM(pair_gain.shape, f32),
            pltpu.VMEM((heads, channels), bf16),
            pltpu.VMEM(bias_norm_gain.shape, f32),
            pltpu.VMEM((single_heads, channels), bf16),
            pltpu.VMEM(single_gain.shape, f32),
            pltpu.SMEM(length.shape, jnp.int32),
            pltpu.VMEM((rows_here, width), bf16),
            dma((cols,)),
            dma((11,)),
            pltpu.VMEM((slab_rows, cols, cols_here, channels), bf16),
            pltpu.VMEM((slab_rows, cols, cols_here, channels), bf16),
            pltpu.VMEM((rows, cols, heads // heads_in, rows_here, heads_in * cols_here), bf16),
            pltpu.VMEM((heads, tokens, tokens), f32),
            pltpu.VMEM((cols, heads_here * slab_rows, tokens), f32),
            pltpu.VMEM((cols, heads_here * slab_rows, tokens), bf16),
            pltpu.VMEM((near, heads_here * slab_rows, tokens), bf16),
            pltpu.VMEM((heads_here, rows_here, tokens), f32),
            pltpu.VMEM((cross_rows, tokens), f32),
            pltpu.VMEM((near, cross_rows, tokens), bf16),
            pltpu.VMEM((near, cross_rows, tokens), bf16),
            pltpu.VMEM((cols, heads_here * near * early, cols_here), f32),
            pltpu.VMEM((near, heads_here * near * early, cols_here), bf16),
            pltpu.VMEM((near, heads_here * near * early, cols_here), bf16),
            pltpu.VMEM((rows_here, width), bf16),
            pltpu.VMEM((tokens, width), bf16),
            pltpu.VMEM((tokens, width), bf16),
            pltpu.VMEM((rows_here, width), f32),
            pltpu.VMEM((cols // 2, 2, rows_here, width), bf16),
            pltpu.VMEM((cols // 2, 2, rows_here, width), bf16),
            pltpu.VMEM(folded(rows_here, width), bf16),
            pltpu.VMEM(folded(rows_here, width), bf16),
            dma,
            dma((slab_rows // math.gcd(slab_rows, 3),)),
            dma,
            dma((1 + early,)),
            dma,
            dma((2,)),
            dma,
            dma((chips - 1,)),
            dma,
            dma((chips,)),
            dma,
            dma,
            dma,
            dma,
            dma,
            dma,
            dma,
            dma,
            dma,
            dma,
            pltpu.SemaphoreType.REGULAR,
            pltpu.SemaphoreType.REGULAR,
            pltpu.SemaphoreType.REGULAR,
        ],
        compiler_params=pltpu.CompilerParams(
            collective_id=0, has_side_effects=True, vmem_limit_bytes=56 * 2**20
        ),
        name="window",
    )(
        length, pair_rep, single_rep, pair_proj, pair_out_weight, single_proj_t, single_out_weight,
        pair_gain, bias_weight.T, bias_norm_gain, single_bias_weight.T, single_gain,
    )
    return store(pair_out, single_out)


def solution(mesh):
    in_specs = (
        P("row", "col", None),
        P(),
        P(),
        P(),
        P(),
        P(),
        P(),
        P(),
        P(None, None, "col"),
        P(),
        P(),
        P("col", None),
    )
    out_specs = (P("row", "col", None), P("row", "col"))
    return jax.shard_map(
        per_device, mesh=mesh, in_specs=in_specs, out_specs=out_specs, check_vma=False
    )
```
